32 devices in a mesh: pipe: 2 (over core), expert: 16 (over z, y, x).
Axes of the slice: x: 2, y: 2, z: 4, core: 2. Of those that a mesh axis runs over, the one named last changes fastest.
Arguments:
- hidden_a: bfloat16 [2, 1024, 3584], P('pipe', 'expert'), may hold values from -6 to 6
- routes_a: int32 [2, 1024, 8], P('pipe', 'expert'), may hold values from 0 to 15, all different within a row; in each aligned block of 64 rows (0 to 63, 64 to 127, ..., all dimensions but the last counted through in order) at most 48 rows name the same one
- hidden_b: bfloat16 [2, 1024, 3584], P('pipe', 'expert'), may hold values from -6 to 6
- routes_b: int32 [2, 1024, 8], P('pipe', 'expert'), may hold values from 0 to 15, all different within a row; in each aligned block of 64 rows (0 to 63, 64 to 127, ..., all dimensions but the last counted through in order) at most 48 rows name the same one
- grad_out_b: bfloat16 [2, 1024, 3584], P('pipe', 'expert'), may hold values from -0.796875 to 0.796875
- router: bfloat16 [2, 16, 3584], P('pipe'), as said below
- w_up: bfloat16 [2, 16, 3584, 1024], P('pipe', 'expert'), as said below
- w_down: bfloat16 [2, 16, 1024, 3584], P('pipe', 'expert'), as said below
Outputs:
- layer_out_a: bfloat16 [2, 1024, 3584], P('pipe', 'expert')
- grad_in_b: bfloat16 [2, 1024, 3584], P('pipe', 'expert')
- router_grad: float32 [2, 16, 3584], P('pipe', 'expert')
The draws below stay inside these ranges and needn't reach their ends.
Inputs may be any that keep to these rules, and one draw needn't show every extreme that they name: `routes_a`: each token names 8 different experts. Among the 64 tokens of one device no expert is named by more than 48 tokens, and in every draw some expert is named by exactly 48 tokens of some device. `routes_b`: as for routes_a. router[1 - p] equals router[p] for every p. w_up[1 - p] equals w_up[p] for every p. w_down[1 - p] equals w_down[p] for every p.
All inputs are finite; a program needn't handle non-finite values.
Results may differ from the reference program's by a relative error of at most 0.014.
Values may be sent and summed in bfloat16 or wider, within the bound.
A program may use at most 128 MiB of HBM per device.

```python
import math
import jax
import jax.numpy as jnp
import numpy as np
from jax import lax

D = 3584
F = 1024
TOP = 8
TOK_DEV = 64
EXPERTS = 16
TOKENS = 1024
CAP = 48
N_PIPE = 2
N_EXPERT = 16


def mirrored_weight(key, inner_shape, fan_in):
    half_shape = (N_PIPE // 2,) + inner_shape
    scale = fan_in ** (-0.5)
    values = jnp.clip(jax.random.normal(key, half_shape, jnp.float32), -6.0, 6.0) * scale
    return jnp.concatenate([values, values[::-1]], axis=0)


def draw_router(key, part):
    return mirrored_weight(jax.random.fold_in(key, 11), (EXPERTS, D), D).astype(jnp.bfloat16)


def draw_w_up(key, part):
    return mirrored_weight(jax.random.fold_in(key, 23), (EXPERTS, D, F), D).astype(jnp.bfloat16)


def draw_w_down(key, part):
    return mirrored_weight(jax.random.fold_in(key, 37), (EXPERTS, F, D), F).astype(jnp.bfloat16)


def steps_of(rng, extent, shards, smallest, high):
    level = 1.0
    for axis_at, shards_of in shards:
        heights = jax.random.uniform(jax.random.fold_in(jax.random.fold_in(rng, 6), axis_at), (shards_of,), jnp.float32, smallest / len(shards), high / len(shards))
        level = level * jnp.repeat(jnp.exp(heights), extent[axis_at] // shards_of).reshape((-1,) + (1,) * (len(extent) - 1 - axis_at))
    return level


def shared_out(rng, own, number, rows, number_of, top, limit, lean):
    ranking = jax.random.permutation(rng, number_of)
    packed, usual = portions_of(number_of, rows * top, limit, lean, True), portions_of(number_of, rows * top, limit, lean, False)
    places = jnp.arange(number_of)

    def named(sizes, offset_by):
        used = int((sizes > 0).sum())
        fixed = max(1, used // 4)
        moved = fixed + (places - fixed + offset_by * (used - fixed)) % max(1, number_of - fixed)
        return jnp.zeros((number_of,), jnp.int32).at[ranking[jnp.where(places < fixed, places, moved)]].set(jnp.asarray(sizes, jnp.int32))

    sizes = jnp.where(number % 4 == 0, named(packed, number // 4), named(usual, number - number // 4 - 1))
    mixed = jax.random.permutation(jax.random.fold_in(own, 3), number_of)
    source_of, taker = mixed[0:number_of // 2 * 2:2], mixed[1:number_of // 2 * 2:2]
    room = jnp.minimum(sizes[source_of] - 1, limit - sizes[taker]) // 2
    room = jnp.where((source_of == ranking[0]) | (taker == ranking[0]) | (sizes[taker] == 0), 0, jnp.maximum(room, 0))
    moved = jax.random.randint(jax.random.fold_in(own, 4), (number_of // 2,), 0, 1 << 20) % (room + 1)
    sizes = sizes.at[source_of].add(-moved).at[taker].add(moved)
    items = jnp.searchsorted(jnp.cumsum(sizes), jnp.arange(rows * top), side="right").astype(jnp.int32)
    grid = items.reshape(top, rows).T
    grid = grid[jax.random.permutation(jax.random.fold_in(own, 1), rows)]
    offset_by = jax.random.randint(jax.random.fold_in(own, 2), (rows, 1), 0, top)
    return jnp.take_along_axis(grid, (jnp.arange(top)[None, :] + offset_by) % top, axis=1)


def portions_of(number_of, total, reach, slope, full):
    weights = [(1 << 20) // math.isqrt(standing ** slope) + 1 for standing in range(1, number_of + 1)]
    largest = reach if full else min(reach, max(-(-total // number_of), total * weights[0] // sum(weights)))
    least = 1 if total - largest >= number_of - 1 else 0
    given, spare = [largest] + [least] * (number_of - 1), total - largest - least * (number_of - 1)
    while spare > 0:
        movable = [i for i in range(1, number_of) if given[i] < largest] or [i for i in range(1, number_of) if given[i] < reach]
        pool, left = sum([weights[i] for i in movable]), spare
        for i in movable:
            more = min(reach - given[i], max(1, left * weights[i] // pool), spare)
            given[i] = given[i] + more
            spare = spare - more
    return np.array(given)


def centred(own_key, dims, scale, most, shards=(), kind=jnp.bfloat16):
    result = scale * jax.random.normal(own_key, dims, jnp.float32)
    if shards:
        result = result * steps_of(own_key, dims, shards, -0.22, 0.18)
    return jnp.clip(result, -most, most).astype(kind)


def setup_inputs(seed: int = 0) -> dict:
    key_list = jax.random.split(jax.random.key(seed), 9)
    hidden_a = centred(key_list[0], (N_PIPE, TOKENS, D), 1.0, 6.0, ((0, 2), (1, 16)))
    routes_a_keys = jax.random.split(jax.random.fold_in(key_list[1], 1), N_PIPE * TOKENS // TOK_DEV)
    routes_a_turns = jax.random.permutation(jax.random.fold_in(key_list[1], 3), N_PIPE * TOKENS // TOK_DEV)
    routes_a = jax.vmap(lambda own, number: shared_out(jax.random.fold_in(key_list[1], 2), own, number, TOK_DEV, EXPERTS, TOP, CAP, 2))(routes_a_keys, routes_a_turns).reshape((N_PIPE, TOKENS, TOP))
    hidden_b = centred(key_list[2], (N_PIPE, TOKENS, D), 1.0, 6.0, ((0, 2), (1, 16)))
    routes_b_keys = jax.random.split(jax.random.fold_in(key_list[3], 1), N_PIPE * TOKENS // TOK_DEV)
    routes_b_turns = jax.random.permutation(jax.random.fold_in(key_list[3], 3), N_PIPE * TOKENS // TOK_DEV)
    routes_b = jax.vmap(lambda own, number: shared_out(jax.random.fold_in(key_list[3], 2), own, number, TOK_DEV, EXPERTS, TOP, CAP, 2))(routes_b_keys, routes_b_turns).reshape((N_PIPE, TOKENS, TOP))
    grad_out_b = centred(key_list[4], (N_PIPE, TOKENS, D), 0.1, 0.796875, ((0, 2), (1, 16)))
    router = draw_router(jax.random.fold_in(key_list[8], 71), 0)
    w_up = draw_w_up(jax.random.fold_in(key_list[8], 71), 0)
    w_down = draw_w_down(jax.random.fold_in(key_list[8], 71), 0)
    return dict(hidden_a=hidden_a, routes_a=routes_a, hidden_b=hidden_b, routes_b=routes_b, grad_out_b=grad_out_b, router=router, w_up=w_up, w_down=w_down)


ROUTED_SCALE = 2.5
EPSILON = 1e-06

def silu_slope(pre):
    sig = jax.nn.sigmoid(pre)
    return sig * (1.0 + pre * (1.0 - sig))

def expert_table(routes_flat):
    slot_width = N_EXPERT * CAP
    onehot = (routes_flat[:, None] == jnp.arange(EXPERTS, dtype=jnp.int32)[None, :]).astype(jnp.int32)
    slot_rank = lax.optimization_barrier(jnp.sum((jnp.cumsum(onehot, axis=0) - 1) * onehot, axis=1))
    slot_index = routes_flat * slot_width + slot_rank
    pair_ids = jnp.arange(routes_flat.shape[0], dtype=jnp.int32)
    pair_table = jnp.zeros((EXPERTS * slot_width,), jnp.int32).at[slot_index].set(pair_ids)
    return (slot_index, pair_table.reshape(EXPERTS, slot_width))

def gate_weights(normed, routes, router_segment):
    logits = jnp.dot(normed, router_segment.T, preferred_element_type=jnp.float32)
    picked = jnp.take_along_axis(logits, routes, axis=1)
    affinity = jax.nn.sigmoid(picked)
    aff_total = lax.optimization_barrier(jnp.sum(affinity, axis=1, keepdims=True))
    return (affinity, aff_total, affinity / aff_total)

def forward_rows(normed, routes, up_segment, down_segment):
    slot_index, pair_table = expert_table(routes.reshape(-1))

    def per_expert(inputs):
        up_one, down_one, entries = inputs
        gathered = normed[entries // TOP]
        pre = jnp.dot(gathered, up_one, preferred_element_type=jnp.float32)
        active = jax.nn.silu(pre).astype(jnp.bfloat16)
        return jnp.dot(active, down_one, preferred_element_type=jnp.float32).astype(jnp.bfloat16)
    results = lax.map(per_expert, (up_segment, down_segment, pair_table))
    return results.reshape(-1, D)[slot_index].reshape(TOKENS, TOP, D)

def backward_rows(normed, grad_out, routes, up_segment, down_segment):
    slot_index, pair_table = expert_table(routes.reshape(-1))

    def per_expert(inputs):
        up_one, down_one, entries = inputs
        gathered = normed[entries // TOP]
        grad_rows = grad_out[entries // TOP]
        pre = jnp.dot(gathered, up_one, preferred_element_type=jnp.float32)
        active = jax.nn.silu(pre).astype(jnp.bfloat16)
        back = jnp.dot(grad_rows, down_one.T, preferred_element_type=jnp.float32)
        score = lax.optimization_barrier(jnp.sum(back * active.astype(jnp.float32), axis=-1)).astype(jnp.bfloat16)
        inner = (back * silu_slope(pre)).astype(jnp.bfloat16)
        lifted = jnp.dot(inner, up_one.T, preferred_element_type=jnp.float32).astype(jnp.bfloat16)
        return (lifted, score)
    lifted, score = lax.map(per_expert, (up_segment, down_segment, pair_table))
    lifted = lifted.reshape(-1, D)[slot_index].reshape(TOKENS, TOP, D)
    score = score.reshape(-1)[slot_index].reshape(TOKENS, TOP)
    return (lifted, score)

def reference(hidden_a, routes_a, hidden_b, routes_b, grad_out_b, router, w_up, w_down):
    outs_a = []
    grads_b = []
    terms = []
    for segment in range(N_PIPE):
        router_segment = router[segment]
        hidden32 = hidden_a[segment].astype(jnp.float32)
        rinv = lax.rsqrt(lax.optimization_barrier(jnp.mean(hidden32 * hidden32, axis=-1, keepdims=True)) + EPSILON)
        normed = (hidden32 * rinv).astype(jnp.bfloat16)
        affinity, aff_total, weight = gate_weights(normed, routes_a[segment], router_segment)
        expert_out = forward_rows(normed, routes_a[segment], w_up[segment], w_down[segment])
        mixed = hidden32 + ROUTED_SCALE * lax.optimization_barrier(jnp.sum(weight[:, :, None] * expert_out.astype(jnp.float32), axis=1))
        outs_a.append(mixed.astype(jnp.bfloat16))
        hidden32 = hidden_b[segment].astype(jnp.float32)
        rinv = lax.rsqrt(lax.optimization_barrier(jnp.mean(hidden32 * hidden32, axis=-1, keepdims=True)) + EPSILON)
        normed = (hidden32 * rinv).astype(jnp.bfloat16)
        affinity, aff_total, weight = gate_weights(normed, routes_b[segment], router_segment)
        lifted, score = backward_rows(normed, grad_out_b[segment], routes_b[segment], w_up[segment], w_down[segment])
        gate_grad = ROUTED_SCALE * score.astype(jnp.float32)
        logit_grad = affinity * (1.0 - affinity) * (gate_grad - lax.optimization_barrier(jnp.sum(gate_grad * weight, axis=1, keepdims=True))) / aff_total
        chosen = (routes_b[segment][:, :, None] == jnp.arange(EXPERTS, dtype=jnp.int32)[None, None, :]).astype(jnp.float32)
        dense = lax.optimization_barrier(jnp.sum(chosen * logit_grad[:, :, None], axis=1))
        normed_grad = ROUTED_SCALE * lax.optimization_barrier(jnp.sum(weight[:, :, None] * lifted.astype(jnp.float32), axis=1))
        normed_grad = normed_grad + jnp.dot(dense, router_segment.astype(jnp.float32), precision=lax.Precision.HIGHEST)
        mean_term = lax.optimization_barrier(jnp.mean(normed_grad * hidden32, axis=-1, keepdims=True))
        grad_in = grad_out_b[segment].astype(jnp.float32) + rinv * normed_grad - hidden32 * rinv ** 3 * mean_term
        grads_b.append(grad_in.astype(jnp.bfloat16))
        terms.append(jnp.dot(dense.T, normed.astype(jnp.float32), precision=lax.Precision.HIGHEST))
    router_grad = jnp.stack([terms[segment] + terms[N_PIPE - 1 - segment] for segment in range(N_PIPE)])
    return (jnp.stack(outs_a), jnp.stack(grads_b), router_grad)
```

```python
import functools
import math

import jax
import jax.numpy as jnp
from jax import lax
from jax.experimental import pallas as pl
from jax.experimental.pallas import tpu as pltpu
from jax.sharding import PartitionSpec as P

ROUTED_SCALE = 2.5
EPSILON = 1e-06


def partner(block, axis, bit):
    count = lax.axis_size(axis)
    route = []
    for low in range(count):
        high = low | 1 << bit
        if high != low and high < count:
            route += [(low, high), (high, low)]
    return lax.ppermute(block, axis, route)


MESH = pl.DeviceIdType.MESH
DMA = pltpu.SemaphoreType.DMA
PLANE = 4


def remote(src, dst, send_sem, recv_sem, target):
    return pltpu.make_async_remote_copy(
        src_ref=src,
        dst_ref=dst,
        send_sem=send_sem,
        recv_sem=recv_sem,
        device_id={"expert": target},
        device_id_type=MESH,
    )


def place():
    me = lax.axis_index("expert")
    z, y, x = me // PLANE, (me // 2) % 2, me % 2
    return (me, z, y, x, me + 1 - 2 * x, me + 2 - 4 * y)


def greet(planes):
    me, z, y, x, x_near, y_near = place()
    barrier = pltpu.get_barrier_semaphore()
    pl.semaphore_signal(barrier, inc=1, device_id={"expert": x_near}, device_id_type=MESH)
    pl.semaphore_signal(barrier, inc=1, device_id={"expert": y_near}, device_id_type=MESH)

    @pl.when(z < planes - 1)
    def _():
        pl.semaphore_signal(barrier, inc=1, device_id={"expert": me + PLANE}, device_id_type=MESH)

    @pl.when(z > 0)
    def _():
        pl.semaphore_signal(barrier, inc=1, device_id={"expert": me - PLANE}, device_id_type=MESH)

    ends = jnp.where(z == 0, 1, 0) + jnp.where(z == planes - 1, 1, 0)
    pl.semaphore_wait(barrier, 4 - ends)


def gather_kernel(count, planes, *refs):
    ins, outs = refs[:count], refs[count : 2 * count]
    own_sem, up_s, down_s, z_r, x_s, x_r, y_s, y_r, d_s, d_r = refs[2 * count :]
    me, z, y, x, x_near, y_near = place()

    def up(k, p, src):
        return remote(src, outs[k].at[p * PLANE + y * 2 + x], up_s.at[k, p], z_r.at[k, p], me + PLANE)

    def down(k, p, src):
        return remote(src, outs[k].at[p * PLANE + y * 2 + x], down_s.at[k, p], z_r.at[k, p], me - PLANE)

    def to_x(k, p, src):
        return remote(src, outs[k].at[p * PLANE + y * 2 + x], x_s.at[k, p], x_r.at[k, p], x_near)

    def to_y(k, p, src):
        return remote(src, outs[k].at[p * PLANE + y * 2 + x], y_s.at[k, p], y_r.at[k, p], y_near)

    def half(k, p, way):
        if way == 0:
            ref = outs[k].at[p * PLANE + y * 2 + 1 - x, 0]
            return remote(ref, ref, d_s.at[k, p, 0], d_r.at[k, p, 0], y_near)
        ref = outs[k].at[p * PLANE + (1 - y) * 2 + x, 1]
        return remote(ref, ref, d_s.at[k, p, 1], d_r.at[k, p, 1], x_near)

    def each(d, act):
        if d == 0:
            act(z, 0)
            return

        @pl.when(z >= d)
        def _():
            act(z - d, 1)

        @pl.when(z + d < planes)
        def _():
            act(z + d, -1)

    def spread(k, p, way, wait):
        src = ins[k] if way == 0 else outs[k].at[p * PLANE + y * 2 + x]

        def do(copy):
            copy.wait_send() if wait else copy.start()

        if way != 0 and not wait:
            up(k, p, src).wait_recv()
        if way >= 0:

            @pl.when(z < planes - 1)
            def _():
                do(up(k, p, src))

        if way <= 0:

            @pl.when(z > 0)
            def _():
                do(down(k, p, src))

        do(to_x(k, p, src))
        do(to_y(k, p, src))

    def relay(k, p, way):
        to_x(k, p, ins[k]).wait_recv()
        half(k, p, 0).start()
        to_y(k, p, ins[k]).wait_recv()
        half(k, p, 1).start()

    def finish(k, p, way):
        for route in range(2):
            half(k, p, route).wait()
        spread(k, p, way, True)

    greet(planes)
    for k in range(count):
        pltpu.make_async_copy(ins[k], outs[k].at[me], own_sem.at[k]).start()
        each(0, lambda p, way: spread(k, p, way, False))
    for k in range(count):
        for d in range(1, planes):
            each(d, lambda p, way: spread(k, p, way, False))
            each(d - 1, lambda p, way: relay(k, p, way))
        each(planes - 1, lambda p, way: relay(k, p, way))
    for k in range(count):
        for d in range(planes):
            each(d, lambda p, way: finish(k, p, way))
        pltpu.make_async_copy(ins[k], outs[k].at[me], own_sem.at[k]).wait()


def gather_all(blocks, collective_id):
    n = lax.axis_size("expert")
    planes = n // PLANE
    count = len(blocks)
    halved = [b.reshape(2, b.shape[0] // 2, b.shape[1]) for b in blocks]
    outs = pl.pallas_call(
        functools.partial(gather_kernel, count, planes),
        out_shape=[jax.ShapeDtypeStruct((n,) + b.shape, b.dtype) for b in halved],
        in_specs=[pl.BlockSpec(memory_space=pltpu.VMEM)] * count,
        out_specs=[pl.BlockSpec(memory_space=pl.ANY)] * count,
        scratch_shapes=[DMA((count,))] + [DMA((count, planes))] * 7 + [DMA((count, planes, 2))] * 2,
        compiler_params=pltpu.CompilerParams(collective_id=collective_id, has_side_effects=True),
    )(*halved)
    return [o.reshape(n * b.shape[0], b.shape[1]) for o, b in zip(outs, blocks)]


def scatter_stages(planes, part, out, a_r, c_r, b_x, b_y, total, z_r, *sems):
    ax_s, ax_r, ay_s, ay_r, cx_s, cx_r, cy_s, cy_r, z_s, up_r, down_r = sems
    me, z, y, x, x_near, y_near = place()
    rows, cols = part.shape[2:]
    step = 16

    def slot(p, yy, xx):
        return p * PLANE + yy * 2 + xx

    def add(dst, *srcs):
        def body(i, carry):
            r = pl.ds(pl.multiple_of(i * step, step), step)
            acc = srcs[0][r, :].astype(jnp.float32)
            for s in srcs[1:]:
                acc = acc + s[r, :].astype(jnp.float32)
            dst[r, :] = acc.astype(dst.dtype)
            return carry

        lax.fori_loop(0, rows // step, body, 0)

    def diagonal(p):
        src = slot(p, 1 - y, 1 - x)
        return (
            remote(part.at[src, 0], a_r.at[p, 0], ay_s.at[p], ay_r.at[p], y_near),
            remote(part.at[src, 1], a_r.at[p, 1], ax_s.at[p], ax_r.at[p], x_near),
        )

    def beside(p):
        return (
            remote(b_x.at[p, 0], c_r.at[p, 0, 0], cx_s.at[p, 0], cx_r.at[p, 0], x_near),
            remote(part.at[slot(p, y, 1 - x), 1], c_r.at[p, 0, 1], cx_s.at[p, 1], cx_r.at[p, 1], x_near),
            remote(b_y.at[p, 0], c_r.at[p, 1, 1], cy_s.at[p, 0], cy_r.at[p, 0], y_near),
            remote(part.at[slot(p, 1 - y, x), 0], c_r.at[p, 1, 0], cy_s.at[p, 1], cy_r.at[p, 1], y_near),
        )

    def rise(p):
        return remote(total.at[p], z_r.at[0, p], z_s.at[p], up_r.at[p], me + PLANE)

    def sink(p):
        return remote(total.at[p], z_r.at[1, p], z_s.at[p], down_r.at[p], me - PLANE)

    def first(p, way):
        for copy in diagonal(p):
            copy.start()
        beside(p)[1].start()
        beside(p)[3].start()

    def second(p, way):
        to_y, to_x = diagonal(p)
        to_y.wait_recv()
        add(b_x.at[p, 0], part.at[slot(p, y, 1 - x), 0], a_r.at[p, 0])
        beside(p)[0].start()
        to_x.wait_recv()
        add(b_y.at[p, 0], part.at[slot(p, 1 - y, x), 1], a_r.at[p, 1])
        beside(p)[2].start()

    def third(p, way):
        for copy in beside(p):
            copy.wait_recv()
        for h in range(2):
            add(total.at[p, h], part.at[slot(p, y, x), h], c_r.at[p, 0, h], c_r.at[p, 1, h])

        def take(copy, level):
            copy.wait_recv()
            for h in range(2):
                add(total.at[p, h], total.at[p, h], z_r.at[level, p, h])

        if way >= 0:

            @pl.when(z > 0)
            def _():
                take(rise(p), 0)

        if way <= 0:

            @pl.when(z < planes - 1)
            def _():
                take(sink(p), 1)

        if way > 0:
            rise(p).start()
        if way < 0:
            sink(p).start()
        if way == 0:
            out[...] = total[p]

    def finish(p, way):
        for copy in diagonal(p) + beside(p):
            copy.wait_send()
        if way != 0:
            rise(p).wait_send()

    return (first, second, third, finish)


def scatter_kernel(planes, count, *refs):
    parts, outs, rest = refs[:count], refs[count : 2 * count], refs[2 * count :]
    per = len(rest) // count
    z = place()[1]
    stages = [
        scatter_stages(planes, parts[k], outs[k], *rest[k * per : (k + 1) * per])
        for k in range(count)
    ]

    def each(d, act):
        if d == 0:
            act(z, 0)
            return

        @pl.when(z >= d)
        def _():
            act(z - d, -1)

        @pl.when(z + d < planes)
        def _():
            act(z + d, 1)

    greet(planes)
    order = list(range(planes - 1, -1, -1))
    for k in range(count):
        for d in order:
            each(d, stages[k][0])
    for i, d in enumerate(order):
        for k in range(count):
            each(d, stages[k][1])
        if i > 0:
            for k in range(count):
                each(order[i - 1], stages[k][2])
    for k in range(count):
        each(0, stages[k][2])
    for k in range(count):
        for d in order:
            each(d, stages[k][3])


def scatter_sums(parts, collective_id):
    n = lax.axis_size("expert")
    planes = n // PLANE
    tokens, cols = parts[0].shape
    rows = tokens // n // 2
    half = (rows, cols)
    kind = parts[0].dtype
    count = len(parts)
    if count > 1 and count * 3 * parts[0].size * kind.itemsize > 56 << 20:
        return [scatter_sums([part], collective_id + k)[0] for k, part in enumerate(parts)]
    outs = pl.pallas_call(
        functools.partial(scatter_kernel, planes, count),
        out_shape=[jax.ShapeDtypeStruct((2,) + half, kind)] * count,
        in_specs=[pl.BlockSpec(memory_space=pltpu.VMEM)] * count,
        out_specs=[pl.BlockSpec(memory_space=pltpu.VMEM)] * count,
        scratch_shapes=(
            [
                pltpu.VMEM((planes, 2) + half, kind),
                pltpu.VMEM((planes, 2, 2) + half, kind),
                pltpu.VMEM((planes, 1) + half, kind),
                pltpu.VMEM((planes, 1) + half, kind),
                pltpu.VMEM((planes, 2) + half, kind),
                pltpu.VMEM((2, planes, 2) + half, kind),
            ]
            + [DMA((planes,))] * 4
            + [DMA((planes, 2))] * 4
            + [DMA((planes,))] * 3
        )
        * count,
        compiler_params=pltpu.CompilerParams(
            collective_id=collective_id, has_side_effects=True, vmem_limit_bytes=60 << 20
        ),
    )(*[part.reshape((n, 2) + half) for part in parts])
    return [out.reshape(2 * rows, cols) for out in outs]


def prepare(hidden, routes, router_segment):
    expert_count = router_segment.shape[0]
    hidden32 = hidden.astype(jnp.float32)
    rinv = lax.rsqrt(jnp.mean(hidden32 * hidden32, axis=-1, keepdims=True) + EPSILON)
    normed = (hidden32 * rinv).astype(jnp.bfloat16)
    logits = jnp.einsum("td,ed->te", normed, router_segment, preferred_element_type=jnp.float32)
    chosen = jnp.any(
        routes[:, :, None] == jnp.arange(expert_count, dtype=jnp.int32)[None, None, :], axis=1
    )
    affinity = jnp.where(chosen, jax.nn.sigmoid(logits), 0.0)
    return (hidden32, rinv, normed, affinity)


def on_device(hidden_a, routes_a, hidden_b, routes_b, grad_out_b, router, w_up, w_down):
    n_expert = lax.axis_size("expert")
    me = lax.axis_index("expert")
    tok_count = hidden_a.shape[1]
    router_segment = router[0]
    expert_count = router_segment.shape[0]
    local_count = w_up.shape[1]
    hidden32_a, rinv_a, normed_a, affinity_a = prepare(hidden_a[0], routes_a[0], router_segment)
    hidden32_b, rinv_b, normed_b, affinity_b = prepare(hidden_b[0], routes_b[0], router_segment)
    grad_out = grad_out_b[0]
    affinity_ab = jnp.concatenate([affinity_a, affinity_b], axis=1)
    lanes = -(-2 * expert_count // 128) * 128
    affinity_ab = jnp.pad(affinity_ab, ((0, 0), (0, lanes - 2 * expert_count)))
    rows_a, rows_b, rows_g, affinities = gather_all([normed_a, normed_b, grad_out, affinity_ab], 1)
    aff_a, aff_b = affinities[:, :expert_count], affinities[:, expert_count : 2 * expert_count]
    total_b = jnp.sum(aff_b, axis=1, keepdims=True)
    weight_a = aff_a / jnp.sum(aff_a, axis=1, keepdims=True)
    weight_b = aff_b / total_b

    def column(table, local):
        return lax.dynamic_slice_in_dim(table, me * local_count + local, 1, axis=1)

    sum_a = 0.0
    sum_b = 0.0
    scores = []
    for local in range(local_count):
        up, down = w_up[0, local], w_down[0, local]
        pre = jnp.dot(rows_a, up, preferred_element_type=jnp.float32)
        active = jax.nn.silu(pre).astype(jnp.bfloat16)
        out = jnp.dot(active, down, preferred_element_type=jnp.float32)
        sum_a = sum_a + out * column(weight_a, local)
    for local in range(local_count):
        up, down = w_up[0, local], w_down[0, local]
        pre = jnp.dot(rows_b, up, preferred_element_type=jnp.float32)
        back = jnp.einsum("td,fd->tf", rows_g, down, preferred_element_type=jnp.float32)
        sig = jax.nn.sigmoid(pre)
        scores.append(jnp.sum(back * (pre * sig), axis=-1))
        inner = (back * (sig * (1.0 + pre * (1.0 - sig)))).astype(jnp.bfloat16)
        lifted = jnp.einsum("tf,df->td", inner, up, preferred_element_type=jnp.float32)
        sum_b = sum_b + lifted * column(weight_b, local)
    sum_ab = scatter_sums([sum_a.astype(jnp.bfloat16), sum_b.astype(jnp.bfloat16)], 2)
    mixed = sum_ab[0].astype(jnp.float32)
    layer_out = (hidden32_a + ROUTED_SCALE * mixed).astype(jnp.bfloat16)

    flat = jnp.stack(scores).reshape(-1)
    padded = jnp.pad(flat, (0, -flat.shape[0] % 2048)).reshape(-1, 128)
    score = gather_all([padded], 4)[0].reshape(n_expert, -1)[:, : flat.shape[0]]
    score = score.reshape(expert_count, -1).T
    score = jnp.where(aff_b > 0.0, score, 0.0)
    gate_grad = ROUTED_SCALE * score
    logit_grad = (
        aff_b
        * (1.0 - aff_b)
        * (gate_grad - jnp.sum(gate_grad * weight_b, axis=1, keepdims=True))
        / total_b
    )
    own_columns = lax.dynamic_slice_in_dim(logit_grad, me * local_count, local_count, axis=1)
    own_term = jnp.dot(
        own_columns.T, rows_b.astype(jnp.float32), precision=lax.Precision.HIGHEST
    )
    mirrored = own_term
    for bit in range(lax.axis_size("pipe").bit_length() - 1):
        mirrored = partner(mirrored, "pipe", bit)
    router_grad = own_term + mirrored

    dense = lax.dynamic_slice_in_dim(logit_grad, me * tok_count, tok_count, axis=0)
    lifted_sum = sum_ab[1].astype(jnp.float32)
    normed_grad = ROUTED_SCALE * lifted_sum + jnp.dot(
        dense, router_segment.astype(jnp.float32), precision=lax.Precision.HIGHEST
    )
    mean_term = jnp.mean(normed_grad * hidden32_b, axis=-1, keepdims=True)
    grad_in = (
        grad_out.astype(jnp.float32) + rinv_b * normed_grad - hidden32_b * rinv_b**3 * mean_term
    )
    return (layer_out[None], grad_in.astype(jnp.bfloat16)[None], router_grad[None])


def fused_kernel(dims, *refs):
    planes, tok, depth, width, dc, n_up, n_pipe = dims
    (a, b, g, tab, wu, wd, out, lg_out, rg_out) = refs[:9]
    (rows, tabs, wu_b, wd_b, bu, bd, act, pre, back) = refs[9:18]
    (o_buf, y_buf, t_buf, z_buf, sc_col, sc_own, sc_all, rg_buf, rg_in) = refs[18:27]
    (own_s, zs, zr, ys, yr, xs, xr, ms, mr, bus, bds) = refs[27:38]
    (rys, ryr, rzs, rzr, scs, scr, gs, gr) = refs[38:46]
    slots = 2 * planes
    m_rows = slots * tok
    chunks = depth // dc
    half_d = depth // 2
    half_f = width // 2
    up_rows = half_d // n_up
    tile = 256
    me, z, y, x, x_near, y_near = place()
    p = lax.axis_index("pipe")
    mirror = n_pipe - 1 - p
    part = (2 * p) // n_pipe
    slot_me = y * planes + z

    def copy(src, dst, send, recv, expert, pipe=p):
        return pltpu.make_async_remote_copy(
            src_ref=src,
            dst_ref=dst,
            send_sem=send,
            recv_sem=recv,
            device_id={"pipe": pipe, "expert": expert},
            device_id_type=MESH,
        )

    def chip(plane, row):
        return plane * PLANE + row * 2 + x

    def of_slot(s):
        return chip(s % planes, s // planes)

    barrier = pltpu.get_barrier_semaphore()

    def hello(pipe, expert):
        pl.semaphore_signal(
            barrier, inc=1, device_id={"pipe": pipe, "expert": expert}, device_id_type=MESH
        )

    for i in range(1, slots):
        hello(p, of_slot((slot_me + i) % slots))
    hello(p, x_near)
    hello(mirror, me)
    hello(mirror, x_near)
    pl.semaphore_wait(barrier, slots - 1 + 3)

    def up_region(which, i):
        return pl.ds(pl.multiple_of(which * half_d + i * up_rows, up_rows), up_rows)

    def up_x(i):
        r = up_region(part, i)
        return copy(wu.at[r], wu_b.at[r], xs.at[i], xr.at[i], x_near)

    def up_m(i, which):
        r = up_region(which, i)
        return copy(wu_b.at[r], wu_b.at[r], ms.at[i], mr.at[i], me, mirror)

    def down_rows(which):
        return pl.ds(pl.multiple_of(which * half_f, half_f), half_f)

    def columns(c):
        return pl.ds(pl.multiple_of(c * dc, dc), dc)

    def down_x(c):
        r = down_rows(part)
        src = wd.at[r, columns(c)]
        return copy(src, wd_b.at[c, r], xs.at[n_up + c], xr.at[n_up + c], x_near)

    def down_m(c, which):
        ref = wd_b.at[c, down_rows(which)]
        return copy(ref, ref, ms.at[n_up + c], mr.at[n_up + c], me, mirror)

    for i in range(n_up):
        up_x(i).start()
    for c in range(chunks):
        down_x(c).start()

    ins = [tab, a, b, g]
    bufs = [tabs, rows.at[0], rows.at[1], rows.at[2]]

    def z_copy(k, d, slot):
        target = chip((z + d) % planes, y)
        return copy(ins[k], bufs[k].at[slot], zs.at[k, d - 1], zr.at[k, d - 1], target)

    def y_copy(k, d, row):
        ref = bufs[k].at[row * planes + (z - d + planes) % planes]
        src = ins[k] if isinstance(d, int) and d == 0 else ref
        return copy(src, ref, ys.at[k, d], yr.at[k, d], y_near)

    if planes == 4:
        low, top = (3 - z) // 3, z // 3
        sources = [1 + 2 * low, 3 - low - top, 2 - low + top]
        targets = [1 + 2 * top, 3 - low - top, 2 + low - top]
    else:
        sources = targets = list(range(1, planes))

    def serve(k, i):
        d = sources[i]
        z_copy(k, d, y * planes + (z - d + planes) % planes).wait_recv()
        y_copy(k, d, y).start()

    def arrived(k):
        for d in range(planes):
            y_copy(k, d, 1 - y).wait_recv()

    for k in range(4):
        y_copy(k, 0, y).start()
        for d in targets:
            z_copy(k, d, slot_me).start()
    own = [pltpu.make_async_copy(ins[k], bufs[k].at[slot_me], own_s.at[k]) for k in range(4)]
    for k in range(4):
        own[k].start()

    def chunk_of(k, c):
        return rows[k, :, :, columns(c)].reshape(m_rows, dc)

    def nn(lhs, rhs):
        return jnp.dot(lhs, rhs, preferred_element_type=jnp.float32)

    def nt(lhs, rhs):
        return lax.dot_general(
            lhs, rhs, (((1,), (1,)), ((), ())), preferred_element_type=jnp.float32
        )

    def load_up(c):
        return pltpu.make_async_copy(wu.at[columns(c)], bu.at[c % 2], bus.at[c % 2])

    def load_down(c):
        return pltpu.make_async_copy(wd.at[:, columns(c)], bd.at[c % 2], bds.at[c % 2])

    def next_chunk(load, c):
        load(c).wait()

        @pl.when(c + 1 < chunks)
        def _():
            load(c + 1).start()

    def clear(dst):
        def body(s, carry):
            dst[pl.ds(pl.multiple_of(s * tok, tok), tok), :] = jnp.zeros((tok, width), jnp.float32)
            return carry

        lax.fori_loop(0, slots, body, 0)

    def project(k, partner, dst):
        clear(dst)
        if not partner:
            load_up(0).start()

        def body(c, carry):
            if not partner:
                next_chunk(load_up, c)
            lhs = chunk_of(k, c)
            for n in range(width // tile):
                cols = pl.ds(n * tile, tile)
                rhs = wu_b[columns(c), cols] if partner else bu[c % 2, :, cols]
                dst[:, cols] += nn(lhs, rhs)
            return carry

        lax.fori_loop(0, chunks, body, 0)

    lane = lax.broadcasted_iota(jnp.int32, (tok, tabs.shape[-1]), 1)

    def pick(s, column):
        return jnp.sum(jnp.where(lane == column, tabs[s], 0.0), axis=-1, keepdims=True)

    experts = 2 * slots
    expert_of = [me, x_near]

    def activate(which, src):
        def body(s, carry):
            r = pl.ds(pl.multiple_of(s * tok, tok), tok)
            v = src[r, :]
            act[which, r, :] = (v * jax.nn.sigmoid(v) * pick(s, expert_of[which])).astype(act.dtype)
            return carry

        lax.fori_loop(0, slots, body, 0)

    def invert():
        def body(s, carry):
            r = pl.ds(pl.multiple_of(s * tok, tok), tok)
            scores = []
            for which in range(2):
                v = pre[which, r, :]
                bk = back[which, r, :]
                sig = jax.nn.sigmoid(v)
                scores.append(jnp.sum(bk * (v * sig), axis=-1, keepdims=True))
                inner = bk * (sig * (1.0 + v * (1.0 - sig)))
                weight = pick(s, experts + expert_of[which])
                act[which, r, :] = (inner * weight).astype(act.dtype)
            even = jnp.where(x == 0, scores[0], scores[1])
            odd = jnp.where(x == 0, scores[1], scores[0])
            sc_col[s] = jnp.where(lane == 0, even, jnp.where(lane == 1, odd, 0.0))
            return carry

        lax.fori_loop(0, slots, body, 0)
        sc_own[...] = sc_col[...].reshape(m_rows, lane.shape[1]).T[:8]

    steps = 2 * chunks

    def rs_y(q):
        src = o_buf.at[q, pl.ds((1 - y) * planes, planes)]
        return copy(src, y_buf.at[q], rys.at[q], ryr.at[q], y_near)

    def rs_z(q, d):
        plane = (z + d) % planes
        src = t_buf.at[q, plane]
        return copy(src, z_buf.at[q, d - 1], rzs.at[q, d - 1], rzr.at[q, d - 1], chip(plane, y))

    def fold_y(q):
        rs_y(q).wait_recv()
        for k in range(planes):
            both = o_buf[q, y * planes + k].astype(jnp.float32) + y_buf[q, k].astype(jnp.float32)
            t_buf[q, k] = both.astype(t_buf.dtype)
        for d in targets:
            rs_z(q, d).start()

    def fold_z(q):
        total = t_buf[q, z].astype(jnp.float32)
        for d in range(1, planes):
            rs_z(q, d).wait_recv()
            total = total + z_buf[q, d - 1].astype(jnp.float32)
        out[q // chunks, :, columns(q % chunks)] = total

    def behind(q):
        @pl.when(q >= 2)
        def _():
            fold_y(q - 2)

        @pl.when(q >= 4)
        def _():
            fold_z(q - 4)

    def store(q, n, value):
        cols = pl.ds(n * tile, tile)
        o_buf[q, :, :, cols] = value.reshape(slots, tok, tile).astype(o_buf.dtype)

    for k in range(3):
        for i in range(planes - 1):
            serve(k, i)
    for k in range(4):
        own[k].wait()
    arrived(0)
    arrived(1)
    project(0, False, back.at[0])
    activate(0, back.at[0])
    serve(3, 0)
    for i in range(n_up):
        up_x(i).wait_recv()
        up_m(i, part).start()
    for i in range(n_up):
        up_m(i, 1 - part).wait_recv()
    project(0, True, back.at[1])
    activate(1, back.at[1])
    for i in range(1, planes - 2):
        serve(3, i)
    arrived(2)
    project(1, False, pre.at[0])
    for i in range(max(1, planes - 2), planes - 1):
        serve(3, i)
    project(1, True, pre.at[1])
    clear(back.at[0])
    clear(back.at[1])
    load_down(0).start()
    down_x(0).wait_recv()
    down_m(0, part).start()
    arrived(3)

    def forward(c, carry):
        next_chunk(load_down, c)
        down_m(c, 1 - part).wait_recv()
        for n in range(dc // tile):
            cols = pl.ds(n * tile, tile)
            store(c, n, nn(act[0], bd[c % 2, :, cols]) + nn(act[1], wd_b[c, :, cols]))
        rs_y(c).start()
        lhs = chunk_of(2, c)
        for n in range(width // tile):
            cols = pl.ds(n * tile, tile)
            back[0, :, cols] += nt(lhs, bd[c % 2, cols, :])
            back[1, :, cols] += nt(lhs, wd_b[c, cols, :])

        @pl.when(c + 1 < chunks)
        def _():
            down_x(c + 1).wait_recv()
            down_m(c + 1, part).start()

        behind(c)
        return carry

    lax.fori_loop(0, chunks, forward, 0)
    load_up(0).start()
    invert()

    def score_copy(i, slot):
        target = of_slot((slot_me + i) % slots)
        return copy(sc_own, sc_all.at[slot], scs.at[i - 1], scr.at[i - 1], target)

    for i in range(1, slots):
        score_copy(i, slot_me).start()

    def backward(c, carry):
        next_chunk(load_up, c)
        q = chunks + c
        for n in range(dc // tile):
            cols = pl.ds(n * tile, tile)
            shared = pl.ds(pl.multiple_of(c * dc + n * tile, tile), tile)
            store(q, n, nt(act[0], bu[c % 2, cols, :]) + nt(act[1], wu_b[shared, :]))
        rs_y(q).start()
        behind(q)
        return carry

    lax.fori_loop(0, chunks, backward, 0)

    sc_all[slot_me] = sc_own[...]
    for i in range(1, slots):
        score_copy(i, (slot_me - i + slots) % slots).wait_recv()
    table = tabs[...].reshape(m_rows, lane.shape[1]).T
    lines = []
    for e in range(experts):
        plane, row, odd = e // PLANE, (e // 2) % 2, e % 2
        lines.append(sc_all[row * planes + plane, odd : odd + 1, :])
    score = jnp.concatenate(lines, axis=0)
    gate = ROUTED_SCALE * score
    mean = jnp.sum(gate * table[experts : 2 * experts], axis=0, keepdims=True)
    logit = table[2 * experts : 3 * experts] * (gate - mean)
    lg_out[...] = logit
    order = lax.broadcasted_iota(jnp.int32, (experts, m_rows), 0)
    mine = jnp.sum(jnp.where(order == me, logit, 0.0), axis=0, keepdims=True)
    theirs = jnp.sum(jnp.where(order == x_near, logit, 0.0), axis=0, keepdims=True)
    both = jnp.concatenate([mine, theirs, jnp.zeros((6, m_rows), jnp.float32)], axis=0)
    high = both.astype(jnp.bfloat16)
    rest = both - high.astype(jnp.float32)
    middle = rest.astype(jnp.bfloat16)
    last = (rest - middle.astype(jnp.float32)).astype(jnp.bfloat16)
    for c in range(chunks):
        cols = pl.ds(c * dc, dc)
        rhs = rows[1, :, :, cols].reshape(m_rows, dc)
        rg_buf[:, cols] = nn(high, rhs) + nn(middle, rhs) + nn(last, rhs)

    def grad_copy(i):
        expert = me if i == 0 else x_near
        pipe = p if i == 1 else mirror
        return copy(rg_buf, rg_in.at[i], gs.at[i], gr.at[i], expert, pipe)

    for i in range(3):
        grad_copy(i).start()
    for q in range(steps - 2, steps):
        fold_y(q)
        fold_z(q - 2)
    for i in range(3):
        grad_copy(i).wait_recv()
    rg_out[...] = rg_buf[0:1, :] + rg_in[0, 0:1, :] + rg_in[1, 1:2, :] + rg_in[2, 1:2, :]
    for q in range(steps - 2, steps):
        fold_z(q)

    for k in range(4):
        for d in range(1, planes):
            z_copy(k, d, slot_me).wait_send()
        for d in range(planes):
            y_copy(k, d, y).wait_send()
    for i in range(n_up):
        up_x(i).wait_send()
        up_m(i, part).wait_send()

    def drain(c, carry):
        down_x(c).wait_send()
        down_m(c, part).wait_send()
        return carry

    lax.fori_loop(0, chunks, drain, 0)

    def drain_rs(q, carry):
        rs_y(q).wait_send()
        for d in range(1, planes):
            rs_z(q, d).wait_send()
        return carry

    lax.fori_loop(0, steps, drain_rs, 0)
    for i in range(1, slots):
        score_copy(i, slot_me).wait_send()
    for i in range(3):
        grad_copy(i).wait_send()


N_UP = 4


def fused_plan(n, tok, depth, width):
    planes = n // PLANE
    slots = 2 * planes
    m_rows = slots * tok
    dc = 512 if depth % 512 == 0 else 256
    chunks = depth // dc
    steps = 2 * chunks
    bf, f32 = jnp.bfloat16, jnp.float32
    buffers = [
        ((3, slots, tok, depth), bf),
        ((slots, tok, 128), f32),
        ((depth, width), bf),
        ((chunks, width, dc), bf),
        ((2, dc, width), bf),
        ((2, width, dc), bf),
        ((2, m_rows, width), bf),
        ((2, m_rows, width), f32),
        ((2, m_rows, width), f32),
        ((steps, slots, tok, dc), bf),
        ((steps, planes, tok, dc), bf),
        ((steps, planes, tok, dc), bf),
        ((steps, planes - 1, tok, dc), bf),
        ((slots, tok, 128), f32),
        ((8, m_rows), f32),
        ((slots, 8, m_rows), f32),
        ((8, depth), f32),
        ((3, 8, depth), f32),
    ]
    sems = [
        (4,),
        (4, planes - 1),
        (4, planes - 1),
        (4, planes),
        (4, planes),
        (N_UP + chunks,),
        (N_UP + chunks,),
        (N_UP + chunks,),
        (N_UP + chunks,),
        (2,),
        (2,),
        (steps,),
        (steps,),
        (steps, planes - 1),
        (steps, planes - 1),
        (slots - 1,),
        (slots - 1,),
        (3,),
        (3,),
    ]
    total = sum(math.prod(shape) * jnp.dtype(kind).itemsize for shape, kind in buffers)
    outs = 2 * tok * depth * 4 + 3 * tok * depth * 2
    fits = total + outs < 64_500_000 and 3 * n <= 128
    return fits, (planes, tok, depth, width, dc, N_UP), buffers, sems


def fused(normed_a, normed_b, grad_out, table, up, down, plan):
    _, dims, buffers, sems = plan
    planes, tok, depth = dims[:3]
    slots = 2 * planes
    vmem = pl.BlockSpec(memory_space=pltpu.VMEM)
    hbm = pl.BlockSpec(memory_space=pl.ANY)
    return pl.pallas_call(
        functools.partial(fused_kernel, dims + (lax.axis_size("pipe"),)),
        out_shape=[
            jax.ShapeDtypeStruct((2, tok, depth), jnp.float32),
            jax.ShapeDtypeStruct((2 * slots, slots * tok), jnp.float32),
            jax.ShapeDtypeStruct((1, depth), jnp.float32),
        ],
        in_specs=[vmem] * 4 + [hbm] * 2,
        out_specs=[vmem] * 3,
        scratch_shapes=[pltpu.VMEM(shape, kind) for shape, kind in buffers]
        + [DMA(shape) for shape in sems],
        compiler_params=pltpu.CompilerParams(
            collective_id=7, has_side_effects=True, vmem_limit_bytes=67_000_000
        ),
    )(normed_a, normed_b, grad_out, table, up, down)


def on_device_fused(
    plan, hidden_a, routes_a, hidden_b, routes_b, grad_out_b, router, w_up, w_down
):
    router_segment = router[0]
    n_expert = router_segment.shape[0]
    planes, tok = plan[1][:2]
    hidden32_a, rinv_a, normed_a, affinity_a = prepare(hidden_a[0], routes_a[0], router_segment)
    hidden32_b, rinv_b, normed_b, affinity_b = prepare(hidden_b[0], routes_b[0], router_segment)
    grad_out = grad_out_b[0]
    total_b = jnp.sum(affinity_b, axis=1, keepdims=True)
    weight_a = affinity_a / jnp.sum(affinity_a, axis=1, keepdims=True)
    weight_b = affinity_b / total_b
    slope_b = affinity_b * (1.0 - affinity_b) / total_b
    table = jnp.concatenate([weight_a, weight_b, slope_b], axis=1)
    table = jnp.pad(table, ((0, 0), (0, 128 - 3 * n_expert)))
    sums, logit_grad, router_grad = fused(
        normed_a, normed_b, grad_out, table, w_up[0, 0], w_down[0, 0], plan
    )
    layer_out = (hidden32_a + ROUTED_SCALE * sums[0]).astype(jnp.bfloat16)
    _, z, y, _, _, _ = place()
    dense = lax.dynamic_slice_in_dim(logit_grad, (y * planes + z) * tok, tok, axis=1)
    normed_grad = ROUTED_SCALE * sums[1] + jnp.einsum(
        "et,ed->td", dense, router_segment.astype(jnp.float32), precision=lax.Precision.HIGHEST
    )
    mean_term = jnp.mean(normed_grad * hidden32_b, axis=-1, keepdims=True)
    grad_in = (
        grad_out.astype(jnp.float32) + rinv_b * normed_grad - hidden32_b * rinv_b**3 * mean_term
    )
    return (layer_out[None], grad_in.astype(jnp.bfloat16)[None], router_grad[None])


def solution(mesh):
    placed = (
        P("pipe", "expert", None),
        P("pipe", "expert", None),
        P("pipe", "expert", None),
        P("pipe", "expert", None),
        P("pipe", "expert", None),
        P("pipe", None, None),
        P("pipe", "expert", None, None),
        P("pipe", "expert", None, None),
    )

    def body(*args):
        w_up = args[6]
        plan = fused_plan(lax.axis_size("expert"), args[0].shape[1], w_up.shape[2], w_up.shape[3])
        if w_up.shape[1] == 1 and plan[0]:
            return on_device_fused(plan, *args)
        return on_device(*args)

    return jax.shard_map(
        body,
        mesh=mesh,
        in_specs=placed,
        out_specs=(P("pipe", "expert", None), P("pipe", "expert", None), P("pipe", "expert", None)),
        check_vma=False,
    )
```

```python
import functools
import math

import jax
import jax.numpy as jnp
from jax import lax
from jax.experimental import pallas as pl
from jax.experimental.pallas import tpu as pltpu
from jax.sharding import PartitionSpec as P

ROUTED_SCALE = 2.5
EPSILON = 1e-06


def partner(block, axis, bit):
    count = lax.axis_size(axis)
    route = []
    for low in range(count):
        high = low | 1 << bit
        if high != low and high < count:
            route += [(low, high), (high, low)]
    return lax.ppermute(block, axis, route)


MESH = pl.DeviceIdType.MESH
DMA = pltpu.SemaphoreType.DMA
PLANE = 4


def remote(src, dst, send_sem, recv_sem, target):
    return pltpu.make_async_remote_copy(
        src_ref=src,
        dst_ref=dst,
        send_sem=send_sem,
        recv_sem=recv_sem,
        device_id={"expert": target},
        device_id_type=MESH,
    )


def place():
    me = lax.axis_index("expert")
    z, y, x = me // PLANE, (me // 2) % 2, me % 2
    return (me, z, y, x, me + 1 - 2 * x, me + 2 - 4 * y)


def greet(planes):
    me, z, y, x, x_near, y_near = place()
    barrier = pltpu.get_barrier_semaphore()
    pl.semaphore_signal(barrier, inc=1, device_id={"expert": x_near}, device_id_type=MESH)
    pl.semaphore_signal(barrier, inc=1, device_id={"expert": y_near}, device_id_type=MESH)

    @pl.when(z < planes - 1)
    def _():
        pl.semaphore_signal(barrier, inc=1, device_id={"expert": me + PLANE}, device_id_type=MESH)

    @pl.when(z > 0)
    def _():
        pl.semaphore_signal(barrier, inc=1, device_id={"expert": me - PLANE}, device_id_type=MESH)

    ends = jnp.where(z == 0, 1, 0) + jnp.where(z == planes - 1, 1, 0)
    pl.semaphore_wait(barrier, 4 - ends)


def gather_kernel(count, planes, *refs):
    ins, outs = refs[:count], refs[count : 2 * count]
    own_sem, up_s, down_s, z_r, x_s, x_r, y_s, y_r, d_s, d_r = refs[2 * count :]
    me, z, y, x, x_near, y_near = place()

    def up(k, p, src):
        return remote(src, outs[k].at[p * PLANE + y * 2 + x], up_s.at[k, p], z_r.at[k, p], me + PLANE)

    def down(k, p, src):
        return remote(src, outs[k].at[p * PLANE + y * 2 + x], down_s.at[k, p], z_r.at[k, p], me - PLANE)

    def to_x(k, p, src):
        return remote(src, outs[k].at[p * PLANE + y * 2 + x], x_s.at[k, p], x_r.at[k, p], x_near)

    def to_y(k, p, src):
        return remote(src, outs[k].at[p * PLANE + y * 2 + x], y_s.at[k, p], y_r.at[k, p], y_near)

    def half(k, p, way):
        if way == 0:
            ref = outs[k].at[p * PLANE + y * 2 + 1 - x, 0]
            return remote(ref, ref, d_s.at[k, p, 0], d_r.at[k, p, 0], y_near)
        ref = outs[k].at[p * PLANE + (1 - y) * 2 + x, 1]
        return remote(ref, ref, d_s.at[k, p, 1], d_r.at[k, p, 1], x_near)

    def each(d, act):
        if d == 0:
            act(z, 0)
            return

        @pl.when(z >= d)
        def _():
            act(z - d, 1)

        @pl.when(z + d < planes)
        def _():
            act(z + d, -1)

    def spread(k, p, way, wait):
        src = ins[k] if way == 0 else outs[k].at[p * PLANE + y * 2 + x]

        def do(copy):
            copy.wait_send() if wait else copy.start()

        if way != 0 and not wait:
            up(k, p, src).wait_recv()
        if way >= 0:

            @pl.when(z < planes - 1)
            def _():
                do(up(k, p, src))

        if way <= 0:

            @pl.when(z > 0)
            def _():
                do(down(k, p, src))

        do(to_x(k, p, src))
        do(to_y(k, p, src))

    def relay(k, p, way):
        to_x(k, p, ins[k]).wait_recv()
        half(k, p, 0).start()
        to_y(k, p, ins[k]).wait_recv()
        half(k, p, 1).start()

    def finish(k, p, way):
        for route in range(2):
            half(k, p, route).wait()
        spread(k, p, way, True)

    greet(planes)
    for k in range(count):
        pltpu.make_async_copy(ins[k], outs[k].at[me], own_sem.at[k]).start()
        each(0, lambda p, way: spread(k, p, way, False))
    for k in range(count):
        for d in range(1, planes):
            each(d, lambda p, way: spread(k, p, way, False))
            each(d - 1, lambda p, way: relay(k, p, way))
        each(planes - 1, lambda p, way: relay(k, p, way))
    for k in range(count):
        for d in range(planes):
            each(d, lambda p, way: finish(k, p, way))
        pltpu.make_async_copy(ins[k], outs[k].at[me], own_sem.at[k]).wait()


def gather_all(blocks, collective_id):
    n = lax.axis_size("expert")
    planes = n // PLANE
    count = len(blocks)
    halved = [b.reshape(2, b.shape[0] // 2, b.shape[1]) for b in blocks]
    outs = pl.pallas_call(
        functools.partial(gather_kernel, count, planes),
        out_shape=[jax.ShapeDtypeStruct((n,) + b.shape, b.dtype) for b in halved],
        in_specs=[pl.BlockSpec(memory_space=pltpu.VMEM)] * count,
        out_specs=[pl.BlockSpec(memory_space=pl.ANY)] * count,
        scratch_shapes=[DMA((count,))] + [DMA((count, planes))] * 7 + [DMA((count, planes, 2))] * 2,
        compiler_params=pltpu.CompilerParams(collective_id=collective_id, has_side_effects=True),
    )(*halved)
    return [o.reshape(n * b.shape[0], b.shape[1]) for o, b in zip(outs, blocks)]


def scatter_stages(planes, part, out, a_r, c_r, b_x, b_y, total, z_r, *sems):
    ax_s, ax_r, ay_s, ay_r, cx_s, cx_r, cy_s, cy_r, z_s, up_r, down_r = sems
    me, z, y, x, x_near, y_near = place()
    rows, cols = part.shape[2:]
    step = 16

    def slot(p, yy, xx):
        return p * PLANE + yy * 2 + xx

    def add(dst, *srcs):
        def body(i, carry):
            r = pl.ds(pl.multiple_of(i * step, step), step)
            acc = srcs[0][r, :].astype(jnp.float32)
            for s in srcs[1:]:
                acc = acc + s[r, :].astype(jnp.float32)
            dst[r, :] = acc.astype(dst.dtype)
            return carry

        lax.fori_loop(0, rows // step, body, 0)

    def diagonal(p):
        src = slot(p, 1 - y, 1 - x)
        return (
            remote(part.at[src, 0], a_r.at[p, 0], ay_s.at[p], ay_r.at[p], y_near),
            remote(part.at[src, 1], a_r.at[p, 1], ax_s.at[p], ax_r.at[p], x_near),
        )

    def beside(p):
        return (
            remote(b_x.at[p, 0], c_r.at[p, 0, 0], cx_s.at[p, 0], cx_r.at[p, 0], x_near),
            remote(part.at[slot(p, y, 1 - x), 1], c_r.at[p, 0, 1], cx_s.at[p, 1], cx_r.at[p, 1], x_near),
            remote(b_y.at[p, 0], c_r.at[p, 1, 1], cy_s.at[p, 0], cy_r.at[p, 0], y_near),
            remote(part.at[slot(p, 1 - y, x), 0], c_r.at[p, 1, 0], cy_s.at[p, 1], cy_r.at[p, 1], y_near),
        )

    def rise(p):
        return remote(total.at[p], z_r.at[0, p], z_s.at[p], up_r.at[p], me + PLANE)

    def sink(p):
        return remote(total.at[p], z_r.at[1, p], z_s.at[p], down_r.at[p], me - PLANE)

    def first(p, way):
        for copy in diagonal(p):
            copy.start()
        beside(p)[1].start()
        beside(p)[3].start()

    def second(p, way):
        to_y, to_x = diagonal(p)
        to_y.wait_recv()
        add(b_x.at[p, 0], part.at[slot(p, y, 1 - x), 0], a_r.at[p, 0])
        beside(p)[0].start()
        to_x.wait_recv()
        add(b_y.at[p, 0], part.at[slot(p, 1 - y, x), 1], a_r.at[p, 1])
        beside(p)[2].start()

    def third(p, way):
        for copy in beside(p):
            copy.wait_recv()
        for h in range(2):
            add(total.at[p, h], part.at[slot(p, y, x), h], c_r.at[p, 0, h], c_r.at[p, 1, h])

        def take(copy, level):
            copy.wait_recv()
            for h in range(2):
                add(total.at[p, h], total.at[p, h], z_r.at[level, p, h])

        if way >= 0:

            @pl.when(z > 0)
            def _():
                take(rise(p), 0)

        if way <= 0:

            @pl.when(z < planes - 1)
            def _():
                take(sink(p), 1)

        if way > 0:
            rise(p).start()
        if way < 0:
            sink(p).start()
        if way == 0:
            out[...] = total[p]

    def finish(p, way):
        for copy in diagonal(p) + beside(p):
            copy.wait_send()
        if way != 0:
            rise(p).wait_send()

    return (first, second, third, finish)


def scatter_kernel(planes, count, *refs):
    parts, outs, rest = refs[:count], refs[count : 2 * count], refs[2 * count :]
    per = len(rest) // count
    z = place()[1]
    stages = [
        scatter_stages(planes, parts[k], outs[k], *rest[k * per : (k + 1) * per])
        for k in range(count)
    ]

    def each(d, act):
        if d == 0:
            act(z, 0)
            return

        @pl.when(z >= d)
        def _():
            act(z - d, -1)

        @pl.when(z + d < planes)
        def _():
            act(z + d, 1)

    greet(planes)
    order = list(range(planes - 1, -1, -1))
    for k in range(count):
        for d in order:
            each(d, stages[k][0])
    for i, d in enumerate(order):
        for k in range(count):
            each(d, stages[k][1])
        if i > 0:
            for k in range(count):
                each(order[i - 1], stages[k][2])
    for k in range(count):
        each(0, stages[k][2])
    for k in range(count):
        for d in order:
            each(d, stages[k][3])


def scatter_sums(parts, collective_id):
    n = lax.axis_size("expert")
    planes = n // PLANE
    tokens, cols = parts[0].shape
    rows = tokens // n // 2
    half = (rows, cols)
    kind = parts[0].dtype
    count = len(parts)
    if count > 1 and count * 3 * parts[0].size * kind.itemsize > 56 << 20:
        return [scatter_sums([part], collective_id + k)[0] for k, part in enumerate(parts)]
    outs = pl.pallas_call(
        functools.partial(scatter_kernel, planes, count),
        out_shape=[jax.ShapeDtypeStruct((2,) + half, kind)] * count,
        in_specs=[pl.BlockSpec(memory_space=pltpu.VMEM)] * count,
        out_specs=[pl.BlockSpec(memory_space=pltpu.VMEM)] * count,
        scratch_shapes=(
            [
                pltpu.VMEM((planes, 2) + half, kind),
                pltpu.VMEM((planes, 2, 2) + half, kind),
                pltpu.VMEM((planes, 1) + half, kind),
                pltpu.VMEM((planes, 1) + half, kind),
                pltpu.VMEM((planes, 2) + half, kind),
                pltpu.VMEM((2, planes, 2) + half, kind),
            ]
            + [DMA((planes,))] * 4
            + [DMA((planes, 2))] * 4
            + [DMA((planes,))] * 3
        )
        * count,
        compiler_params=pltpu.CompilerParams(
            collective_id=collective_id, has_side_effects=True, vmem_limit_bytes=60 << 20
        ),
    )(*[part.reshape((n, 2) + half) for part in parts])
    return [out.reshape(2 * rows, cols) for out in outs]


def prepare(hidden, routes, router_segment):
    expert_count = router_segment.shape[0]
    hidden32 = hidden.astype(jnp.float32)
    rinv = lax.rsqrt(jnp.mean(hidden32 * hidden32, axis=-1, keepdims=True) + EPSILON)
    normed = (hidden32 * rinv).astype(jnp.bfloat16)
    logits = jnp.einsum("td,ed->te", normed, router_segment, preferred_element_type=jnp.float32)
    chosen = jnp.any(
        routes[:, :, None] == jnp.arange(expert_count, dtype=jnp.int32)[None, None, :], axis=1
    )
    affinity = jnp.where(chosen, jax.nn.sigmoid(logits), 0.0)
    return (hidden32, rinv, normed, affinity)


def on_device(hidden_a, routes_a, hidden_b, routes_b, grad_out_b, router, w_up, w_down):
    n_expert = lax.axis_size("expert")
    me = lax.axis_index("expert")
    tok_count = hidden_a.shape[1]
    router_segment = router[0]
    expert_count = router_segment.shape[0]
    local_count = w_up.shape[1]
    hidden32_a, rinv_a, normed_a, affinity_a = prepare(hidden_a[0], routes_a[0], router_segment)
    hidden32_b, rinv_b, normed_b, affinity_b = prepare(hidden_b[0], routes_b[0], router_segment)
    grad_out = grad_out_b[0]
    affinity_ab = jnp.concatenate([affinity_a, affinity_b], axis=1)
    lanes = -(-2 * expert_count // 128) * 128
    affinity_ab = jnp.pad(affinity_ab, ((0, 0), (0, lanes - 2 * expert_count)))
    rows_a, rows_b, rows_g, affinities = gather_all([normed_a, normed_b, grad_out, affinity_ab], 1)
    aff_a, aff_b = affinities[:, :expert_count], affinities[:, expert_count : 2 * expert_count]
    total_b = jnp.sum(aff_b, axis=1, keepdims=True)
    weight_a = aff_a / jnp.sum(aff_a, axis=1, keepdims=True)
    weight_b = aff_b / total_b

    def column(table, local):
        return lax.dynamic_slice_in_dim(table, me * local_count + local, 1, axis=1)

    sum_a = 0.0
    sum_b = 0.0
    scores = []
    for local in range(local_count):
        up, down = w_up[0, local], w_down[0, local]
        pre = jnp.dot(rows_a, up, preferred_element_type=jnp.float32)
        active = jax.nn.silu(pre).astype(jnp.bfloat16)
        out = jnp.dot(active, down, preferred_element_type=jnp.float32)
        sum_a = sum_a + out * column(weight_a, local)
    for local in range(local_count):
        up, down = w_up[0, local], w_down[0, local]
        pre = jnp.dot(rows_b, up, preferred_element_type=jnp.float32)
        back = jnp.einsum("td,fd->tf", rows_g, down, preferred_element_type=jnp.float32)
        sig = jax.nn.sigmoid(pre)
        scores.append(jnp.sum(back * (pre * sig), axis=-1))
        inner = (back * (sig * (1.0 + pre * (1.0 - sig)))).astype(jnp.bfloat16)
        lifted = jnp.einsum("tf,df->td", inner, up, preferred_element_type=jnp.float32)
        sum_b = sum_b + lifted * column(weight_b, local)
    sum_ab = scatter_sums([sum_a.astype(jnp.bfloat16), sum_b.astype(jnp.bfloat16)], 2)
    mixed = sum_ab[0].astype(jnp.float32)
    layer_out = (hidden32_a + ROUTED_SCALE * mixed).astype(jnp.bfloat16)

    flat = jnp.stack(scores).reshape(-1)
    padded = jnp.pad(flat, (0, -flat.shape[0] % 2048)).reshape(-1, 128)
    score = gather_all([padded], 4)[0].reshape(n_expert, -1)[:, : flat.shape[0]]
    score = score.reshape(expert_count, -1).T
    score = jnp.where(aff_b > 0.0, score, 0.0)
    gate_grad = ROUTED_SCALE * score
    logit_grad = (
        aff_b
        * (1.0 - aff_b)
        * (gate_grad - jnp.sum(gate_grad * weight_b, axis=1, keepdims=True))
        / total_b
    )
    own_columns = lax.dynamic_slice_in_dim(logit_grad, me * local_count, local_count, axis=1)
    own_term = jnp.dot(
        own_columns.T, rows_b.astype(jnp.float32), precision=lax.Precision.HIGHEST
    )
    mirrored = own_term
    for bit in range(lax.axis_size("pipe").bit_length() - 1):
        mirrored = partner(mirrored, "pipe", bit)
    router_grad = own_term + mirrored

    dense = lax.dynamic_slice_in_dim(logit_grad, me * tok_count, tok_count, axis=0)
    lifted_sum = sum_ab[1].astype(jnp.float32)
    normed_grad = ROUTED_SCALE * lifted_sum + jnp.dot(
        dense, router_segment.astype(jnp.float32), precision=lax.Precision.HIGHEST
    )
    mean_term = jnp.mean(normed_grad * hidden32_b, axis=-1, keepdims=True)
    grad_in = (
        grad_out.astype(jnp.float32) + rinv_b * normed_grad - hidden32_b * rinv_b**3 * mean_term
    )
    return (layer_out[None], grad_in.astype(jnp.bfloat16)[None], router_grad[None])


def fused_kernel(dims, *refs):
    planes, tok, depth, width, dc, rc, n_up, ring, n_pipe = dims
    (hid_a, hid_b, g, routes_a, routes_b, router, wu, wd, out_a, out_b, rg_out) = refs[:11]
    (rows, tabs, wu_b, wd_b, bu, bd, act, pre, back, silu, inner) = refs[11:22]
    (o_buf, y_buf, t_buf, z_buf, f_buf, sc_col, sc_own, sc_all, rg_buf, rg_in) = refs[22:32]
    (router_t, rinv_b, lifted) = refs[32:35]
    (own_s, zs, zr, ys, yr, xs, xr, ms, mr, bus, bds) = refs[35:46]
    (rys, ryr, rzs, rzr, rfs, scs, scr, gs, gr) = refs[46:55]
    slots = 2 * planes
    experts = 2 * slots
    m_rows = slots * tok
    chunks = depth // dc
    half_d = depth // 2
    half_f = width // 2
    half_t = tok // 2
    up_rows = half_d // n_up
    tile = 256
    lanes = tabs.shape[-1]
    me, z, y, x, x_near, y_near = place()
    p = lax.axis_index("pipe")
    mirror = n_pipe - 1 - p
    part = (2 * p) // n_pipe
    slot_me = y * planes + z
    pair = z + 1 - 2 * (z % 2)
    opposite = (z + 2) % planes
    other = (pair + 2) % planes
    middle = (z + 1) // 2 == 1

    def copy(src, dst, send, recv, expert, pipe=p):
        return pltpu.make_async_remote_copy(
            src_ref=src,
            dst_ref=dst,
            send_sem=send,
            recv_sem=recv,
            device_id={"pipe": pipe, "expert": expert},
            device_id_type=MESH,
        )

    def chip(plane, row):
        return plane * PLANE + row * 2 + x

    def of_slot(s):
        return chip(s % planes, s // planes)

    barrier = pltpu.get_barrier_semaphore()

    def hello(pipe, expert):
        pl.semaphore_signal(
            barrier, inc=1, device_id={"pipe": pipe, "expert": expert}, device_id_type=MESH
        )

    for i in range(1, slots):
        hello(p, of_slot((slot_me + i) % slots))
    hello(p, x_near)
    hello(mirror, me)
    hello(mirror, x_near)

    own_g = pltpu.make_async_copy(g, rows.at[2, slot_me], own_s.at[0])
    own_g.start()

    def nn(lhs, rhs):
        return jnp.dot(lhs, rhs, preferred_element_type=jnp.float32)

    def nt(lhs, rhs):
        return lax.dot_general(
            lhs, rhs, (((1,), (1,)), ((), ())), preferred_element_type=jnp.float32
        )

    def normalize(k, src):
        step = 16

        def body(i, carry):
            r = pl.ds(pl.multiple_of(i * step, step), step)
            h = src[r, :].astype(jnp.float32)
            rinv = lax.rsqrt(jnp.mean(h * h, axis=-1, keepdims=True) + EPSILON)
            rows[k, slot_me, r, :] = (h * rinv).astype(rows.dtype)
            if k == 1:
                rinv_b[r, :] = jnp.broadcast_to(rinv, (step, lanes))
            return carry

        lax.fori_loop(0, tok // step, body, 0)

    normalize(0, hid_a)
    normalize(1, hid_b)
    for i in range(3):
        router_t[i * experts : (i + 1) * experts] = router[...]
    router_t[3 * experts :] = jnp.zeros((lanes - 3 * experts, depth), router_t.dtype)
    lane = lax.broadcasted_iota(jnp.int32, (tok, lanes), 1)
    expert_lane = lax.rem(lane, experts)

    def affinity(k, routes, section):
        logits = nt(rows[k, slot_me], router_t[...])
        named = routes[...]
        chosen = expert_lane == named[:, 0:1]
        for i in range(1, named.shape[1]):
            chosen = jnp.logical_or(chosen, expert_lane == named[:, i : i + 1])
        sig = jnp.where(chosen, jax.nn.sigmoid(logits), 0.0)
        here = jnp.where(lax.div(lane, experts) == section, sig, 0.0)
        return sig, here, jnp.sum(here, axis=-1, keepdims=True)

    _, here_a, total_a = affinity(0, routes_a, 0)
    sig_b, here_b, total_b = affinity(1, routes_b, 1)
    slope_b = jnp.where(lax.div(lane, experts) == 2, sig_b * (1.0 - sig_b), 0.0)
    tabs[slot_me] = here_a / total_a + here_b / total_b + slope_b / total_b

    pl.semaphore_wait(barrier, slots - 1 + 3)

    def up_region(which, i):
        return pl.ds(pl.multiple_of(which * half_d + i * up_rows, up_rows), up_rows)

    def up_x(i):
        r = up_region(part, i)
        return copy(wu.at[r], wu_b.at[r], xs.at[i], xr.at[i], x_near)

    def up_m(i, which):
        r = up_region(which, i)
        return copy(wu_b.at[r], wu_b.at[r], ms.at[i], mr.at[i], me, mirror)

    def down_rows(which):
        return pl.ds(pl.multiple_of(which * half_f, half_f), half_f)

    def columns(c):
        return pl.ds(pl.multiple_of(c * dc, dc), dc)

    def fine_columns(c):
        return pl.ds(pl.multiple_of(c * rc, rc), rc)

    def down_x(c):
        r = down_rows(part)
        src = wd.at[r, columns(c)]
        return copy(src, wd_b.at[c, r], xs.at[n_up + c], xr.at[n_up + c], x_near)

    def down_m(c, which):
        ref = wd_b.at[c, down_rows(which)]
        return copy(ref, ref, ms.at[n_up + c], mr.at[n_up + c], me, mirror)

    for i in range(n_up):
        up_x(i).start()
    for c in range(chunks):
        down_x(c).start()

    bufs = [tabs, rows.at[0], rows.at[1], rows.at[2]]

    def block(k, row, source):
        return bufs[k].at[row * planes + source]

    def mine(k):
        return g if k == 3 else bufs[k].at[slot_me]

    def z_send(k, target):
        dst = bufs[k].at[slot_me]
        return copy(mine(k), dst, zs.at[k, target], zr.at[k, z], chip(target, y))

    def z_take(k, source):
        ref = block(k, y, source)
        return copy(ref, ref, zs.at[k, source], zr.at[k, source], chip(source, y))

    def z_relay(k):
        ref = block(k, y, opposite)
        return copy(ref, ref, zs.at[k, z], zr.at[k, opposite], chip(pair, y))

    def late(ref):
        return ref.at[pl.ds(half_t, half_t)]

    def early(ref):
        return ref.at[pl.ds(0, half_t)]

    def cross(k, source):
        ref = late(block(k, 1 - y, source))
        return copy(ref, ref, zs.at[k, planes], zr.at[k, planes], chip(pair, y))

    def y_send(k):
        return copy(mine(k), bufs[k].at[slot_me], ys.at[k, z], yr.at[k, z], y_near)

    def y_copy(k, source, row):
        ref = block(k, row, source)
        return copy(ref, ref, ys.at[k, source], yr.at[k, source], y_near)

    def y_half(k, row):
        ref = early(block(k, row, pair))
        return copy(ref, ref, ys.at[k, pair], yr.at[k, pair], y_near)

    def spread(k):
        y_send(k).start()
        z_send(k, pair).start()

        @pl.when(middle)
        def _():
            z_send(k, other).start()

        z_send(k, opposite).start()

    def serve(k, i):
        if i == 0:
            z_take(k, pair).wait_recv()
            y_half(k, y).start()
            y_copy(k, z, 1 - y).wait_recv()
            cross(k, z).start()
        if i == 1:
            z_take(k, opposite).wait_recv()

            @pl.when(middle)
            def _():
                z_relay(k).start()

            y_copy(k, opposite, y).start()
        if i == 2:
            z_take(k, other).wait_recv()
            y_copy(k, other, y).start()

    def arrived(k):
        y_half(k, 1 - y).wait_recv()
        y_copy(k, opposite, 1 - y).wait_recv()
        y_copy(k, other, 1 - y).wait_recv()
        cross(k, pair).wait_recv()

    for k in range(4):
        spread(k)

    def chunk_of(k, c):
        return rows[k, :, :, columns(c)].reshape(m_rows, dc)

    def load_up(c):
        return pltpu.make_async_copy(wu.at[columns(c)], bu.at[c % 2], bus.at[c % 2])

    def load_fine(c):
        return pltpu.make_async_copy(wu.at[fine_columns(c)], bu.at[c % 2, :rc], bus.at[c % 2])

    def load_down(c):
        return pltpu.make_async_copy(wd.at[:, columns(c)], bd.at[c % 2], bds.at[c % 2])

    def next_chunk(load, c, count=chunks):
        load(c).wait()

        @pl.when(c + 1 < count)
        def _():
            load(c + 1).start()

    def block_rows(s):
        return pl.ds(pl.multiple_of(s * tok, tok), tok)

    def clear(dst):
        def body(s, carry):
            dst[block_rows(s), :] = jnp.zeros((tok, width), jnp.float32)
            return carry

        lax.fori_loop(0, slots, body, 0)

    def project(k, partner, dst):
        clear(dst)
        if not partner:
            load_up(0).start()

        def body(c, carry):
            if not partner:
                next_chunk(load_up, c)
            lhs = chunk_of(k, c)
            for n in range(width // tile):
                cols = pl.ds(n * tile, tile)
                rhs = wu_b[columns(c), cols] if partner else bu[c % 2, :, cols]
                dst[:, cols] += nn(lhs, rhs)
            return carry

        lax.fori_loop(0, chunks, body, 0)

    def pick(s, column):
        return jnp.sum(jnp.where(lane == column, tabs[s], 0.0), axis=-1, keepdims=True)

    expert_of = [me, x_near]

    def activate(which, src):
        def body(s, carry):
            v = src[block_rows(s), :]
            weight = pick(s, expert_of[which])
            act[which, block_rows(s), :] = (v * jax.nn.sigmoid(v) * weight).astype(act.dtype)
            return carry

        lax.fori_loop(0, slots, body, 0)

    def prepare_b(which):
        def body(s, carry):
            r = block_rows(s)
            v = pre[which, r, :]
            sig = jax.nn.sigmoid(v)
            silu[which, r, :] = (v * sig).astype(silu.dtype)
            weight = pick(s, experts + expert_of[which])
            pre[which, r, :] = sig * (1.0 + v * (1.0 - sig)) * weight
            return carry

        lax.fori_loop(0, slots, body, 0)

    def invert(which):
        def body(s, carry):
            r = block_rows(s)
            bk = back[which, r, :]
            score = jnp.sum(bk * silu[which, r, :].astype(jnp.float32), axis=-1, keepdims=True)
            inner[which, r, :] = (bk * pre[which, r, :]).astype(inner.dtype)
            at = x if which == 0 else 1 - x
            held = 0.0 if which == 0 else sc_col[s]
            sc_col[s] = jnp.where(lane == at, score, held)
            return carry

        lax.fori_loop(0, slots, body, 0)

    fine = depth // rc
    steps = 2 * fine

    def rs_y(q):
        src = o_buf.at[q % ring, pl.ds((1 - y) * planes, planes)]
        return copy(src, y_buf.at[q], rys.at[q], ryr.at[q], y_near)

    def rs_z(q, target, place_at):
        src = t_buf.at[q % ring, target]
        return copy(src, z_buf.at[q, place_at], rzs.at[q], rzr.at[q], chip(target, y))

    def rs_far(q):
        src = t_buf.at[q % ring, other]
        return copy(src, f_buf.at[q], rzs.at[q], rfs.at[q], chip(pair, y))

    def sent_z(q):
        src = t_buf.at[q % ring, pl.ds(0, planes - 1)]
        dst = z_buf.at[q, pl.ds(0, planes - 1)]
        copy(src, dst, rzs.at[q], rzr.at[q], chip(pair, y)).wait_send()

    def fold_y(q):
        rs_y(q).wait_recv()

        def clean():
            sent_z(q - ring)

        if isinstance(q, int):
            if q >= ring:
                clean()
        else:
            pl.when(q >= ring)(clean)
        for k in range(planes):
            first = o_buf[q % ring, y * planes + k].astype(jnp.float32)
            t_buf[q % ring, k] = (first + y_buf[q, k].astype(jnp.float32)).astype(t_buf.dtype)
        rs_z(q, pair, 0).start()

        @pl.when(middle)
        def _():
            rs_z(q, other, 2).start()

        @pl.when(jnp.logical_not(middle))
        def _():
            rs_far(q).start()
            rs_z(q, opposite, 1).start()

    def relay_z(q):
        @pl.when(middle)
        def _():
            rs_far(q).wait_recv()
            total = t_buf[q % ring, opposite].astype(jnp.float32) + f_buf[q].astype(jnp.float32)
            t_buf[q % ring, opposite] = total.astype(t_buf.dtype)
            rs_z(q, opposite, 1).start()

    def take_z(q, count):
        src = t_buf.at[q % ring, pl.ds(0, count)]
        dst = z_buf.at[q, pl.ds(0, count)]
        copy(src, dst, rzs.at[q], rzr.at[q], chip(pair, y)).wait_recv()
        total = t_buf[q % ring, z].astype(jnp.float32)
        for i in range(count):
            total = total + z_buf[q, i].astype(jnp.float32)
        return total

    def fold_z(q):
        def settle(total):
            def of_a():
                cols = fine_columns(q)
                mixed = hid_a[:, cols].astype(jnp.float32) + ROUTED_SCALE * total
                out_a[:, cols] = mixed.astype(out_a.dtype)

            def of_b():
                lifted[:, fine_columns(q - fine)] = total

            if isinstance(q, int):
                of_a() if q < fine else of_b()
            else:
                pl.when(q < fine)(of_a)
                pl.when(q >= fine)(of_b)

        @pl.when(middle)
        def _():
            settle(take_z(q, planes - 1))

        @pl.when(jnp.logical_not(middle))
        def _():
            settle(take_z(q, planes - 2))

    lags = ((2, fold_y), (4, relay_z), (6, fold_z))

    def behind(q):
        for lag, stage in lags:
            if isinstance(q, int):
                if lag <= q < steps + lag:
                    stage(q - lag)
            else:
                pl.when(q >= lag)(functools.partial(stage, q - lag))

    def store(q, value):
        def clean():
            rs_y(q - ring).wait_send()

        pl.when(q >= ring)(clean)
        o_buf[q % ring] = value.reshape(slots, tok, rc).astype(o_buf.dtype)
        rs_y(q).start()

    for k in range(3):
        for i in range(3):
            serve(k, i)
    own_g.wait()
    arrived(0)
    arrived(1)
    project(0, False, back.at[0])
    activate(0, back.at[0])
    serve(3, 0)
    for i in range(n_up):
        up_x(i).wait_recv()
        up_m(i, part).start()
    for i in range(n_up):
        up_m(i, 1 - part).wait_recv()
    project(0, True, back.at[1])
    activate(1, back.at[1])
    serve(3, 1)
    arrived(2)
    project(1, False, pre.at[0])
    prepare_b(0)
    serve(3, 2)
    project(1, True, pre.at[1])
    prepare_b(1)
    clear(back.at[0])
    clear(back.at[1])
    load_down(0).start()
    load_fine(0).start()
    down_x(0).wait_recv()
    down_m(0, part).start()
    arrived(3)

    def forward(c, carry):
        next_chunk(load_down, c)
        down_m(c, 1 - part).wait_recv()
        for n in range(dc // rc):
            cols = pl.ds(n * rc, rc)
            value = nn(act[0], bd[c % 2, :, cols]) + nn(act[1], wd_b[c, :, cols])
            store(c * (dc // rc) + n, value)
        lhs = chunk_of(2, c)
        for n in range(width // tile):
            cols = pl.ds(n * tile, tile)
            back[1, :, cols] += nt(lhs, wd_b[c, cols, :])

        @pl.when(c + 1 < chunks)
        def _():
            down_x(c + 1).wait_recv()
            down_m(c + 1, part).start()

        for n in range(dc // rc):
            behind(c * (dc // rc) + n)
        return carry

    def own_back(c, carry):
        next_chunk(load_down, c)
        lhs = chunk_of(2, c)
        for n in range(width // tile):
            cols = pl.ds(n * tile, tile)
            back[0, :, cols] += nt(lhs, bd[c % 2, cols, :])
        return carry

    first = min(4, chunks - 1)
    lax.fori_loop(0, first, forward, 0)
    load_down(first).wait()
    load_down(0).start()
    lax.fori_loop(0, chunks, own_back, 0)
    invert(0)
    load_down(first).start()
    lax.fori_loop(first, chunks, forward, 0)
    invert(1)

    def score_copy(i, slot):
        target = of_slot((slot_me + i) % slots)
        return copy(sc_own, sc_all.at[slot], scs.at[i - 1], scr.at[i - 1], target)

    def backward(c, carry):
        next_chunk(load_fine, c, fine)
        q = fine + c
        value = nt(inner[0], bu[c % 2, :rc, :]) + nt(inner[1], wu_b[fine_columns(c), :])
        store(q, value)
        behind(q)

        @pl.when(c == 1)
        def _():
            sc_own[...] = sc_col[...].reshape(m_rows, lanes).T[:8]
            for i in range(1, slots):
                score_copy(i, slot_me).start()

        return carry

    lax.fori_loop(0, fine, backward, 0)

    sc_all[slot_me] = sc_own[...]
    for i in range(1, slots):
        score_copy(i, (slot_me - i + slots) % slots).wait_recv()
    table = tabs[...].reshape(m_rows, lanes).T
    lines = []
    for e in range(experts):
        plane, row, odd = e // PLANE, (e // 2) % 2, e % 2
        lines.append(sc_all[row * planes + plane, odd : odd + 1, :])
    score = jnp.concatenate(lines, axis=0)
    gate = ROUTED_SCALE * score
    mean = jnp.sum(gate * table[experts : 2 * experts], axis=0, keepdims=True)
    logit = table[2 * experts : 3 * experts] * (gate - mean)
    order = lax.broadcasted_iota(jnp.int32, (experts, m_rows), 0)
    one = jnp.sum(jnp.where(order == me, logit, 0.0), axis=0, keepdims=True)
    two = jnp.sum(jnp.where(order == x_near, logit, 0.0), axis=0, keepdims=True)
    both = jnp.concatenate([one, two, jnp.zeros((6, m_rows), jnp.float32)], axis=0)

    def thirds(v):
        high = v.astype(jnp.bfloat16)
        rest = v - high.astype(jnp.float32)
        medium = rest.astype(jnp.bfloat16)
        return (high, medium, (rest - medium.astype(jnp.float32)).astype(jnp.bfloat16))

    pieces = thirds(both)
    for c in range(chunks):
        cols = pl.ds(c * dc, dc)
        rhs = rows[1, :, :, cols].reshape(m_rows, dc)
        rg_buf[:, cols] = nn(pieces[0], rhs) + nn(pieces[1], rhs) + nn(pieces[2], rhs)

    def grad_copy(i):
        expert = me if i == 0 else x_near
        pipe = p if i == 1 else mirror
        return copy(rg_buf, rg_in.at[i], gs.at[i], gr.at[i], expert, pipe)

    for i in range(3):
        grad_copy(i).start()
    padded = jnp.concatenate([logit, jnp.zeros((lanes - experts, m_rows), jnp.float32)], axis=0)
    sc_col[...] = padded.T.reshape(slots, tok, lanes)
    for q in range(steps, steps + 3):
        behind(q)
    dense = thirds(sc_col[slot_me])
    for q in range(steps + 3, steps + lags[-1][0]):
        behind(q)

    inv = rinv_b[:, 0:1]
    dots = jnp.zeros((tok, 1), jnp.float32)
    for c in range(chunks):
        cols = pl.ds(c * dc, dc)
        rhs = router_t[:, cols]
        extra = nn(dense[0], rhs) + nn(dense[1], rhs) + nn(dense[2], rhs)
        v = ROUTED_SCALE * lifted[:, cols] + extra
        lifted[:, cols] = v
        dots = dots + jnp.sum(v * hid_b[:, cols].astype(jnp.float32), axis=-1, keepdims=True)
    slope = inv * inv * inv * (dots / depth)
    for c in range(chunks):
        cols = pl.ds(c * dc, dc)
        grad = g[:, cols].astype(jnp.float32) + inv * lifted[:, cols]
        grad = grad - hid_b[:, cols].astype(jnp.float32) * slope
        out_b[:, cols] = grad.astype(out_b.dtype)
    for i in range(3):
        grad_copy(i).wait_recv()
    rg_out[...] = rg_buf[0:1, :] + rg_in[0, 0:1, :] + rg_in[1, 1:2, :] + rg_in[2, 1:2, :]

    for k in range(4):
        z_send(k, pair).wait_send()
        z_send(k, opposite).wait_send()

        @pl.when(middle)
        def _():
            z_send(k, other).wait_send()
            z_relay(k).wait_send()

        cross(k, z).wait_send()
        y_send(k).wait_send()
        y_half(k, y).wait_send()
        for source in (opposite, other):
            y_copy(k, source, y).wait_send()
    for i in range(n_up):
        up_x(i).wait_send()
        up_m(i, part).wait_send()

    def drain(c, carry):
        down_x(c).wait_send()
        down_m(c, part).wait_send()
        return carry

    lax.fori_loop(0, chunks, drain, 0)

    def drain_rs(q, carry):
        rs_y(q).wait_send()
        sent_z(q)
        return carry

    lax.fori_loop(steps - ring, steps, drain_rs, 0)
    for i in range(1, slots):
        score_copy(i, slot_me).wait_send()
    for i in range(3):
        grad_copy(i).wait_send()


N_UP = 4
RING = 8


def fused_plan(n, tok, depth, width):
    planes = n // PLANE
    slots = 2 * planes
    m_rows = slots * tok
    dc = 512 if depth % 512 == 0 else 256
    rc = 256
    chunks = depth // dc
    steps = 2 * (depth // rc)
    bf, f32 = jnp.bfloat16, jnp.float32
    buffers = [
        ((3, slots, tok, depth), bf),
        ((slots, tok, 128), f32),
        ((depth, width), bf),
        ((chunks, width, dc), bf),
        ((2, dc, width), bf),
        ((2, width, dc), bf),
        ((2, m_rows, width), bf),
        ((2, m_rows, width), f32),
        ((2, m_rows, width), f32),
        ((2, m_rows, width), bf),
        ((2, m_rows, width), bf),
        ((RING, slots, tok, rc), bf),
        ((steps, planes, tok, rc), bf),
        ((RING, planes, tok, rc), bf),
        ((steps, planes - 1, tok, rc), bf),
        ((steps, tok, rc), bf),
        ((slots, tok, 128), f32),
        ((8, m_rows), f32),
        ((slots, 8, m_rows), f32),
        ((8, depth), f32),
        ((3, 8, depth), f32),
        ((128, depth), bf),
        ((tok, 128), f32),
        ((tok, depth), f32),
    ]
    sems = (
        [(1,)]
        + [(4, planes + 1)] * 2
        + [(4, planes)] * 2
        + [(N_UP + chunks,)] * 4
        + [(2,)] * 2
        + [(steps,)] * 5
        + [(slots - 1,)] * 2
        + [(3,)] * 2
    )
    total = sum(math.prod(shape) * jnp.dtype(kind).itemsize for shape, kind in buffers)
    fits = total + 5 * tok * depth * 2 < 64_500_000 and 3 * n <= 128 and planes == 4
    return fits, (planes, tok, depth, width, dc, rc, N_UP, RING), buffers, sems


def fused(plan, *args):
    _, dims, buffers, sems = plan
    tok, depth = dims[1:3]
    vmem = pl.BlockSpec(memory_space=pltpu.VMEM)
    hbm = pl.BlockSpec(memory_space=pl.ANY)
    return pl.pallas_call(
        functools.partial(fused_kernel, dims + (lax.axis_size("pipe"),)),
        out_shape=[
            jax.ShapeDtypeStruct((tok, depth), jnp.bfloat16),
            jax.ShapeDtypeStruct((tok, depth), jnp.bfloat16),
            jax.ShapeDtypeStruct((1, depth), jnp.float32),
        ],
        in_specs=[vmem] * 6 + [hbm] * 2,
        out_specs=[vmem] * 3,
        scratch_shapes=[pltpu.VMEM(shape, kind) for shape, kind in buffers]
        + [DMA(shape) for shape in sems],
        compiler_params=pltpu.CompilerParams(
            collective_id=7, has_side_effects=True, vmem_limit_bytes=67_000_000
        ),
    )(*args)


def on_device_fused(
    plan, hidden_a, routes_a, hidden_b, routes_b, grad_out_b, router, w_up, w_down
):
    outs = fused(
        plan,
        hidden_a[0],
        hidden_b[0],
        grad_out_b[0],
        routes_a[0],
        routes_b[0],
        router[0],
        w_up[0, 0],
        w_down[0, 0],
    )
    return tuple(o[None] for o in outs)


def solution(mesh):
    placed = (
        P("pipe", "expert", None),
        P("pipe", "expert", None),
        P("pipe", "expert", None),
        P("pipe", "expert", None),
        P("pipe", "expert", None),
        P("pipe", None, None),
        P("pipe", "expert", None, None),
        P("pipe", "expert", None, None),
    )

    def body(*args):
        w_up = args[6]
        plan = fused_plan(lax.axis_size("expert"), args[0].shape[1], w_up.shape[2], w_up.shape[3])
        if w_up.shape[1] == 1 and plan[0]:
            return on_device_fused(plan, *args)
        return on_device(*args)

    return jax.shard_map(
        body,
        mesh=mesh,
        in_specs=placed,
        out_specs=(P("pipe", "expert", None), P("pipe", "expert", None), P("pipe", "expert", None)),
        check_vma=False,
    )
```

```python
import functools
import math

import jax
import jax.numpy as jnp
from jax import lax
from jax.experimental import pallas as pl
from jax.experimental.pallas import tpu as pltpu
from jax.sharding import PartitionSpec as P

ROUTED_SCALE = 2.5
EPSILON = 1e-06


def partner(block, axis, bit):
    count = lax.axis_size(axis)
    route = []
    for low in range(count):
        high = low | 1 << bit
        if high != low and high < count:
            route += [(low, high), (high, low)]
    return lax.ppermute(block, axis, route)


MESH = pl.DeviceIdType.MESH
DMA = pltpu.SemaphoreType.DMA
PLANE = 4


def remote(src, dst, send_sem, recv_sem, target):
    return pltpu.make_async_remote_copy(
        src_ref=src,
        dst_ref=dst,
        send_sem=send_sem,
        recv_sem=recv_sem,
        device_id={"expert": target},
        device_id_type=MESH,
    )


def place():
    me = lax.axis_index("expert")
    z, y, x = me // PLANE, (me // 2) % 2, me % 2
    return (me, z, y, x, me + 1 - 2 * x, me + 2 - 4 * y)


def greet(planes):
    me, z, y, x, x_near, y_near = place()
    barrier = pltpu.get_barrier_semaphore()
    pl.semaphore_signal(barrier, inc=1, device_id={"expert": x_near}, device_id_type=MESH)
    pl.semaphore_signal(barrier, inc=1, device_id={"expert": y_near}, device_id_type=MESH)

    @pl.when(z < planes - 1)
    def _():
        pl.semaphore_signal(barrier, inc=1, device_id={"expert": me + PLANE}, device_id_type=MESH)

    @pl.when(z > 0)
    def _():
        pl.semaphore_signal(barrier, inc=1, device_id={"expert": me - PLANE}, device_id_type=MESH)

    ends = jnp.where(z == 0, 1, 0) + jnp.where(z == planes - 1, 1, 0)
    pl.semaphore_wait(barrier, 4 - ends)


def gather_kernel(count, planes, *refs):
    ins, outs = refs[:count], refs[count : 2 * count]
    own_sem, up_s, down_s, z_r, x_s, x_r, y_s, y_r, d_s, d_r = refs[2 * count :]
    me, z, y, x, x_near, y_near = place()

    def up(k, p, src):
        return remote(src, outs[k].at[p * PLANE + y * 2 + x], up_s.at[k, p], z_r.at[k, p], me + PLANE)

    def down(k, p, src):
        return remote(src, outs[k].at[p * PLANE + y * 2 + x], down_s.at[k, p], z_r.at[k, p], me - PLANE)

    def to_x(k, p, src):
        return remote(src, outs[k].at[p * PLANE + y * 2 + x], x_s.at[k, p], x_r.at[k, p], x_near)

    def to_y(k, p, src):
        return remote(src, outs[k].at[p * PLANE + y * 2 + x], y_s.at[k, p], y_r.at[k, p], y_near)

    def half(k, p, way):
        if way == 0:
            ref = outs[k].at[p * PLANE + y * 2 + 1 - x, 0]
            return remote(ref, ref, d_s.at[k, p, 0], d_r.at[k, p, 0], y_near)
        ref = outs[k].at[p * PLANE + (1 - y) * 2 + x, 1]
        return remote(ref, ref, d_s.at[k, p, 1], d_r.at[k, p, 1], x_near)

    def each(d, act):
        if d == 0:
            act(z, 0)
            return

        @pl.when(z >= d)
        def _():
            act(z - d, 1)

        @pl.when(z + d < planes)
        def _():
            act(z + d, -1)

    def spread(k, p, way, wait):
        src = ins[k] if way == 0 else outs[k].at[p * PLANE + y * 2 + x]

        def do(copy):
            copy.wait_send() if wait else copy.start()

        if way != 0 and not wait:
            up(k, p, src).wait_recv()
        if way >= 0:

            @pl.when(z < planes - 1)
            def _():
                do(up(k, p, src))

        if way <= 0:

            @pl.when(z > 0)
            def _():
                do(down(k, p, src))

        do(to_x(k, p, src))
        do(to_y(k, p, src))

    def relay(k, p, way):
        to_x(k, p, ins[k]).wait_recv()
        half(k, p, 0).start()
        to_y(k, p, ins[k]).wait_recv()
        half(k, p, 1).start()

    def finish(k, p, way):
        for route in range(2):
            half(k, p, route).wait()
        spread(k, p, way, True)

    greet(planes)
    for k in range(count):
        pltpu.make_async_copy(ins[k], outs[k].at[me], own_sem.at[k]).start()
        each(0, lambda p, way: spread(k, p, way, False))
    for k in range(count):
        for d in range(1, planes):
            each(d, lambda p, way: spread(k, p, way, False))
            each(d - 1, lambda p, way: relay(k, p, way))
        each(planes - 1, lambda p, way: relay(k, p, way))
    for k in range(count):
        for d in range(planes):
            each(d, lambda p, way: finish(k, p, way))
        pltpu.make_async_copy(ins[k], outs[k].at[me], own_sem.at[k]).wait()


def gather_all(blocks, collective_id):
    n = lax.axis_size("expert")
    planes = n // PLANE
    count = len(blocks)
    halved = [b.reshape(2, b.shape[0] // 2, b.shape[1]) for b in blocks]
    outs = pl.pallas_call(
        functools.partial(gather_kernel, count, planes),
        out_shape=[jax.ShapeDtypeStruct((n,) + b.shape, b.dtype) for b in halved],
        in_specs=[pl.BlockSpec(memory_space=pltpu.VMEM)] * count,
        out_specs=[pl.BlockSpec(memory_space=pl.ANY)] * count,
        scratch_shapes=[DMA((count,))] + [DMA((count, planes))] * 7 + [DMA((count, planes, 2))] * 2,
        compiler_params=pltpu.CompilerParams(collective_id=collective_id, has_side_effects=True),
    )(*halved)
    return [o.reshape(n * b.shape[0], b.shape[1]) for o, b in zip(outs, blocks)]


def scatter_stages(planes, part, out, a_r, c_r, b_x, b_y, total, z_r, *sems):
    ax_s, ax_r, ay_s, ay_r, cx_s, cx_r, cy_s, cy_r, z_s, up_r, down_r = sems
    me, z, y, x, x_near, y_near = place()
    rows, cols = part.shape[2:]
    step = 16

    def slot(p, yy, xx):
        return p * PLANE + yy * 2 + xx

    def add(dst, *srcs):
        def body(i, carry):
            r = pl.ds(pl.multiple_of(i * step, step), step)
            acc = srcs[0][r, :].astype(jnp.float32)
            for s in srcs[1:]:
                acc = acc + s[r, :].astype(jnp.float32)
            dst[r, :] = acc.astype(dst.dtype)
            return carry

        lax.fori_loop(0, rows // step, body, 0)

    def diagonal(p):
        src = slot(p, 1 - y, 1 - x)
        return (
            remote(part.at[src, 0], a_r.at[p, 0], ay_s.at[p], ay_r.at[p], y_near),
            remote(part.at[src, 1], a_r.at[p, 1], ax_s.at[p], ax_r.at[p], x_near),
        )

    def beside(p):
        return (
            remote(b_x.at[p, 0], c_r.at[p, 0, 0], cx_s.at[p, 0], cx_r.at[p, 0], x_near),
            remote(part.at[slot(p, y, 1 - x), 1], c_r.at[p, 0, 1], cx_s.at[p, 1], cx_r.at[p, 1], x_near),
            remote(b_y.at[p, 0], c_r.at[p, 1, 1], cy_s.at[p, 0], cy_r.at[p, 0], y_near),
            remote(part.at[slot(p, 1 - y, x), 0], c_r.at[p, 1, 0], cy_s.at[p, 1], cy_r.at[p, 1], y_near),
        )

    def rise(p):
        return remote(total.at[p], z_r.at[0, p], z_s.at[p], up_r.at[p], me + PLANE)

    def sink(p):
        return remote(total.at[p], z_r.at[1, p], z_s.at[p], down_r.at[p], me - PLANE)

    def first(p, way):
        for copy in diagonal(p):
            copy.start()
        beside(p)[1].start()
        beside(p)[3].start()

    def second(p, way):
        to_y, to_x = diagonal(p)
        to_y.wait_recv()
        add(b_x.at[p, 0], part.at[slot(p, y, 1 - x), 0], a_r.at[p, 0])
        beside(p)[0].start()
        to_x.wait_recv()
        add(b_y.at[p, 0], part.at[slot(p, 1 - y, x), 1], a_r.at[p, 1])
        beside(p)[2].start()

    def third(p, way):
        for copy in beside(p):
            copy.wait_recv()
        for h in range(2):
            add(total.at[p, h], part.at[slot(p, y, x), h], c_r.at[p, 0, h], c_r.at[p, 1, h])

        def take(copy, level):
            copy.wait_recv()
            for h in range(2):
                add(total.at[p, h], total.at[p, h], z_r.at[level, p, h])

        if way >= 0:

            @pl.when(z > 0)
            def _():
                take(rise(p), 0)

        if way <= 0:

            @pl.when(z < planes - 1)
            def _():
                take(sink(p), 1)

        if way > 0:
            rise(p).start()
        if way < 0:
            sink(p).start()
        if way == 0:
            out[...] = total[p]

    def finish(p, way):
        for copy in diagonal(p) + beside(p):
            copy.wait_send()
        if way != 0:
            rise(p).wait_send()

    return (first, second, third, finish)


def scatter_kernel(planes, count, *refs):
    parts, outs, rest = refs[:count], refs[count : 2 * count], refs[2 * count :]
    per = len(rest) // count
    z = place()[1]
    stages = [
        scatter_stages(planes, parts[k], outs[k], *rest[k * per : (k + 1) * per])
        for k in range(count)
    ]

    def each(d, act):
        if d == 0:
            act(z, 0)
            return

        @pl.when(z >= d)
        def _():
            act(z - d, -1)

        @pl.when(z + d < planes)
        def _():
            act(z + d, 1)

    greet(planes)
    order = list(range(planes - 1, -1, -1))
    for k in range(count):
        for d in order:
            each(d, stages[k][0])
    for i, d in enumerate(order):
        for k in range(count):
            each(d, stages[k][1])
        if i > 0:
            for k in range(count):
                each(order[i - 1], stages[k][2])
    for k in range(count):
        each(0, stages[k][2])
    for k in range(count):
        for d in order:
            each(d, stages[k][3])


def scatter_sums(parts, collective_id):
    n = lax.axis_size("expert")
    planes = n // PLANE
    tokens, cols = parts[0].shape
    rows = tokens // n // 2
    half = (rows, cols)
    kind = parts[0].dtype
    count = len(parts)
    if count > 1 and count * 3 * parts[0].size * kind.itemsize > 56 << 20:
        return [scatter_sums([part], collective_id + k)[0] for k, part in enumerate(parts)]
    outs = pl.pallas_call(
        functools.partial(scatter_kernel, planes, count),
        out_shape=[jax.ShapeDtypeStruct((2,) + half, kind)] * count,
        in_specs=[pl.BlockSpec(memory_space=pltpu.VMEM)] * count,
        out_specs=[pl.BlockSpec(memory_space=pltpu.VMEM)] * count,
        scratch_shapes=(
            [
                pltpu.VMEM((planes, 2) + half, kind),
                pltpu.VMEM((planes, 2, 2) + half, kind),
                pltpu.VMEM((planes, 1) + half, kind),
                pltpu.VMEM((planes, 1) + half, kind),
                pltpu.VMEM((planes, 2) + half, kind),
                pltpu.VMEM((2, planes, 2) + half, kind),
            ]
            + [DMA((planes,))] * 4
            + [DMA((planes, 2))] * 4
            + [DMA((planes,))] * 3
        )
        * count,
        compiler_params=pltpu.CompilerParams(
            collective_id=collective_id, has_side_effects=True, vmem_limit_bytes=60 << 20
        ),
    )(*[part.reshape((n, 2) + half) for part in parts])
    return [out.reshape(2 * rows, cols) for out in outs]


def prepare(hidden, routes, router_segment):
    expert_count = router_segment.shape[0]
    hidden32 = hidden.astype(jnp.float32)
    rinv = lax.rsqrt(jnp.mean(hidden32 * hidden32, axis=-1, keepdims=True) + EPSILON)
    normed = (hidden32 * rinv).astype(jnp.bfloat16)
    logits = jnp.einsum("td,ed->te", normed, router_segment, preferred_element_type=jnp.float32)
    chosen = jnp.any(
        routes[:, :, None] == jnp.arange(expert_count, dtype=jnp.int32)[None, None, :], axis=1
    )
    affinity = jnp.where(chosen, jax.nn.sigmoid(logits), 0.0)
    return (hidden32, rinv, normed, affinity)


def on_device(hidden_a, routes_a, hidden_b, routes_b, grad_out_b, router, w_up, w_down):
    n_expert = lax.axis_size("expert")
    me = lax.axis_index("expert")
    tok_count = hidden_a.shape[1]
    router_segment = router[0]
    expert_count = router_segment.shape[0]
    local_count = w_up.shape[1]
    hidden32_a, rinv_a, normed_a, affinity_a = prepare(hidden_a[0], routes_a[0], router_segment)
    hidden32_b, rinv_b, normed_b, affinity_b = prepare(hidden_b[0], routes_b[0], router_segment)
    grad_out = grad_out_b[0]
    affinity_ab = jnp.concatenate([affinity_a, affinity_b], axis=1)
    lanes = -(-2 * expert_count // 128) * 128
    affinity_ab = jnp.pad(affinity_ab, ((0, 0), (0, lanes - 2 * expert_count)))
    rows_a, rows_b, rows_g, affinities = gather_all([normed_a, normed_b, grad_out, affinity_ab], 1)
    aff_a, aff_b = affinities[:, :expert_count], affinities[:, expert_count : 2 * expert_count]
    total_b = jnp.sum(aff_b, axis=1, keepdims=True)
    weight_a = aff_a / jnp.sum(aff_a, axis=1, keepdims=True)
    weight_b = aff_b / total_b

    def column(table, local):
        return lax.dynamic_slice_in_dim(table, me * local_count + local, 1, axis=1)

    sum_a = 0.0
    sum_b = 0.0
    scores = []
    for local in range(local_count):
        up, down = w_up[0, local], w_down[0, local]
        pre = jnp.dot(rows_a, up, preferred_element_type=jnp.float32)
        active = jax.nn.silu(pre).astype(jnp.bfloat16)
        out = jnp.dot(active, down, preferred_element_type=jnp.float32)
        sum_a = sum_a + out * column(weight_a, local)
    for local in range(local_count):
        up, down = w_up[0, local], w_down[0, local]
        pre = jnp.dot(rows_b, up, preferred_element_type=jnp.float32)
        back = jnp.einsum("td,fd->tf", rows_g, down, preferred_element_type=jnp.float32)
        sig = jax.nn.sigmoid(pre)
        scores.append(jnp.sum(back * (pre * sig), axis=-1))
        inner = (back * (sig * (1.0 + pre * (1.0 - sig)))).astype(jnp.bfloat16)
        lifted = jnp.einsum("tf,df->td", inner, up, preferred_element_type=jnp.float32)
        sum_b = sum_b + lifted * column(weight_b, local)
    sum_ab = scatter_sums([sum_a.astype(jnp.bfloat16), sum_b.astype(jnp.bfloat16)], 2)
    mixed = sum_ab[0].astype(jnp.float32)
    layer_out = (hidden32_a + ROUTED_SCALE * mixed).astype(jnp.bfloat16)

    flat = jnp.stack(scores).reshape(-1)
    padded = jnp.pad(flat, (0, -flat.shape[0] % 2048)).reshape(-1, 128)
    score = gather_all([padded], 4)[0].reshape(n_expert, -1)[:, : flat.shape[0]]
    score = score.reshape(expert_count, -1).T
    score = jnp.where(aff_b > 0.0, score, 0.0)
    gate_grad = ROUTED_SCALE * score
    logit_grad = (
        aff_b
        * (1.0 - aff_b)
        * (gate_grad - jnp.sum(gate_grad * weight_b, axis=1, keepdims=True))
        / total_b
    )
    own_columns = lax.dynamic_slice_in_dim(logit_grad, me * local_count, local_count, axis=1)
    own_term = jnp.dot(
        own_columns.T, rows_b.astype(jnp.float32), precision=lax.Precision.HIGHEST
    )
    mirrored = own_term
    for bit in range(lax.axis_size("pipe").bit_length() - 1):
        mirrored = partner(mirrored, "pipe", bit)
    router_grad = own_term + mirrored

    dense = lax.dynamic_slice_in_dim(logit_grad, me * tok_count, tok_count, axis=0)
    lifted_sum = sum_ab[1].astype(jnp.float32)
    normed_grad = ROUTED_SCALE * lifted_sum + jnp.dot(
        dense, router_segment.astype(jnp.float32), precision=lax.Precision.HIGHEST
    )
    mean_term = jnp.mean(normed_grad * hidden32_b, axis=-1, keepdims=True)
    grad_in = (
        grad_out.astype(jnp.float32) + rinv_b * normed_grad - hidden32_b * rinv_b**3 * mean_term
    )
    return (layer_out[None], grad_in.astype(jnp.bfloat16)[None], router_grad[None])


def fused_kernel(dims, *refs):
    planes, tok, depth, width, dc, rc, n_up, ring, n_pipe = dims
    (hid_a, hid_b, g, routes_a, routes_b, router, wu, wd, out_a, out_b, rg_out) = refs[:11]
    (rows, tabs, wu_b, wd_b, bu, bd, act, pre, back, silu, inner) = refs[11:22]
    (o_buf, y_buf, t_buf, z_buf, f_buf, sc_col, sc_own, sc_all, rg_buf, rg_in) = refs[22:32]
    (router_t, rinv_b, lifted) = refs[32:35]
    (own_s, zs, zr, ys, yr, xs, xr, ms, mr, bus, bds) = refs[35:46]
    (rys, ryr, rzs, rzr, rfs, scs, scr, gs, gr) = refs[46:55]
    slots = 2 * planes
    experts = 2 * slots
    m_rows = slots * tok
    chunks = depth // dc
    half_d = depth // 2
    half_f = width // 2
    half_t = tok // 2
    up_rows = half_d // n_up
    tile = 256
    lanes = tabs.shape[-1]
    me, z, y, x, x_near, y_near = place()
    p = lax.axis_index("pipe")
    mirror = n_pipe - 1 - p
    part = (2 * p) // n_pipe
    slot_me = y * planes + z
    pair = z + 1 - 2 * (z % 2)
    opposite = (z + 2) % planes
    other = (pair + 2) % planes
    middle = (z + 1) // 2 == 1

    def copy(src, dst, send, recv, expert, pipe=p):
        return pltpu.make_async_remote_copy(
            src_ref=src,
            dst_ref=dst,
            send_sem=send,
            recv_sem=recv,
            device_id={"pipe": pipe, "expert": expert},
            device_id_type=MESH,
        )

    def chip(plane, row):
        return plane * PLANE + row * 2 + x

    def of_slot(s):
        return chip(s % planes, s // planes)

    barrier = pltpu.get_barrier_semaphore()

    def hello(pipe, expert):
        pl.semaphore_signal(
            barrier, inc=1, device_id={"pipe": pipe, "expert": expert}, device_id_type=MESH
        )

    for i in range(1, slots):
        hello(p, of_slot((slot_me + i) % slots))
    hello(p, x_near)
    hello(mirror, me)
    hello(mirror, x_near)

    own_g = pltpu.make_async_copy(g, rows.at[2, slot_me], own_s.at[0])
    own_g.start()

    def nn(lhs, rhs):
        return jnp.dot(lhs, rhs, preferred_element_type=jnp.float32)

    def nt(lhs, rhs):
        return lax.dot_general(
            lhs, rhs, (((1,), (1,)), ((), ())), preferred_element_type=jnp.float32
        )

    def normalize(k, src):
        step = 16

        def body(i, carry):
            r = pl.ds(pl.multiple_of(i * step, step), step)
            h = src[r, :].astype(jnp.float32)
            rinv = lax.rsqrt(jnp.mean(h * h, axis=-1, keepdims=True) + EPSILON)
            rows[k, slot_me, r, :] = (h * rinv).astype(rows.dtype)
            if k == 1:
                rinv_b[r, :] = jnp.broadcast_to(rinv, (step, lanes))
            return carry

        lax.fori_loop(0, tok // step, body, 0)

    normalize(0, hid_a)
    normalize(1, hid_b)
    for i in range(3):
        router_t[i * experts : (i + 1) * experts] = router[...]
    router_t[3 * experts :] = jnp.zeros((lanes - 3 * experts, depth), router_t.dtype)
    lane = lax.broadcasted_iota(jnp.int32, (tok, lanes), 1)
    expert_lane = lax.rem(lane, experts)

    def affinity(k, routes, section):
        logits = nt(rows[k, slot_me], router_t[...])
        named = routes[...].T
        chosen = expert_lane == named[:, 0:1]
        for i in range(1, named.shape[1]):
            chosen = jnp.logical_or(chosen, expert_lane == named[:, i : i + 1])
        sig = jnp.where(chosen, jax.nn.sigmoid(logits), 0.0)
        here = jnp.where(lax.div(lane, experts) == section, sig, 0.0)
        return sig, here, jnp.sum(here, axis=-1, keepdims=True)

    _, here_a, total_a = affinity(0, routes_a, 0)
    sig_b, here_b, total_b = affinity(1, routes_b, 1)
    slope_b = jnp.where(lax.div(lane, experts) == 2, sig_b * (1.0 - sig_b), 0.0)
    tabs[slot_me] = here_a / total_a + here_b / total_b + slope_b / total_b

    pl.semaphore_wait(barrier, slots - 1 + 3)

    def up_region(which, i):
        return pl.ds(pl.multiple_of(which * half_d + i * up_rows, up_rows), up_rows)

    def up_x(i):
        r = up_region(part, i)
        return copy(wu.at[r], wu_b.at[r], xs.at[i], xr.at[i], x_near)

    def up_m(i, which):
        r = up_region(which, i)
        return copy(wu_b.at[r], wu_b.at[r], ms.at[i], mr.at[i], me, mirror)

    def down_rows(which):
        return pl.ds(pl.multiple_of(which * half_f, half_f), half_f)

    def columns(c):
        return pl.ds(pl.multiple_of(c * dc, dc), dc)

    def fine_columns(c):
        return pl.ds(pl.multiple_of(c * rc, rc), rc)

    def down_x(c):
        r = down_rows(part)
        src = wd.at[r, columns(c)]
        return copy(src, wd_b.at[c, r], xs.at[n_up + c], xr.at[n_up + c], x_near)

    def down_m(c, which):
        ref = wd_b.at[c, down_rows(which)]
        return copy(ref, ref, ms.at[n_up + c], mr.at[n_up + c], me, mirror)

    for i in range(n_up):
        up_x(i).start()
    for c in range(chunks):
        down_x(c).start()

    bufs = [tabs, rows.at[0], rows.at[1], rows.at[2]]

    def block(k, row, source):
        return bufs[k].at[row * planes + source]

    def mine(k):
        return g if k == 3 else bufs[k].at[slot_me]

    def z_send(k, target):
        dst = bufs[k].at[slot_me]
        return copy(mine(k), dst, zs.at[k, target], zr.at[k, z], chip(target, y))

    def z_take(k, source):
        ref = block(k, y, source)
        return copy(ref, ref, zs.at[k, source], zr.at[k, source], chip(source, y))

    def z_relay(k):
        ref = block(k, y, opposite)
        return copy(ref, ref, zs.at[k, z], zr.at[k, opposite], chip(pair, y))

    def late(ref):
        return ref.at[pl.ds(half_t, half_t)]

    def early(ref):
        return ref.at[pl.ds(0, half_t)]

    def cross(k, source):
        ref = late(block(k, 1 - y, source))
        return copy(ref, ref, zs.at[k, planes], zr.at[k, planes], chip(pair, y))

    def y_send(k):
        return copy(mine(k), bufs[k].at[slot_me], ys.at[k, z], yr.at[k, z], y_near)

    def y_copy(k, source, row):
        ref = block(k, row, source)
        return copy(ref, ref, ys.at[k, source], yr.at[k, source], y_near)

    def y_half(k, row):
        ref = early(block(k, row, pair))
        return copy(ref, ref, ys.at[k, pair], yr.at[k, pair], y_near)

    def spread(k):
        y_send(k).start()

        @pl.when(middle)
        def _():
            if k < 2:
                z_send(k, pair).start()
            z_send(k, other).start()

        @pl.when(jnp.logical_not(middle))
        def _():
            z_send(k, pair).start()
            if k == 0:
                z_send(k, other).start()

        z_send(k, opposite).start()

    def serve(k, i):
        if i == 0:
            z_take(k, pair).wait_recv()
            if k < 2:
                y_copy(k, pair, y).start()
            else:
                y_half(k, y).start()
                y_copy(k, z, 1 - y).wait_recv()
                cross(k, z).start()
        if i == 1:
            z_take(k, opposite).wait_recv()

            @pl.when(middle)
            def _():
                if k > 0:
                    z_relay(k).start()
                if 0 < k < 3:
                    z_send(k + 1, pair).start()

            y_copy(k, opposite, y).start()
        if i == 2:
            z_take(k, other).wait_recv()
            y_copy(k, other, y).start()

    def arrived(k):
        if k < 2:
            y_copy(k, z, 1 - y).wait_recv()
            y_copy(k, pair, 1 - y).wait_recv()
        else:
            y_half(k, 1 - y).wait_recv()
            cross(k, pair).wait_recv()
        y_copy(k, opposite, 1 - y).wait_recv()
        y_copy(k, other, 1 - y).wait_recv()

    for k in range(4):
        spread(k)

    def chunk_of(k, c):
        return rows[k, :, :, columns(c)].reshape(m_rows, dc)

    class Pieces:
        def __init__(self, src, dst, sem):
            self.whole = pltpu.make_async_copy(src, dst, sem)
            count = 4
            step = dst.shape[0] // count
            self.parts = [
                pltpu.make_async_copy(src.at[r], dst.at[r], sem)
                for r in (pl.ds(i * step, step) for i in range(count))
            ]

        def start(self):
            for part_copy in self.parts:
                part_copy.start()

        def wait(self):
            self.whole.wait()

    depth_of = bu.shape[0]

    def load_up(c):
        return Pieces(wu.at[columns(c)], bu.at[c % depth_of], bus.at[c % depth_of])

    def load_fine(c):
        return Pieces(wu.at[fine_columns(c)], bu.at[c % depth_of, pl.ds(0, rc)], bus.at[c % depth_of])

    def load_down(c):
        return Pieces(wd.at[:, columns(c)], bd.at[c % depth_of], bds.at[c % depth_of])

    def prime(load, lo, hi):
        for c in range(lo, min(hi, lo + depth_of - 1)):
            load(c).start()

    def next_chunk(load, c, count=chunks):
        load(c).wait()

        @pl.when(c + depth_of - 1 < count)
        def _():
            load(c + depth_of - 1).start()

    def block_rows(s):
        return pl.ds(pl.multiple_of(s * tok, tok), tok)

    def clear(dst):
        def body(s, carry):
            dst[block_rows(s), :] = jnp.zeros((tok, width), jnp.float32)
            return carry

        lax.fori_loop(0, slots, body, 0)

    def project(k, partner, dst):
        clear(dst)
        if not partner:
            prime(load_up, 0, chunks)

        def body(c, carry):
            if not partner:
                next_chunk(load_up, c)
            lhs = chunk_of(k, c)
            for n in range(width // tile):
                cols = pl.ds(n * tile, tile)
                rhs = wu_b[columns(c), cols] if partner else bu[c % depth_of, :, cols]
                dst[:, cols] += nn(lhs, rhs)
            return carry

        lax.fori_loop(0, chunks, body, 0)

    def pick(s, column):
        return jnp.sum(jnp.where(lane == column, tabs[s], 0.0), axis=-1, keepdims=True)

    expert_of = [me, x_near]

    def activate(which, src):
        def body(s, carry):
            v = src[block_rows(s), :]
            weight = pick(s, expert_of[which])
            act[which, block_rows(s), :] = (v * jax.nn.sigmoid(v) * weight).astype(act.dtype)
            return carry

        lax.fori_loop(0, slots, body, 0)

    def prepare_b(which):
        def body(s, carry):
            r = block_rows(s)
            v = pre[which, r, :]
            sig = jax.nn.sigmoid(v)
            silu[which, r, :] = (v * sig).astype(silu.dtype)
            weight = pick(s, experts + expert_of[which])
            pre[which, r, :] = sig * (1.0 + v * (1.0 - sig)) * weight
            return carry

        lax.fori_loop(0, slots, body, 0)

    def invert(which):
        def body(s, carry):
            r = block_rows(s)
            bk = back[which, r, :]
            score = jnp.sum(bk * silu[which, r, :].astype(jnp.float32), axis=-1, keepdims=True)
            inner[which, r, :] = (bk * pre[which, r, :]).astype(inner.dtype)
            at = x if which == 0 else 1 - x
            held = 0.0 if which == 0 else sc_col[s]
            sc_col[s] = jnp.where(lane == at, score, held)
            return carry

        lax.fori_loop(0, slots, body, 0)

    fine = depth // rc
    steps = 2 * fine

    def rs_y(q):
        src = o_buf.at[q % ring, pl.ds((1 - y) * planes, planes)]
        return copy(src, y_buf.at[q], rys.at[q], ryr.at[q], y_near)

    def rs_z(q, target, place_at):
        src = t_buf.at[q % ring, target]
        return copy(src, z_buf.at[q, place_at], rzs.at[q], rzr.at[q], chip(target, y))

    def rs_far(q):
        src = t_buf.at[q % ring, other]
        return copy(src, f_buf.at[q], rzs.at[q], rfs.at[q], chip(pair, y))

    def sent_z(q):
        src = t_buf.at[q % ring, pl.ds(0, planes - 1)]
        dst = z_buf.at[q, pl.ds(0, planes - 1)]
        copy(src, dst, rzs.at[q], rzr.at[q], chip(pair, y)).wait_send()

    def fold_y(q):
        rs_y(q).wait_recv()

        def clean():
            sent_z(q - ring)

        if isinstance(q, int):
            if q >= ring:
                clean()
        else:
            pl.when(q >= ring)(clean)
        for k in range(planes):
            first = o_buf[q % ring, y * planes + k].astype(jnp.float32)
            t_buf[q % ring, k] = (first + y_buf[q, k].astype(jnp.float32)).astype(t_buf.dtype)
        rs_z(q, pair, 0).start()

        @pl.when(middle)
        def _():
            rs_z(q, other, 2).start()

        @pl.when(jnp.logical_not(middle))
        def _():
            rs_far(q).start()
            rs_z(q, opposite, 1).start()

    def relay_z(q):
        @pl.when(middle)
        def _():
            rs_far(q).wait_recv()
            total = t_buf[q % ring, opposite].astype(jnp.float32) + f_buf[q].astype(jnp.float32)
            t_buf[q % ring, opposite] = total.astype(t_buf.dtype)
            rs_z(q, opposite, 1).start()

    def take_z(q, count):
        src = t_buf.at[q % ring, pl.ds(0, count)]
        dst = z_buf.at[q, pl.ds(0, count)]
        copy(src, dst, rzs.at[q], rzr.at[q], chip(pair, y)).wait_recv()
        total = t_buf[q % ring, z].astype(jnp.float32)
        for i in range(count):
            total = total + z_buf[q, i].astype(jnp.float32)
        return total

    def fold_z(q):
        def settle(total):
            def of_a():
                out_a[:, fine_columns(q)] = ROUTED_SCALE * total

            def of_b():
                lifted[:, fine_columns(q - fine)] = total

            if isinstance(q, int):
                of_a() if q < fine else of_b()
            else:
                pl.when(q < fine)(of_a)
                pl.when(q >= fine)(of_b)

        @pl.when(middle)
        def _():
            settle(take_z(q, planes - 1))

        @pl.when(jnp.logical_not(middle))
        def _():
            settle(take_z(q, planes - 2))

    lags = ((4, fold_y), (6, relay_z), (8, fold_z))

    def behind(q):
        for lag, stage in lags:
            if isinstance(q, int):
                if lag <= q < steps + lag:
                    stage(q - lag)
            else:
                pl.when(q >= lag)(functools.partial(stage, q - lag))

    def store(q, value):
        def clean():
            rs_y(q - ring).wait_send()

        pl.when(q >= ring)(clean)
        o_buf[q % ring] = value.reshape(slots, tok, rc).astype(o_buf.dtype)
        rs_y(q).start()

    def take_up(i):
        up_x(i).wait_recv()
        up_m(i, part).start()

    def own_back(c, carry):
        next_chunk(load_down, c)
        lhs = chunk_of(2, c)
        for n in range(width // tile):
            cols = pl.ds(n * tile, tile)
            back[0, :, cols] += nt(lhs, bd[c % depth_of, cols, :])
        return carry

    def partner_back(c, carry):
        lhs = chunk_of(2, c)
        for n in range(width // tile):
            cols = pl.ds(n * tile, tile)
            back[1, :, cols] += nt(lhs, wd_b[c, cols, :])
        return carry

    for k in range(2):
        for i in range(3):
            serve(k, i)
    serve(2, 0)
    serve(2, 1)
    own_g.wait()
    arrived(0)
    arrived(1)
    take_up(0)
    take_up(1)
    project(0, False, back.at[0])
    activate(0, back.at[0])
    serve(3, 0)
    serve(3, 1)
    serve(2, 2)
    for i in range(2, n_up):
        take_up(i)
    for i in range(n_up):
        up_m(i, 1 - part).wait_recv()
    project(0, True, back.at[1])
    activate(1, back.at[1])
    hold = min(4, chunks - 2)
    prime(load_down, 0, hold + 1)
    clear(back.at[0])
    clear(back.at[1])

    def take_down(c):
        down_x(c).wait_recv()
        down_m(c, part).start()

    take_down(0)
    def forward(c, carry):
        load_down(c).wait()
        ahead = c + depth_of - 1

        @pl.when(jnp.logical_and(ahead < chunks, jnp.logical_or(ahead <= hold, c > hold)))
        def _():
            load_down(ahead).start()

        down_m(c, 1 - part).wait_recv()
        for n in range(dc // rc):
            cols = pl.ds(n * rc, rc)
            value = nn(act[0], bd[c % depth_of, :, cols]) + nn(act[1], wd_b[c, :, cols])
            store(c * (dc // rc) + n, value)

        @pl.when(c + 2 < chunks)
        def _():
            take_down(c + 1)

        @pl.when(c == 0)
        def _():
            serve(3, 2)

        @pl.when(c == hold - 2)
        def _():
            arrived(2)
            project(1, False, pre.at[0])
            prepare_b(0)

        @pl.when(c == hold - 1)
        def _():
            project(1, True, pre.at[1])
            prepare_b(1)

        @pl.when(c == hold)
        def _():
            arrived(3)
            prime(load_down, 0, chunks)
            lax.fori_loop(0, chunks, own_back, 0)
            prime(load_down, hold + 1, chunks)
            prime(load_fine, 0, fine)
            lax.fori_loop(0, hold + 1, partner_back, 0)

        @pl.when(c > hold)
        def _():
            partner_back(c, 0)

        for n in range(dc // rc):
            behind(c * (dc // rc) + n)

        @pl.when(c == hold + 1)
        def _():
            invert(0)

        @pl.when(c + 2 == chunks)
        def _():
            take_down(c + 1)

        return carry

    lax.fori_loop(0, chunks, forward, 0)
    invert(1)

    def score_copy(i, slot):
        target = of_slot((slot_me + i) % slots)
        return copy(sc_own, sc_all.at[slot], scs.at[i - 1], scr.at[i - 1], target)

    def backward(c, carry):
        next_chunk(load_fine, c, fine)
        q = fine + c
        value = nt(inner[0], bu[c % depth_of, :rc, :]) + nt(inner[1], wu_b[fine_columns(c), :])
        store(q, value)
        behind(q)

        @pl.when(c == 1)
        def _():
            sc_own[...] = sc_col[...].reshape(m_rows, lanes).T[:8]
            for i in range(1, slots):
                score_copy(i, slot_me).start()

        return carry

    lax.fori_loop(0, fine, backward, 0)

    sc_all[slot_me] = sc_own[...]
    for i in range(1, slots):
        score_copy(i, (slot_me - i + slots) % slots).wait_recv()
    table = tabs[...].reshape(m_rows, lanes).T
    lines = []
    for e in range(experts):
        plane, row, odd = e // PLANE, (e // 2) % 2, e % 2
        lines.append(sc_all[row * planes + plane, odd : odd + 1, :])
    score = jnp.concatenate(lines, axis=0)
    gate = ROUTED_SCALE * score
    mean = jnp.sum(gate * table[experts : 2 * experts], axis=0, keepdims=True)
    logit = table[2 * experts : 3 * experts] * (gate - mean)
    order = lax.broadcasted_iota(jnp.int32, (experts, m_rows), 0)
    one = jnp.sum(jnp.where(order == me, logit, 0.0), axis=0, keepdims=True)
    two = jnp.sum(jnp.where(order == x_near, logit, 0.0), axis=0, keepdims=True)
    both = jnp.concatenate([one, two, jnp.zeros((6, m_rows), jnp.float32)], axis=0)

    def thirds(v):
        high = v.astype(jnp.bfloat16)
        rest = v - high.astype(jnp.float32)
        medium = rest.astype(jnp.bfloat16)
        return (high, medium, (rest - medium.astype(jnp.float32)).astype(jnp.bfloat16))

    pieces = thirds(both)
    for c in range(chunks):
        cols = pl.ds(c * dc, dc)
        rhs = rows[1, :, :, cols].reshape(m_rows, dc)
        rg_buf[:, cols] = nn(pieces[0], rhs) + nn(pieces[1], rhs) + nn(pieces[2], rhs)

    def grad_copy(i):
        expert = me if i == 0 else x_near
        pipe = p if i == 1 else mirror
        return copy(rg_buf, rg_in.at[i], gs.at[i], gr.at[i], expert, pipe)

    for i in range(3):
        grad_copy(i).start()
    padded = jnp.concatenate([logit, jnp.zeros((lanes - experts, m_rows), jnp.float32)], axis=0)
    sc_col[...] = padded.T.reshape(slots, tok, lanes)
    for q in range(steps, steps + 3):
        behind(q)
    dense = thirds(sc_col[slot_me])
    for q in range(steps + 3, steps + lags[-1][0]):
        behind(q)

    inv = rinv_b[:, 0:1]
    dots = jnp.zeros((tok, 1), jnp.float32)
    for c in range(chunks):
        cols = pl.ds(c * dc, dc)
        rhs = router_t[:, cols]
        extra = nn(dense[0], rhs) + nn(dense[1], rhs) + nn(dense[2], rhs)
        v = ROUTED_SCALE * lifted[:, cols] + extra
        lifted[:, cols] = v
        dots = dots + jnp.sum(v * hid_b[:, cols].astype(jnp.float32), axis=-1, keepdims=True)
    slope = inv * inv * inv * (dots / depth)
    for c in range(chunks):
        cols = pl.ds(c * dc, dc)
        hidden = hid_b[:, cols].astype(jnp.float32)
        out_b[:, cols] = inv * lifted[:, cols] - hidden * slope
    for i in range(3):
        grad_copy(i).wait_recv()
    rg_out[0:1, :] = rg_buf[0:1, :] + rg_in[0, 0:1, :]
    rg_out[1:2, :] = rg_in[1, 1:2, :] + rg_in[2, 1:2, :]

    for k in range(4):
        z_send(k, pair).wait_send()
        z_send(k, opposite).wait_send()

        if k == 0:
            z_send(k, other).wait_send()
        else:

            @pl.when(middle)
            def _():
                z_send(k, other).wait_send()
                z_relay(k).wait_send()

        y_send(k).wait_send()
        if k < 2:
            y_copy(k, pair, y).wait_send()
        else:
            cross(k, z).wait_send()
            y_half(k, y).wait_send()
        for source in (opposite, other):
            y_copy(k, source, y).wait_send()
    for i in range(n_up):
        up_x(i).wait_send()
        up_m(i, part).wait_send()

    def drain(c, carry):
        down_x(c).wait_send()
        down_m(c, part).wait_send()
        return carry

    lax.fori_loop(0, chunks, drain, 0)

    def drain_rs(q, carry):
        rs_y(q).wait_send()
        sent_z(q)
        return carry

    lax.fori_loop(steps - ring, steps, drain_rs, 0)
    for i in range(1, slots):
        score_copy(i, slot_me).wait_send()
    for i in range(3):
        grad_copy(i).wait_send()


N_UP = 4
RING = 8
AHEAD = 3


def fused_plan(n, tok, depth, width):
    planes = n // PLANE
    slots = 2 * planes
    m_rows = slots * tok
    dc = 512 if depth % 512 == 0 else 256
    rc = 256
    chunks = depth // dc
    steps = 2 * (depth // rc)
    bf, f32 = jnp.bfloat16, jnp.float32
    buffers = [
        ((3, slots, tok, depth), bf),
        ((slots, tok, 128), f32),
        ((depth, width), bf),
        ((chunks, width, dc), bf),
        ((AHEAD, dc, width), bf),
        ((AHEAD, width, dc), bf),
        ((2, m_rows, width), bf),
        ((2, m_rows, width), f32),
        ((2, m_rows, width), f32),
        ((2, m_rows, width), bf),
        ((2, m_rows, width), bf),
        ((RING, slots, tok, rc), bf),
        ((steps, planes, tok, rc), bf),
        ((RING, planes, tok, rc), bf),
        ((steps, planes - 1, tok, rc), bf),
        ((steps, tok, rc), bf),
        ((slots, tok, 128), f32),
        ((8, m_rows), f32),
        ((slots, 8, m_rows), f32),
        ((8, depth), f32),
        ((3, 8, depth), f32),
        ((128, depth), bf),
        ((tok, 128), f32),
        ((tok, depth), f32),
    ]
    sems = (
        [(1,)]
        + [(4, planes + 1)] * 2
        + [(4, planes)] * 2
        + [(N_UP + chunks,)] * 4
        + [(AHEAD,)] * 2
        + [(steps,)] * 5
        + [(slots - 1,)] * 2
        + [(3,)] * 2
    )
    total = sum(math.prod(shape) * jnp.dtype(kind).itemsize for shape, kind in buffers)
    fits = total + 7 * tok * depth * 2 < 64_500_000 and 3 * n <= 128 and planes == 4
    return fits, (planes, tok, depth, width, dc, rc, N_UP, RING), buffers, sems


def fused(plan, *args):
    _, dims, buffers, sems = plan
    tok, depth = dims[1:3]
    vmem = pl.BlockSpec(memory_space=pltpu.VMEM)
    hbm = pl.BlockSpec(memory_space=pl.ANY)
    return pl.pallas_call(
        functools.partial(fused_kernel, dims + (lax.axis_size("pipe"),)),
        out_shape=[
            jax.ShapeDtypeStruct((tok, depth), jnp.float32),
            jax.ShapeDtypeStruct((tok, depth), jnp.float32),
            jax.ShapeDtypeStruct((2, depth), jnp.float32),
        ],
        in_specs=[vmem] * 6 + [hbm] * 2,
        out_specs=[vmem] * 3,
        scratch_shapes=[pltpu.VMEM(shape, kind) for shape, kind in buffers]
        + [DMA(shape) for shape in sems],
        compiler_params=pltpu.CompilerParams(
            collective_id=7, has_side_effects=True, vmem_limit_bytes=67_000_000
        ),
    )(*args)


def on_device_fused(
    plan, hidden_a, routes_a, hidden_b, routes_b, grad_out_b, router, w_up, w_down
):
    mixed, delta, terms = fused(
        plan,
        hidden_a[0],
        hidden_b[0],
        grad_out_b[0],
        routes_a[0].T,
        routes_b[0].T,
        router[0],
        w_up[0, 0],
        w_down[0, 0],
    )
    layer_out = (hidden_a[0].astype(jnp.float32) + mixed).astype(jnp.bfloat16)
    grad_in = (grad_out_b[0].astype(jnp.float32) + delta).astype(jnp.bfloat16)
    return (layer_out[None], grad_in[None], jnp.sum(terms, axis=0)[None, None])


def solution(mesh):
    placed = (
        P("pipe", "expert", None),
        P("pipe", "expert", None),
        P("pipe", "expert", None),
        P("pipe", "expert", None),
        P("pipe", "expert", None),
        P("pipe", None, None),
        P("pipe", "expert", None, None),
        P("pipe", "expert", None, None),
    )

    def body(*args):
        w_up = args[6]
        plan = fused_plan(lax.axis_size("expert"), args[0].shape[1], w_up.shape[2], w_up.shape[3])
        if w_up.shape[1] == 1 and plan[0]:
            return on_device_fused(plan, *args)
        return on_device(*args)

    return jax.shard_map(
        body,
        mesh=mesh,
        in_specs=placed,
        out_specs=(P("pipe", "expert", None), P("pipe", "expert", None), P("pipe", "expert", None)),
        check_vma=False,
    )
```

```python
import functools
import math

import jax
import jax.numpy as jnp
from jax import lax
from jax.experimental import pallas as pl
from jax.experimental.pallas import tpu as pltpu
from jax.sharding import PartitionSpec as P

ROUTED_SCALE = 2.5
EPSILON = 1e-06


def partner(block, axis, bit):
    count = lax.axis_size(axis)
    route = []
    for low in range(count):
        high = low | 1 << bit
        if high != low and high < count:
            route += [(low, high), (high, low)]
    return lax.ppermute(block, axis, route)


MESH = pl.DeviceIdType.MESH
DMA = pltpu.SemaphoreType.DMA
PLANE = 4


def remote(src, dst, send_sem, recv_sem, target):
    return pltpu.make_async_remote_copy(
        src_ref=src,
        dst_ref=dst,
        send_sem=send_sem,
        recv_sem=recv_sem,
        device_id={"expert": target},
        device_id_type=MESH,
    )


def place():
    me = lax.axis_index("expert")
    z, y, x = me // PLANE, (me // 2) % 2, me % 2
    return (me, z, y, x, me + 1 - 2 * x, me + 2 - 4 * y)


def greet(planes):
    me, z, y, x, x_near, y_near = place()
    barrier = pltpu.get_barrier_semaphore()
    pl.semaphore_signal(barrier, inc=1, device_id={"expert": x_near}, device_id_type=MESH)
    pl.semaphore_signal(barrier, inc=1, device_id={"expert": y_near}, device_id_type=MESH)

    @pl.when(z < planes - 1)
    def _():
        pl.semaphore_signal(barrier, inc=1, device_id={"expert": me + PLANE}, device_id_type=MESH)

    @pl.when(z > 0)
    def _():
        pl.semaphore_signal(barrier, inc=1, device_id={"expert": me - PLANE}, device_id_type=MESH)

    ends = jnp.where(z == 0, 1, 0) + jnp.where(z == planes - 1, 1, 0)
    pl.semaphore_wait(barrier, 4 - ends)


def gather_kernel(count, planes, *refs):
    ins, outs = refs[:count], refs[count : 2 * count]
    own_sem, up_s, down_s, z_r, x_s, x_r, y_s, y_r, d_s, d_r = refs[2 * count :]
    me, z, y, x, x_near, y_near = place()

    def up(k, p, src):
        return remote(src, outs[k].at[p * PLANE + y * 2 + x], up_s.at[k, p], z_r.at[k, p], me + PLANE)

    def down(k, p, src):
        return remote(src, outs[k].at[p * PLANE + y * 2 + x], down_s.at[k, p], z_r.at[k, p], me - PLANE)

    def to_x(k, p, src):
        return remote(src, outs[k].at[p * PLANE + y * 2 + x], x_s.at[k, p], x_r.at[k, p], x_near)

    def to_y(k, p, src):
        return remote(src, outs[k].at[p * PLANE + y * 2 + x], y_s.at[k, p], y_r.at[k, p], y_near)

    def half(k, p, way):
        if way == 0:
            ref = outs[k].at[p * PLANE + y * 2 + 1 - x, 0]
            return remote(ref, ref, d_s.at[k, p, 0], d_r.at[k, p, 0], y_near)
        ref = outs[k].at[p * PLANE + (1 - y) * 2 + x, 1]
        return remote(ref, ref, d_s.at[k, p, 1], d_r.at[k, p, 1], x_near)

    def each(d, act):
        if d == 0:
            act(z, 0)
            return

        @pl.when(z >= d)
        def _():
            act(z - d, 1)

        @pl.when(z + d < planes)
        def _():
            act(z + d, -1)

    def spread(k, p, way, wait):
        src = ins[k] if way == 0 else outs[k].at[p * PLANE + y * 2 + x]

        def do(copy):
            copy.wait_send() if wait else copy.start()

        if way != 0 and not wait:
            up(k, p, src).wait_recv()
        if way >= 0:

            @pl.when(z < planes - 1)
            def _():
                do(up(k, p, src))

        if way <= 0:

            @pl.when(z > 0)
            def _():
                do(down(k, p, src))

        do(to_x(k, p, src))
        do(to_y(k, p, src))

    def relay(k, p, way):
        to_x(k, p, ins[k]).wait_recv()
        half(k, p, 0).start()
        to_y(k, p, ins[k]).wait_recv()
        half(k, p, 1).start()

    def finish(k, p, way):
        for route in range(2):
            half(k, p, route).wait()
        spread(k, p, way, True)

    greet(planes)
    for k in range(count):
        pltpu.make_async_copy(ins[k], outs[k].at[me], own_sem.at[k]).start()
        each(0, lambda p, way: spread(k, p, way, False))
    for k in range(count):
        for d in range(1, planes):
            each(d, lambda p, way: spread(k, p, way, False))
            each(d - 1, lambda p, way: relay(k, p, way))
        each(planes - 1, lambda p, way: relay(k, p, way))
    for k in range(count):
        for d in range(planes):
            each(d, lambda p, way: finish(k, p, way))
        pltpu.make_async_copy(ins[k], outs[k].at[me], own_sem.at[k]).wait()


def gather_all(blocks, collective_id):
    n = lax.axis_size("expert")
    planes = n // PLANE
    count = len(blocks)
    halved = [b.reshape(2, b.shape[0] // 2, b.shape[1]) for b in blocks]
    outs = pl.pallas_call(
        functools.partial(gather_kernel, count, planes),
        out_shape=[jax.ShapeDtypeStruct((n,) + b.shape, b.dtype) for b in halved],
        in_specs=[pl.BlockSpec(memory_space=pltpu.VMEM)] * count,
        out_specs=[pl.BlockSpec(memory_space=pl.ANY)] * count,
        scratch_shapes=[DMA((count,))] + [DMA((count, planes))] * 7 + [DMA((count, planes, 2))] * 2,
        compiler_params=pltpu.CompilerParams(collective_id=collective_id, has_side_effects=True),
    )(*halved)
    return [o.reshape(n * b.shape[0], b.shape[1]) for o, b in zip(outs, blocks)]


def scatter_stages(planes, part, out, a_r, c_r, b_x, b_y, total, z_r, *sems):
    ax_s, ax_r, ay_s, ay_r, cx_s, cx_r, cy_s, cy_r, z_s, up_r, down_r = sems
    me, z, y, x, x_near, y_near = place()
    rows, cols = part.shape[2:]
    step = 16

    def slot(p, yy, xx):
        return p * PLANE + yy * 2 + xx

    def add(dst, *srcs):
        def body(i, carry):
            r = pl.ds(pl.multiple_of(i * step, step), step)
            acc = srcs[0][r, :].astype(jnp.float32)
            for s in srcs[1:]:
                acc = acc + s[r, :].astype(jnp.float32)
            dst[r, :] = acc.astype(dst.dtype)
            return carry

        lax.fori_loop(0, rows // step, body, 0)

    def diagonal(p):
        src = slot(p, 1 - y, 1 - x)
        return (
            remote(part.at[src, 0], a_r.at[p, 0], ay_s.at[p], ay_r.at[p], y_near),
            remote(part.at[src, 1], a_r.at[p, 1], ax_s.at[p], ax_r.at[p], x_near),
        )

    def beside(p):
        return (
            remote(b_x.at[p, 0], c_r.at[p, 0, 0], cx_s.at[p, 0], cx_r.at[p, 0], x_near),
            remote(part.at[slot(p, y, 1 - x), 1], c_r.at[p, 0, 1], cx_s.at[p, 1], cx_r.at[p, 1], x_near),
            remote(b_y.at[p, 0], c_r.at[p, 1, 1], cy_s.at[p, 0], cy_r.at[p, 0], y_near),
            remote(part.at[slot(p, 1 - y, x), 0], c_r.at[p, 1, 0], cy_s.at[p, 1], cy_r.at[p, 1], y_near),
        )

    def rise(p):
        return remote(total.at[p], z_r.at[0, p], z_s.at[p], up_r.at[p], me + PLANE)

    def sink(p):
        return remote(total.at[p], z_r.at[1, p], z_s.at[p], down_r.at[p], me - PLANE)

    def first(p, way):
        for copy in diagonal(p):
            copy.start()
        beside(p)[1].start()
        beside(p)[3].start()

    def second(p, way):
        to_y, to_x = diagonal(p)
        to_y.wait_recv()
        add(b_x.at[p, 0], part.at[slot(p, y, 1 - x), 0], a_r.at[p, 0])
        beside(p)[0].start()
        to_x.wait_recv()
        add(b_y.at[p, 0], part.at[slot(p, 1 - y, x), 1], a_r.at[p, 1])
        beside(p)[2].start()

    def third(p, way):
        for copy in beside(p):
            copy.wait_recv()
        for h in range(2):
            add(total.at[p, h], part.at[slot(p, y, x), h], c_r.at[p, 0, h], c_r.at[p, 1, h])

        def take(copy, level):
            copy.wait_recv()
            for h in range(2):
                add(total.at[p, h], total.at[p, h], z_r.at[level, p, h])

        if way >= 0:

            @pl.when(z > 0)
            def _():
                take(rise(p), 0)

        if way <= 0:

            @pl.when(z < planes - 1)
            def _():
                take(sink(p), 1)

        if way > 0:
            rise(p).start()
        if way < 0:
            sink(p).start()
        if way == 0:
            out[...] = total[p]

    def finish(p, way):
        for copy in diagonal(p) + beside(p):
            copy.wait_send()
        if way != 0:
            rise(p).wait_send()

    return (first, second, third, finish)


def scatter_kernel(planes, count, *refs):
    parts, outs, rest = refs[:count], refs[count : 2 * count], refs[2 * count :]
    per = len(rest) // count
    z = place()[1]
    stages = [
        scatter_stages(planes, parts[k], outs[k], *rest[k * per : (k + 1) * per])
        for k in range(count)
    ]

    def each(d, act):
        if d == 0:
            act(z, 0)
            return

        @pl.when(z >= d)
        def _():
            act(z - d, -1)

        @pl.when(z + d < planes)
        def _():
            act(z + d, 1)

    greet(planes)
    order = list(range(planes - 1, -1, -1))
    for k in range(count):
        for d in order:
            each(d, stages[k][0])
    for i, d in enumerate(order):
        for k in range(count):
            each(d, stages[k][1])
        if i > 0:
            for k in range(count):
                each(order[i - 1], stages[k][2])
    for k in range(count):
        each(0, stages[k][2])
    for k in range(count):
        for d in order:
            each(d, stages[k][3])


def scatter_sums(parts, collective_id):
    n = lax.axis_size("expert")
    planes = n // PLANE
    tokens, cols = parts[0].shape
    rows = tokens // n // 2
    half = (rows, cols)
    kind = parts[0].dtype
    count = len(parts)
    if count > 1 and count * 3 * parts[0].size * kind.itemsize > 56 << 20:
        return [scatter_sums([part], collective_id + k)[0] for k, part in enumerate(parts)]
    outs = pl.pallas_call(
        functools.partial(scatter_kernel, planes, count),
        out_shape=[jax.ShapeDtypeStruct((2,) + half, kind)] * count,
        in_specs=[pl.BlockSpec(memory_space=pltpu.VMEM)] * count,
        out_specs=[pl.BlockSpec(memory_space=pltpu.VMEM)] * count,
        scratch_shapes=(
            [
                pltpu.VMEM((planes, 2) + half, kind),
                pltpu.VMEM((planes, 2, 2) + half, kind),
                pltpu.VMEM((planes, 1) + half, kind),
                pltpu.VMEM((planes, 1) + half, kind),
                pltpu.VMEM((planes, 2) + half, kind),
                pltpu.VMEM((2, planes, 2) + half, kind),
            ]
            + [DMA((planes,))] * 4
            + [DMA((planes, 2))] * 4
            + [DMA((planes,))] * 3
        )
        * count,
        compiler_params=pltpu.CompilerParams(
            collective_id=collective_id, has_side_effects=True, vmem_limit_bytes=60 << 20
        ),
    )(*[part.reshape((n, 2) + half) for part in parts])
    return [out.reshape(2 * rows, cols) for out in outs]


def prepare(hidden, routes, router_segment):
    expert_count = router_segment.shape[0]
    hidden32 = hidden.astype(jnp.float32)
    rinv = lax.rsqrt(jnp.mean(hidden32 * hidden32, axis=-1, keepdims=True) + EPSILON)
    normed = (hidden32 * rinv).astype(jnp.bfloat16)
    logits = jnp.einsum("td,ed->te", normed, router_segment, preferred_element_type=jnp.float32)
    chosen = jnp.any(
        routes[:, :, None] == jnp.arange(expert_count, dtype=jnp.int32)[None, None, :], axis=1
    )
    affinity = jnp.where(chosen, jax.nn.sigmoid(logits), 0.0)
    return (hidden32, rinv, normed, affinity)


def on_device(hidden_a, routes_a, hidden_b, routes_b, grad_out_b, router, w_up, w_down):
    n_expert = lax.axis_size("expert")
    me = lax.axis_index("expert")
    tok_count = hidden_a.shape[1]
    router_segment = router[0]
    expert_count = router_segment.shape[0]
    local_count = w_up.shape[1]
    hidden32_a, rinv_a, normed_a, affinity_a = prepare(hidden_a[0], routes_a[0], router_segment)
    hidden32_b, rinv_b, normed_b, affinity_b = prepare(hidden_b[0], routes_b[0], router_segment)
    grad_out = grad_out_b[0]
    affinity_ab = jnp.concatenate([affinity_a, affinity_b], axis=1)
    lanes = -(-2 * expert_count // 128) * 128
    affinity_ab = jnp.pad(affinity_ab, ((0, 0), (0, lanes - 2 * expert_count)))
    rows_a, rows_b, rows_g, affinities = gather_all([normed_a, normed_b, grad_out, affinity_ab], 1)
    aff_a, aff_b = affinities[:, :expert_count], affinities[:, expert_count : 2 * expert_count]
    total_b = jnp.sum(aff_b, axis=1, keepdims=True)
    weight_a = aff_a / jnp.sum(aff_a, axis=1, keepdims=True)
    weight_b = aff_b / total_b

    def column(table, local):
        return lax.dynamic_slice_in_dim(table, me * local_count + local, 1, axis=1)

    sum_a = 0.0
    sum_b = 0.0
    scores = []
    for local in range(local_count):
        up, down = w_up[0, local], w_down[0, local]
        pre = jnp.dot(rows_a, up, preferred_element_type=jnp.float32)
        active = jax.nn.silu(pre).astype(jnp.bfloat16)
        out = jnp.dot(active, down, preferred_element_type=jnp.float32)
        sum_a = sum_a + out * column(weight_a, local)
    for local in range(local_count):
        up, down = w_up[0, local], w_down[0, local]
        pre = jnp.dot(rows_b, up, preferred_element_type=jnp.float32)
        back = jnp.einsum("td,fd->tf", rows_g, down, preferred_element_type=jnp.float32)
        sig = jax.nn.sigmoid(pre)
        scores.append(jnp.sum(back * (pre * sig), axis=-1))
        inner = (back * (sig * (1.0 + pre * (1.0 - sig)))).astype(jnp.bfloat16)
        lifted = jnp.einsum("tf,df->td", inner, up, preferred_element_type=jnp.float32)
        sum_b = sum_b + lifted * column(weight_b, local)
    sum_ab = scatter_sums([sum_a.astype(jnp.bfloat16), sum_b.astype(jnp.bfloat16)], 2)
    mixed = sum_ab[0].astype(jnp.float32)
    layer_out = (hidden32_a + ROUTED_SCALE * mixed).astype(jnp.bfloat16)

    flat = jnp.stack(scores).reshape(-1)
    padded = jnp.pad(flat, (0, -flat.shape[0] % 2048)).reshape(-1, 128)
    score = gather_all([padded], 4)[0].reshape(n_expert, -1)[:, : flat.shape[0]]
    score = score.reshape(expert_count, -1).T
    score = jnp.where(aff_b > 0.0, score, 0.0)
    gate_grad = ROUTED_SCALE * score
    logit_grad = (
        aff_b
        * (1.0 - aff_b)
        * (gate_grad - jnp.sum(gate_grad * weight_b, axis=1, keepdims=True))
        / total_b
    )
    own_columns = lax.dynamic_slice_in_dim(logit_grad, me * local_count, local_count, axis=1)
    own_term = jnp.dot(
        own_columns.T, rows_b.astype(jnp.float32), precision=lax.Precision.HIGHEST
    )
    mirrored = own_term
    for bit in range(lax.axis_size("pipe").bit_length() - 1):
        mirrored = partner(mirrored, "pipe", bit)
    router_grad = own_term + mirrored

    dense = lax.dynamic_slice_in_dim(logit_grad, me * tok_count, tok_count, axis=0)
    lifted_sum = sum_ab[1].astype(jnp.float32)
    normed_grad = ROUTED_SCALE * lifted_sum + jnp.dot(
        dense, router_segment.astype(jnp.float32), precision=lax.Precision.HIGHEST
    )
    mean_term = jnp.mean(normed_grad * hidden32_b, axis=-1, keepdims=True)
    grad_in = (
        grad_out.astype(jnp.float32) + rinv_b * normed_grad - hidden32_b * rinv_b**3 * mean_term
    )
    return (layer_out[None], grad_in.astype(jnp.bfloat16)[None], router_grad[None])


def fused_kernel(dims, *refs):
    planes, tok, depth, width, kc, dc, rc, n_up, ring, n_pipe = dims
    (hid_a, hid_b, g, routes_a, routes_b, router, wu, wd, out_a, out_b, rg_out) = refs[:11]
    (rows, tabs, wu_b, wd_b, bu, bd, act, pre, back, silu, inner) = refs[11:22]
    (o_buf, y_buf, t_buf, z_buf, f_buf, sc_col, sc_own, sc_all, rg_buf, rg_in) = refs[22:32]
    (router_t, rinv_b, lifted) = refs[32:35]
    (own_s, zs, zr, ys, yr, xs, xr, ms, mr, bus, bds) = refs[35:46]
    (rys, ryr, rzs, rzr, rfs, scs, scr, gs, gr) = refs[46:55]
    slots = 2 * planes
    experts = 2 * slots
    m_rows = slots * tok
    chunks = depth // dc
    half_d = depth // 2
    half_f = width // 2
    half_t = tok // 2
    up_rows = half_d // n_up
    tile = 256
    lanes = tabs.shape[-1]
    me, z, y, x, x_near, y_near = place()
    p = lax.axis_index("pipe")
    mirror = n_pipe - 1 - p
    part = (2 * p) // n_pipe
    slot_me = y * planes + z
    pair = z + 1 - 2 * (z % 2)
    opposite = (z + 2) % planes
    other = (pair + 2) % planes
    middle = (z + 1) // 2 == 1

    def copy(src, dst, send, recv, expert, pipe=p):
        return pltpu.make_async_remote_copy(
            src_ref=src,
            dst_ref=dst,
            send_sem=send,
            recv_sem=recv,
            device_id={"pipe": pipe, "expert": expert},
            device_id_type=MESH,
        )

    def chip(plane, row):
        return plane * PLANE + row * 2 + x

    def of_slot(s):
        return chip(s % planes, s // planes)

    barrier = pltpu.get_barrier_semaphore()

    def hello(pipe, expert):
        pl.semaphore_signal(
            barrier, inc=1, device_id={"pipe": pipe, "expert": expert}, device_id_type=MESH
        )

    for i in range(1, slots):
        hello(p, of_slot((slot_me + i) % slots))
    hello(p, x_near)
    hello(mirror, me)
    hello(mirror, x_near)

    own_g = pltpu.make_async_copy(g, rows.at[2, slot_me], own_s.at[0])
    own_g.start()

    pl.semaphore_wait(barrier, slots - 1 + 3)

    def up_region(which, i):
        return pl.ds(pl.multiple_of(which * half_d + i * up_rows, up_rows), up_rows)

    def up_x(i):
        r = up_region(part, i)
        return copy(wu.at[r], wu_b.at[r], xs.at[i], xr.at[i], x_near)

    def up_m(i, which):
        r = up_region(which, i)
        return copy(wu_b.at[r], wu_b.at[r], ms.at[i], mr.at[i], me, mirror)

    def down_rows(which):
        return pl.ds(pl.multiple_of(which * half_f, half_f), half_f)

    def columns(c):
        return pl.ds(pl.multiple_of(c * dc, dc), dc)

    def wide_columns(c):
        return pl.ds(pl.multiple_of(c * kc, kc), kc)

    def fine_columns(c):
        return pl.ds(pl.multiple_of(c * rc, rc), rc)

    def down_x(c):
        r = down_rows(part)
        src = wd.at[r, columns(c)]
        return copy(src, wd_b.at[c, r], xs.at[n_up + c], xr.at[n_up + c], x_near)

    def down_m(c, which):
        ref = wd_b.at[c, down_rows(which)]
        return copy(ref, ref, ms.at[n_up + c], mr.at[n_up + c], me, mirror)

    for i in range(n_up):
        up_x(i).start()
    for c in range(chunks):
        down_x(c).start()

    bufs = [tabs, rows.at[0], rows.at[1], rows.at[2]]

    def block(k, row, source):
        return bufs[k].at[row * planes + source]

    def mine(k):
        return g if k == 3 else bufs[k].at[slot_me]

    def z_send(k, target):
        dst = bufs[k].at[slot_me]
        return copy(mine(k), dst, zs.at[k, target], zr.at[k, z], chip(target, y))

    def z_take(k, source):
        ref = block(k, y, source)
        return copy(ref, ref, zs.at[k, source], zr.at[k, source], chip(source, y))

    def z_relay(k):
        ref = block(k, y, opposite)
        return copy(ref, ref, zs.at[k, z], zr.at[k, opposite], chip(pair, y))

    def late(ref):
        return ref.at[pl.ds(half_t, half_t)]

    def early(ref):
        return ref.at[pl.ds(0, half_t)]

    def cross(k, source):
        ref = late(block(k, 1 - y, source))
        return copy(ref, ref, zs.at[k, planes], zr.at[k, planes], chip(pair, y))

    def y_send(k):
        return copy(mine(k), bufs[k].at[slot_me], ys.at[k, z], yr.at[k, z], y_near)

    def y_copy(k, source, row):
        ref = block(k, row, source)
        return copy(ref, ref, ys.at[k, source], yr.at[k, source], y_near)

    def y_half(k, row):
        ref = early(block(k, row, pair))
        return copy(ref, ref, ys.at[k, pair], yr.at[k, pair], y_near)

    def spread(k):
        if k < 3:
            y_send(k).start()

        @pl.when(middle)
        def _():
            if k < 2:
                z_send(k, pair).start()
            z_send(k, other).start()

        @pl.when(jnp.logical_not(middle))
        def _():
            z_send(k, pair).start()
            if k == 0:
                z_send(k, other).start()

        z_send(k, opposite).start()

    def serve(k, i):
        if i == 0:
            z_take(k, pair).wait_recv()
            if k < 2:
                y_copy(k, pair, y).start()
            else:
                y_half(k, y).start()
                y_copy(k, z, 1 - y).wait_recv()
                cross(k, z).start()
        if i == 1:
            z_take(k, opposite).wait_recv()

            @pl.when(middle)
            def _():
                if k > 0:
                    z_relay(k).start()
                if 0 < k < 3:
                    z_send(k + 1, pair).start()

            y_copy(k, opposite, y).start()
        if i == 2:
            z_take(k, other).wait_recv()
            y_copy(k, other, y).start()

    def arrived(k):
        if k < 2:
            y_copy(k, z, 1 - y).wait_recv()
            y_copy(k, pair, 1 - y).wait_recv()
        else:
            y_half(k, 1 - y).wait_recv()
            cross(k, pair).wait_recv()
        y_copy(k, opposite, 1 - y).wait_recv()
        y_copy(k, other, 1 - y).wait_recv()

    y_send(3).start()

    def nn(lhs, rhs):
        return jnp.dot(lhs, rhs, preferred_element_type=jnp.float32)

    def nt(lhs, rhs):
        return lax.dot_general(
            lhs, rhs, (((1,), (1,)), ((), ())), preferred_element_type=jnp.float32
        )

    def normalize(k, src):
        step = 16

        def body(i, carry):
            r = pl.ds(pl.multiple_of(i * step, step), step)
            h = src[r, :].astype(jnp.float32)
            rinv = lax.rsqrt(jnp.mean(h * h, axis=-1, keepdims=True) + EPSILON)
            rows[k, slot_me, r, :] = (h * rinv).astype(rows.dtype)
            if k == 1:
                rinv_b[r, :] = jnp.broadcast_to(rinv, (step, lanes))
            return carry

        lax.fori_loop(0, tok // step, body, 0)

    normalize(0, hid_a)
    normalize(1, hid_b)
    for i in range(3):
        router_t[i * experts : (i + 1) * experts] = router[...]
    router_t[3 * experts :] = jnp.zeros((lanes - 3 * experts, depth), router_t.dtype)
    lane = lax.broadcasted_iota(jnp.int32, (tok, lanes), 1)
    expert_lane = lax.rem(lane, experts)

    def affinity(k, routes, section):
        logits = nt(rows[k, slot_me], router_t[...])
        named = routes[...].T
        chosen = expert_lane == named[:, 0:1]
        for i in range(1, named.shape[1]):
            chosen = jnp.logical_or(chosen, expert_lane == named[:, i : i + 1])
        sig = jnp.where(chosen, jax.nn.sigmoid(logits), 0.0)
        here = jnp.where(lax.div(lane, experts) == section, sig, 0.0)
        return sig, here, jnp.sum(here, axis=-1, keepdims=True)

    _, here_a, total_a = affinity(0, routes_a, 0)
    sig_b, here_b, total_b = affinity(1, routes_b, 1)
    slope_b = jnp.where(lax.div(lane, experts) == 2, sig_b * (1.0 - sig_b), 0.0)
    tabs[slot_me] = here_a / total_a + here_b / total_b + slope_b / total_b

    for k in range(4):
        spread(k)

    def chunk_of(k, cols):
        return rows[k, :, :, cols].reshape(m_rows, cols.size)

    class Pieces:
        def __init__(self, src, dst, sem):
            self.whole = pltpu.make_async_copy(src, dst, sem)
            count = 4
            step = dst.shape[0] // count
            self.parts = [
                pltpu.make_async_copy(src.at[r], dst.at[r], sem)
                for r in (pl.ds(i * step, step) for i in range(count))
            ]

        def start(self):
            for part_copy in self.parts:
                part_copy.start()

        def wait(self):
            self.whole.wait()

    depth_of = bu.shape[0]

    def load_up(c):
        return Pieces(wu.at[wide_columns(c)], bu.at[c % depth_of], bus.at[c % depth_of])

    def load_fine(c):
        return Pieces(wu.at[fine_columns(c)], bu.at[c % depth_of, pl.ds(0, rc)], bus.at[c % depth_of])

    def load_down(c):
        dst = bd.at[c % depth_of, :, pl.ds(0, dc)]
        return Pieces(wd.at[:, columns(c)], dst, bds.at[c % depth_of])

    def prime(load, lo, hi):
        for c in range(lo, min(hi, lo + depth_of - 1)):
            load(c).start()

    def next_chunk(load, c, count=chunks):
        load(c).wait()

        @pl.when(c + depth_of - 1 < count)
        def _():
            load(c + depth_of - 1).start()

    def block_rows(s):
        return pl.ds(pl.multiple_of(s * tok, tok), tok)

    def clear(dst):
        def body(s, carry):
            dst[block_rows(s), :] = jnp.zeros((tok, width), jnp.float32)
            return carry

        lax.fori_loop(0, slots, body, 0)

    def project(k, partner, dst):
        clear(dst)
        count = depth // kc
        if not partner:
            prime(load_up, 0, count)

        def body(c, carry):
            if not partner:
                next_chunk(load_up, c, count)
            lhs = chunk_of(k, wide_columns(c))
            for n in range(width // tile):
                cols = pl.ds(n * tile, tile)
                rhs = wu_b[wide_columns(c), cols] if partner else bu[c % depth_of, :, cols]
                dst[:, cols] += nn(lhs, rhs)
            return carry

        lax.fori_loop(0, count, body, 0)

    def pick(s, column):
        return jnp.sum(jnp.where(lane == column, tabs[s], 0.0), axis=-1, keepdims=True)

    expert_of = [me, x_near]

    def activate(which, src):
        def body(s, carry):
            v = src[block_rows(s), :]
            weight = pick(s, expert_of[which])
            act[which, block_rows(s), :] = (v * jax.nn.sigmoid(v) * weight).astype(act.dtype)
            return carry

        lax.fori_loop(0, slots, body, 0)

    def prepare_b(which):
        def body(s, carry):
            r = block_rows(s)
            v = pre[which, r, :]
            sig = jax.nn.sigmoid(v)
            silu[which, r, :] = (v * sig).astype(silu.dtype)
            weight = pick(s, experts + expert_of[which])
            pre[which, r, :] = sig * (1.0 + v * (1.0 - sig)) * weight
            return carry

        lax.fori_loop(0, slots, body, 0)

    def invert(which):
        def body(s, carry):
            r = block_rows(s)
            bk = back[which, r, :]
            score = jnp.sum(bk * silu[which, r, :].astype(jnp.float32), axis=-1, keepdims=True)
            inner[which, r, :] = (bk * pre[which, r, :]).astype(inner.dtype)
            at = x if which == 0 else 1 - x
            held = 0.0 if which == 0 else sc_col[s]
            sc_col[s] = jnp.where(lane == at, score, held)
            return carry

        lax.fori_loop(0, slots, body, 0)

    fine = depth // rc
    steps = 2 * fine

    def rs_y(q):
        src = o_buf.at[q % ring, pl.ds((1 - y) * planes, planes)]
        return copy(src, y_buf.at[q], rys.at[q], ryr.at[q], y_near)

    def rs_z(q, target, place_at):
        src = t_buf.at[q % ring, target]
        return copy(src, z_buf.at[q, place_at], rzs.at[q], rzr.at[q], chip(target, y))

    def rs_far(q):
        src = t_buf.at[q % ring, other]
        return copy(src, f_buf.at[q], rzs.at[q], rfs.at[q], chip(pair, y))

    def sent_z(q):
        src = t_buf.at[q % ring, pl.ds(0, planes - 1)]
        dst = z_buf.at[q, pl.ds(0, planes - 1)]
        copy(src, dst, rzs.at[q], rzr.at[q], chip(pair, y)).wait_send()

    def fold_y(q):
        rs_y(q).wait_recv()

        def clean():
            sent_z(q - ring)

        if isinstance(q, int):
            if q >= ring:
                clean()
        else:
            pl.when(q >= ring)(clean)
        for k in range(planes):
            first = o_buf[q % ring, y * planes + k].astype(jnp.float32)
            t_buf[q % ring, k] = (first + y_buf[q, k].astype(jnp.float32)).astype(t_buf.dtype)
        rs_z(q, pair, 0).start()

        @pl.when(middle)
        def _():
            rs_z(q, other, 2).start()

        @pl.when(jnp.logical_not(middle))
        def _():
            rs_far(q).start()
            rs_z(q, opposite, 1).start()

    def relay_z(q):
        @pl.when(middle)
        def _():
            rs_far(q).wait_recv()
            total = t_buf[q % ring, opposite].astype(jnp.float32) + f_buf[q].astype(jnp.float32)
            t_buf[q % ring, opposite] = total.astype(t_buf.dtype)
            rs_z(q, opposite, 1).start()

    def take_z(q, count):
        src = t_buf.at[q % ring, pl.ds(0, count)]
        dst = z_buf.at[q, pl.ds(0, count)]
        copy(src, dst, rzs.at[q], rzr.at[q], chip(pair, y)).wait_recv()
        total = t_buf[q % ring, z].astype(jnp.float32)
        for i in range(count):
            total = total + z_buf[q, i].astype(jnp.float32)
        return total

    def fold_z(q):
        def settle(total):
            def of_a():
                out_a[:, fine_columns(q)] = ROUTED_SCALE * total

            def of_b():
                lifted[:, fine_columns(q - fine)] = total

            if isinstance(q, int):
                of_a() if q < fine else of_b()
            else:
                pl.when(q < fine)(of_a)
                pl.when(q >= fine)(of_b)

        @pl.when(middle)
        def _():
            settle(take_z(q, planes - 1))

        @pl.when(jnp.logical_not(middle))
        def _():
            settle(take_z(q, planes - 2))

    lags = ((4, fold_y), (6, relay_z), (8, fold_z))

    def behind(q):
        for lag, stage in lags:
            if isinstance(q, int):
                if lag <= q < steps + lag:
                    stage(q - lag)
            else:
                pl.when(q >= lag)(functools.partial(stage, q - lag))

    def store(q, value):
        def clean():
            rs_y(q - ring).wait_send()

        pl.when(q >= ring)(clean)
        o_buf[q % ring] = value.reshape(slots, tok, rc).astype(o_buf.dtype)
        rs_y(q).start()

    def take_up(i):
        up_x(i).wait_recv()
        up_m(i, part).start()

    def load_wide(c):
        return Pieces(wd.at[:, wide_columns(c)], bd.at[c % depth_of], bds.at[c % depth_of])

    def own_back(c, carry):
        next_chunk(load_wide, c, depth // kc)
        lhs = chunk_of(2, wide_columns(c))
        for n in range(width // tile):
            cols = pl.ds(n * tile, tile)
            back[0, :, cols] += nt(lhs, bd[c % depth_of, cols, :])
        return carry

    def partner_back(c, carry):
        lhs = chunk_of(2, columns(c))
        for n in range(width // tile):
            cols = pl.ds(n * tile, tile)
            back[1, :, cols] += nt(lhs, wd_b[c, cols, :])
        return carry

    for k in range(2):
        for i in range(3):
            serve(k, i)
    serve(2, 0)
    serve(2, 1)
    own_g.wait()
    arrived(0)
    arrived(1)
    take_up(0)
    take_up(1)
    project(0, False, back.at[0])
    activate(0, back.at[0])
    serve(2, 2)

    def serve_last():
        serve(3, 0)
        serve(3, 1)

    pl.when(middle)(serve_last)
    for i in range(2, n_up):
        take_up(i)
    for i in range(n_up):
        up_m(i, 1 - part).wait_recv()
    project(0, True, back.at[1])
    activate(1, back.at[1])
    pl.when(jnp.logical_not(middle))(serve_last)
    marks = [chunks * i // 14 for i in (3, 5, 7, 9)]
    hold = marks[2]
    prime(load_down, 0, hold + 1)
    clear(back.at[0])
    clear(back.at[1])

    def take_down(c):
        down_x(c).wait_recv()
        down_m(c, part).start()

    take_down(0)
    take_down(1)
    def forward(c, carry):
        load_down(c).wait()
        ahead = c + depth_of - 1

        @pl.when(jnp.logical_and(ahead < chunks, jnp.logical_or(ahead <= hold, c > hold)))
        def _():
            load_down(ahead).start()

        down_m(c, 1 - part).wait_recv()
        for n in range(dc // rc):
            cols = pl.ds(n * rc, rc)
            value = nn(act[0], bd[c % depth_of, :, cols]) + nn(act[1], wd_b[c, :, cols])
            store(c * (dc // rc) + n, value)

        @pl.when(c == 0)
        def _():
            serve(3, 2)

        @pl.when(c == marks[0])
        def _():
            arrived(2)
            project(1, False, pre.at[0])
            prepare_b(0)

        @pl.when(c == marks[1])
        def _():
            project(1, True, pre.at[1])
            prepare_b(1)

        @pl.when(c == hold)
        def _():
            arrived(3)
            prime(load_wide, 0, depth // kc)
            lax.fori_loop(0, depth // kc, own_back, 0)
            prime(load_down, hold + 1, chunks)
            prime(load_fine, 0, fine)

        @pl.when(c == marks[3])
        def _():
            lax.fori_loop(0, marks[3] + 1, partner_back, 0)
            invert(0)

        @pl.when(c > marks[3])
        def _():
            partner_back(c, 0)

        @pl.when(c + 1 < chunks)
        def _():
            for n in range(dc // rc):
                behind(c * (dc // rc) + n)

        @pl.when(c + 3 < chunks)
        def _():
            take_down(c + 2)

        @pl.when(c + 2 == chunks)
        def _():
            take_down(c + 1)

        return carry

    lax.fori_loop(0, chunks, forward, 0)
    invert(1)

    def score_copy(i, slot):
        target = of_slot((slot_me + i) % slots)
        return copy(sc_own, sc_all.at[slot], scs.at[i - 1], scr.at[i - 1], target)

    def backward(c, carry):
        next_chunk(load_fine, c, fine)
        q = fine + c
        value = nt(inner[0], bu[c % depth_of, :rc, :]) + nt(inner[1], wu_b[fine_columns(c), :])
        store(q, value)
        behind(q - 1)

        @pl.when(c == 1)
        def _():
            sc_own[...] = sc_col[...].reshape(m_rows, lanes).T[:8]
            for i in range(1, slots):
                score_copy(i, slot_me).start()

        return carry

    lax.fori_loop(0, fine, backward, 0)

    sc_all[slot_me] = sc_own[...]
    for i in range(1, slots):
        score_copy(i, (slot_me - i + slots) % slots).wait_recv()
    table = tabs[...].reshape(m_rows, lanes).T
    lines = []
    for e in range(experts):
        plane, row, odd = e // PLANE, (e // 2) % 2, e % 2
        lines.append(sc_all[row * planes + plane, odd : odd + 1, :])
    score = jnp.concatenate(lines, axis=0)
    gate = ROUTED_SCALE * score
    mean = jnp.sum(gate * table[experts : 2 * experts], axis=0, keepdims=True)
    logit = table[2 * experts : 3 * experts] * (gate - mean)
    order = lax.broadcasted_iota(jnp.int32, (experts, m_rows), 0)
    one = jnp.sum(jnp.where(order == me, logit, 0.0), axis=0, keepdims=True)
    two = jnp.sum(jnp.where(order == x_near, logit, 0.0), axis=0, keepdims=True)
    both = jnp.concatenate([one, two, jnp.zeros((6, m_rows), jnp.float32)], axis=0)

    def thirds(v):
        high = v.astype(jnp.bfloat16)
        rest = v - high.astype(jnp.float32)
        medium = rest.astype(jnp.bfloat16)
        return (high, medium, (rest - medium.astype(jnp.float32)).astype(jnp.bfloat16))

    pieces = thirds(both)
    for c in range(depth // kc):
        cols = pl.ds(c * kc, kc)
        rhs = rows[1, :, :, cols].reshape(m_rows, kc)
        rg_buf[:, cols] = nn(pieces[0], rhs) + nn(pieces[1], rhs) + nn(pieces[2], rhs)

    def grad_copy(i):
        expert = me if i == 0 else x_near
        pipe = p if i == 1 else mirror
        return copy(rg_buf, rg_in.at[i], gs.at[i], gr.at[i], expert, pipe)

    for i in range(3):
        grad_copy(i).start()
    padded = jnp.concatenate([logit, jnp.zeros((lanes - experts, m_rows), jnp.float32)], axis=0)
    sc_col[...] = padded.T.reshape(slots, tok, lanes)
    for q in range(steps - 1, steps + 3):
        behind(q)
    dense = thirds(sc_col[slot_me])
    for q in range(steps + 3, steps + lags[-1][0]):
        behind(q)

    inv = rinv_b[:, 0:1]
    dots = jnp.zeros((tok, 1), jnp.float32)
    for c in range(depth // kc):
        cols = pl.ds(c * kc, kc)
        rhs = router_t[:, cols]
        extra = nn(dense[0], rhs) + nn(dense[1], rhs) + nn(dense[2], rhs)
        v = ROUTED_SCALE * lifted[:, cols] + extra
        lifted[:, cols] = v
        dots = dots + jnp.sum(v * hid_b[:, cols].astype(jnp.float32), axis=-1, keepdims=True)
    slope = inv * inv * inv * (dots / depth)
    for c in range(depth // kc):
        cols = pl.ds(c * kc, kc)
        hidden = hid_b[:, cols].astype(jnp.float32)
        out_b[:, cols] = inv * lifted[:, cols] - hidden * slope
    for i in range(3):
        grad_copy(i).wait_recv()
    rg_out[0:1, :] = rg_buf[0:1, :] + rg_in[0, 0:1, :]
    rg_out[1:2, :] = rg_in[1, 1:2, :] + rg_in[2, 1:2, :]

    for k in range(4):
        z_send(k, pair).wait_send()
        z_send(k, opposite).wait_send()

        if k == 0:
            z_send(k, other).wait_send()
        else:

            @pl.when(middle)
            def _():
                z_send(k, other).wait_send()
                z_relay(k).wait_send()

        y_send(k).wait_send()
        if k < 2:
            y_copy(k, pair, y).wait_send()
        else:
            cross(k, z).wait_send()
            y_half(k, y).wait_send()
        for source in (opposite, other):
            y_copy(k, source, y).wait_send()
    for i in range(n_up):
        up_x(i).wait_send()
        up_m(i, part).wait_send()

    def drain(c, carry):
        down_x(c).wait_send()
        down_m(c, part).wait_send()
        return carry

    lax.fori_loop(0, chunks, drain, 0)

    def drain_rs(q, carry):
        rs_y(q).wait_send()
        sent_z(q)
        return carry

    lax.fori_loop(steps - ring, steps, drain_rs, 0)
    for i in range(1, slots):
        score_copy(i, slot_me).wait_send()
    for i in range(3):
        grad_copy(i).wait_send()


N_UP = 4
RING = 8
AHEAD = 3


def fused_plan(n, tok, depth, width):
    planes = n // PLANE
    slots = 2 * planes
    m_rows = slots * tok
    kc = 512 if depth % 512 == 0 else 256
    dc = rc = 256
    chunks = depth // dc
    steps = 2 * (depth // rc)
    bf, f32 = jnp.bfloat16, jnp.float32
    buffers = [
        ((3, slots, tok, depth), bf),
        ((slots, tok, 128), f32),
        ((depth, width), bf),
        ((chunks, width, dc), bf),
        ((AHEAD, kc, width), bf),
        ((AHEAD, width, kc), bf),
        ((2, m_rows, width), bf),
        ((2, m_rows, width), f32),
        ((2, m_rows, width), f32),
        ((2, m_rows, width), bf),
        ((2, m_rows, width), bf),
        ((RING, slots, tok, rc), bf),
        ((steps, planes, tok, rc), bf),
        ((RING, planes, tok, rc), bf),
        ((steps, planes - 1, tok, rc), bf),
        ((steps, tok, rc), bf),
        ((slots, tok, 128), f32),
        ((8, m_rows), f32),
        ((slots, 8, m_rows), f32),
        ((8, depth), f32),
        ((3, 8, depth), f32),
        ((128, depth), bf),
        ((tok, 128), f32),
        ((tok, depth), f32),
    ]
    sems = (
        [(1,)]
        + [(4, planes + 1)] * 2
        + [(4, planes)] * 2
        + [(N_UP + chunks,)] * 4
        + [(AHEAD,)] * 2
        + [(steps,)] * 5
        + [(slots - 1,)] * 2
        + [(3,)] * 2
    )
    total = sum(math.prod(shape) * jnp.dtype(kind).itemsize for shape, kind in buffers)
    fits = total + 7 * tok * depth * 2 < 64_500_000 and 3 * n <= 128 and planes == 4
    return fits, (planes, tok, depth, width, kc, dc, rc, N_UP, RING), buffers, sems


def fused(plan, *args):
    _, dims, buffers, sems = plan
    tok, depth = dims[1:3]
    vmem = pl.BlockSpec(memory_space=pltpu.VMEM)
    hbm = pl.BlockSpec(memory_space=pl.ANY)
    return pl.pallas_call(
        functools.partial(fused_kernel, dims + (lax.axis_size("pipe"),)),
        out_shape=[
            jax.ShapeDtypeStruct((tok, depth), jnp.float32),
            jax.ShapeDtypeStruct((tok, depth), jnp.float32),
            jax.ShapeDtypeStruct((2, depth), jnp.float32),
        ],
        in_specs=[vmem] * 6 + [hbm] * 2,
        out_specs=[vmem] * 3,
        scratch_shapes=[pltpu.VMEM(shape, kind) for shape, kind in buffers]
        + [DMA(shape) for shape in sems],
        compiler_params=pltpu.CompilerParams(
            collective_id=7, has_side_effects=True, vmem_limit_bytes=67_000_000
        ),
    )(*args)


def on_device_fused(
    plan, hidden_a, routes_a, hidden_b, routes_b, grad_out_b, router, w_up, w_down
):
    mixed, delta, terms = fused(
        plan,
        hidden_a[0],
        hidden_b[0],
        grad_out_b[0],
        routes_a[0].T,
        routes_b[0].T,
        router[0],
        w_up[0, 0],
        w_down[0, 0],
    )
    layer_out = (hidden_a[0].astype(jnp.float32) + mixed).astype(jnp.bfloat16)
    grad_in = (grad_out_b[0].astype(jnp.float32) + delta).astype(jnp.bfloat16)
    return (layer_out[None], grad_in[None], jnp.sum(terms, axis=0)[None, None])


def solution(mesh):
    placed = (
        P("pipe", "expert", None),
        P("pipe", "expert", None),
        P("pipe", "expert", None),
        P("pipe", "expert", None),
        P("pipe", "expert", None),
        P("pipe", None, None),
        P("pipe", "expert", None, None),
        P("pipe", "expert", None, None),
    )

    def body(*args):
        w_up = args[6]
        plan = fused_plan(lax.axis_size("expert"), args[0].shape[1], w_up.shape[2], w_up.shape[3])
        if w_up.shape[1] == 1 and plan[0]:
            return on_device_fused(plan, *args)
        return on_device(*args)

    return jax.shard_map(
        body,
        mesh=mesh,
        in_specs=placed,
        out_specs=(P("pipe", "expert", None), P("pipe", "expert", None), P("pipe", "expert", None)),
        check_vma=False,
    )
```

```python
import functools
import math

import jax
import jax.numpy as jnp
from jax import lax
from jax.experimental import pallas as pl
from jax.experimental.pallas import tpu as pltpu
from jax.sharding import PartitionSpec as P

ROUTED_SCALE = 2.5
EPSILON = 1e-06


def partner(block, axis, bit):
    count = lax.axis_size(axis)
    route = []
    for low in range(count):
        high = low | 1 << bit
        if high != low and high < count:
            route += [(low, high), (high, low)]
    return lax.ppermute(block, axis, route)


MESH = pl.DeviceIdType.MESH
DMA = pltpu.SemaphoreType.DMA
PLANE = 4


def remote(src, dst, send_sem, recv_sem, target):
    return pltpu.make_async_remote_copy(
        src_ref=src,
        dst_ref=dst,
        send_sem=send_sem,
        recv_sem=recv_sem,
        device_id={"expert": target},
        device_id_type=MESH,
    )


def place():
    me = lax.axis_index("expert")
    z, y, x = me // PLANE, (me // 2) % 2, me % 2
    return (me, z, y, x, me + 1 - 2 * x, me + 2 - 4 * y)


def greet(planes):
    me, z, y, x, x_near, y_near = place()
    barrier = pltpu.get_barrier_semaphore()
    pl.semaphore_signal(barrier, inc=1, device_id={"expert": x_near}, device_id_type=MESH)
    pl.semaphore_signal(barrier, inc=1, device_id={"expert": y_near}, device_id_type=MESH)

    @pl.when(z < planes - 1)
    def _():
        pl.semaphore_signal(barrier, inc=1, device_id={"expert": me + PLANE}, device_id_type=MESH)

    @pl.when(z > 0)
    def _():
        pl.semaphore_signal(barrier, inc=1, device_id={"expert": me - PLANE}, device_id_type=MESH)

    ends = jnp.where(z == 0, 1, 0) + jnp.where(z == planes - 1, 1, 0)
    pl.semaphore_wait(barrier, 4 - ends)


def gather_kernel(count, planes, *refs):
    ins, outs = refs[:count], refs[count : 2 * count]
    own_sem, up_s, down_s, z_r, x_s, x_r, y_s, y_r, d_s, d_r = refs[2 * count :]
    me, z, y, x, x_near, y_near = place()

    def up(k, p, src):
        return remote(src, outs[k].at[p * PLANE + y * 2 + x], up_s.at[k, p], z_r.at[k, p], me + PLANE)

    def down(k, p, src):
        return remote(src, outs[k].at[p * PLANE + y * 2 + x], down_s.at[k, p], z_r.at[k, p], me - PLANE)

    def to_x(k, p, src):
        return remote(src, outs[k].at[p * PLANE + y * 2 + x], x_s.at[k, p], x_r.at[k, p], x_near)

    def to_y(k, p, src):
        return remote(src, outs[k].at[p * PLANE + y * 2 + x], y_s.at[k, p], y_r.at[k, p], y_near)

    def half(k, p, way):
        if way == 0:
            ref = outs[k].at[p * PLANE + y * 2 + 1 - x, 0]
            return remote(ref, ref, d_s.at[k, p, 0], d_r.at[k, p, 0], y_near)
        ref = outs[k].at[p * PLANE + (1 - y) * 2 + x, 1]
        return remote(ref, ref, d_s.at[k, p, 1], d_r.at[k, p, 1], x_near)

    def each(d, act):
        if d == 0:
            act(z, 0)
            return

        @pl.when(z >= d)
        def _():
            act(z - d, 1)

        @pl.when(z + d < planes)
        def _():
            act(z + d, -1)

    def spread(k, p, way, wait):
        src = ins[k] if way == 0 else outs[k].at[p * PLANE + y * 2 + x]

        def do(copy):
            copy.wait_send() if wait else copy.start()

        if way != 0 and not wait:
            up(k, p, src).wait_recv()
        if way >= 0:

            @pl.when(z < planes - 1)
            def _():
                do(up(k, p, src))

        if way <= 0:

            @pl.when(z > 0)
            def _():
                do(down(k, p, src))

        do(to_x(k, p, src))
        do(to_y(k, p, src))

    def relay(k, p, way):
        to_x(k, p, ins[k]).wait_recv()
        half(k, p, 0).start()
        to_y(k, p, ins[k]).wait_recv()
        half(k, p, 1).start()

    def finish(k, p, way):
        for route in range(2):
            half(k, p, route).wait()
        spread(k, p, way, True)

    greet(planes)
    for k in range(count):
        pltpu.make_async_copy(ins[k], outs[k].at[me], own_sem.at[k]).start()
        each(0, lambda p, way: spread(k, p, way, False))
    for k in range(count):
        for d in range(1, planes):
            each(d, lambda p, way: spread(k, p, way, False))
            each(d - 1, lambda p, way: relay(k, p, way))
        each(planes - 1, lambda p, way: relay(k, p, way))
    for k in range(count):
        for d in range(planes):
            each(d, lambda p, way: finish(k, p, way))
        pltpu.make_async_copy(ins[k], outs[k].at[me], own_sem.at[k]).wait()


def gather_all(blocks, collective_id):
    n = lax.axis_size("expert")
    planes = n // PLANE
    count = len(blocks)
    halved = [b.reshape(2, b.shape[0] // 2, b.shape[1]) for b in blocks]
    outs = pl.pallas_call(
        functools.partial(gather_kernel, count, planes),
        out_shape=[jax.ShapeDtypeStruct((n,) + b.shape, b.dtype) for b in halved],
        in_specs=[pl.BlockSpec(memory_space=pltpu.VMEM)] * count,
        out_specs=[pl.BlockSpec(memory_space=pl.ANY)] * count,
        scratch_shapes=[DMA((count,))] + [DMA((count, planes))] * 7 + [DMA((count, planes, 2))] * 2,
        compiler_params=pltpu.CompilerParams(collective_id=collective_id, has_side_effects=True),
    )(*halved)
    return [o.reshape(n * b.shape[0], b.shape[1]) for o, b in zip(outs, blocks)]


def scatter_stages(planes, part, out, a_r, c_r, b_x, b_y, total, z_r, *sems):
    ax_s, ax_r, ay_s, ay_r, cx_s, cx_r, cy_s, cy_r, z_s, up_r, down_r = sems
    me, z, y, x, x_near, y_near = place()
    rows, cols = part.shape[2:]
    step = 16

    def slot(p, yy, xx):
        return p * PLANE + yy * 2 + xx

    def add(dst, *srcs):
        def body(i, carry):
            r = pl.ds(pl.multiple_of(i * step, step), step)
            acc = srcs[0][r, :].astype(jnp.float32)
            for s in srcs[1:]:
                acc = acc + s[r, :].astype(jnp.float32)
            dst[r, :] = acc.astype(dst.dtype)
            return carry

        lax.fori_loop(0, rows // step, body, 0)

    def diagonal(p):
        src = slot(p, 1 - y, 1 - x)
        return (
            remote(part.at[src, 0], a_r.at[p, 0], ay_s.at[p], ay_r.at[p], y_near),
            remote(part.at[src, 1], a_r.at[p, 1], ax_s.at[p], ax_r.at[p], x_near),
        )

    def beside(p):
        return (
            remote(b_x.at[p, 0], c_r.at[p, 0, 0], cx_s.at[p, 0], cx_r.at[p, 0], x_near),
            remote(part.at[slot(p, y, 1 - x), 1], c_r.at[p, 0, 1], cx_s.at[p, 1], cx_r.at[p, 1], x_near),
            remote(b_y.at[p, 0], c_r.at[p, 1, 1], cy_s.at[p, 0], cy_r.at[p, 0], y_near),
            remote(part.at[slot(p, 1 - y, x), 0], c_r.at[p, 1, 0], cy_s.at[p, 1], cy_r.at[p, 1], y_near),
        )

    def rise(p):
        return remote(total.at[p], z_r.at[0, p], z_s.at[p], up_r.at[p], me + PLANE)

    def sink(p):
        return remote(total.at[p], z_r.at[1, p], z_s.at[p], down_r.at[p], me - PLANE)

    def first(p, way):
        for copy in diagonal(p):
            copy.start()
        beside(p)[1].start()
        beside(p)[3].start()

    def second(p, way):
        to_y, to_x = diagonal(p)
        to_y.wait_recv()
        add(b_x.at[p, 0], part.at[slot(p, y, 1 - x), 0], a_r.at[p, 0])
        beside(p)[0].start()
        to_x.wait_recv()
        add(b_y.at[p, 0], part.at[slot(p, 1 - y, x), 1], a_r.at[p, 1])
        beside(p)[2].start()

    def third(p, way):
        for copy in beside(p):
            copy.wait_recv()
        for h in range(2):
            add(total.at[p, h], part.at[slot(p, y, x), h], c_r.at[p, 0, h], c_r.at[p, 1, h])

        def take(copy, level):
            copy.wait_recv()
            for h in range(2):
                add(total.at[p, h], total.at[p, h], z_r.at[level, p, h])

        if way >= 0:

            @pl.when(z > 0)
            def _():
                take(rise(p), 0)

        if way <= 0:

            @pl.when(z < planes - 1)
            def _():
                take(sink(p), 1)

        if way > 0:
            rise(p).start()
        if way < 0:
            sink(p).start()
        if way == 0:
            out[...] = total[p]

    def finish(p, way):
        for copy in diagonal(p) + beside(p):
            copy.wait_send()
        if way != 0:
            rise(p).wait_send()

    return (first, second, third, finish)


def scatter_kernel(planes, count, *refs):
    parts, outs, rest = refs[:count], refs[count : 2 * count], refs[2 * count :]
    per = len(rest) // count
    z = place()[1]
    stages = [
        scatter_stages(planes, parts[k], outs[k], *rest[k * per : (k + 1) * per])
        for k in range(count)
    ]

    def each(d, act):
        if d == 0:
            act(z, 0)
            return

        @pl.when(z >= d)
        def _():
            act(z - d, -1)

        @pl.when(z + d < planes)
        def _():
            act(z + d, 1)

    greet(planes)
    order = list(range(planes - 1, -1, -1))
    for k in range(count):
        for d in order:
            each(d, stages[k][0])
    for i, d in enumerate(order):
        for k in range(count):
            each(d, stages[k][1])
        if i > 0:
            for k in range(count):
                each(order[i - 1], stages[k][2])
    for k in range(count):
        each(0, stages[k][2])
    for k in range(count):
        for d in order:
            each(d, stages[k][3])


def scatter_sums(parts, collective_id):
    n = lax.axis_size("expert")
    planes = n // PLANE
    tokens, cols = parts[0].shape
    rows = tokens // n // 2
    half = (rows, cols)
    kind = parts[0].dtype
    count = len(parts)
    if count > 1 and count * 3 * parts[0].size * kind.itemsize > 56 << 20:
        return [scatter_sums([part], collective_id + k)[0] for k, part in enumerate(parts)]
    outs = pl.pallas_call(
        functools.partial(scatter_kernel, planes, count),
        out_shape=[jax.ShapeDtypeStruct((2,) + half, kind)] * count,
        in_specs=[pl.BlockSpec(memory_space=pltpu.VMEM)] * count,
        out_specs=[pl.BlockSpec(memory_space=pltpu.VMEM)] * count,
        scratch_shapes=(
            [
                pltpu.VMEM((planes, 2) + half, kind),
                pltpu.VMEM((planes, 2, 2) + half, kind),
                pltpu.VMEM((planes, 1) + half, kind),
                pltpu.VMEM((planes, 1) + half, kind),
                pltpu.VMEM((planes, 2) + half, kind),
                pltpu.VMEM((2, planes, 2) + half, kind),
            ]
            + [DMA((planes,))] * 4
            + [DMA((planes, 2))] * 4
            + [DMA((planes,))] * 3
        )
        * count,
        compiler_params=pltpu.CompilerParams(
            collective_id=collective_id, has_side_effects=True, vmem_limit_bytes=60 << 20
        ),
    )(*[part.reshape((n, 2) + half) for part in parts])
    return [out.reshape(2 * rows, cols) for out in outs]


def prepare(hidden, routes, router_segment):
    expert_count = router_segment.shape[0]
    hidden32 = hidden.astype(jnp.float32)
    rinv = lax.rsqrt(jnp.mean(hidden32 * hidden32, axis=-1, keepdims=True) + EPSILON)
    normed = (hidden32 * rinv).astype(jnp.bfloat16)
    logits = jnp.einsum("td,ed->te", normed, router_segment, preferred_element_type=jnp.float32)
    chosen = jnp.any(
        routes[:, :, None] == jnp.arange(expert_count, dtype=jnp.int32)[None, None, :], axis=1
    )
    affinity = jnp.where(chosen, jax.nn.sigmoid(logits), 0.0)
    return (hidden32, rinv, normed, affinity)


def on_device(hidden_a, routes_a, hidden_b, routes_b, grad_out_b, router, w_up, w_down):
    n_expert = lax.axis_size("expert")
    me = lax.axis_index("expert")
    tok_count = hidden_a.shape[1]
    router_segment = router[0]
    expert_count = router_segment.shape[0]
    local_count = w_up.shape[1]
    hidden32_a, rinv_a, normed_a, affinity_a = prepare(hidden_a[0], routes_a[0], router_segment)
    hidden32_b, rinv_b, normed_b, affinity_b = prepare(hidden_b[0], routes_b[0], router_segment)
    grad_out = grad_out_b[0]
    affinity_ab = jnp.concatenate([affinity_a, affinity_b], axis=1)
    lanes = -(-2 * expert_count // 128) * 128
    affinity_ab = jnp.pad(affinity_ab, ((0, 0), (0, lanes - 2 * expert_count)))
    rows_a, rows_b, rows_g, affinities = gather_all([normed_a, normed_b, grad_out, affinity_ab], 1)
    aff_a, aff_b = affinities[:, :expert_count], affinities[:, expert_count : 2 * expert_count]
    total_b = jnp.sum(aff_b, axis=1, keepdims=True)
    weight_a = aff_a / jnp.sum(aff_a, axis=1, keepdims=True)
    weight_b = aff_b / total_b

    def column(table, local):
        return lax.dynamic_slice_in_dim(table, me * local_count + local, 1, axis=1)

    sum_a = 0.0
    sum_b = 0.0
    scores = []
    for local in range(local_count):
        up, down = w_up[0, local], w_down[0, local]
        pre = jnp.dot(rows_a, up, preferred_element_type=jnp.float32)
        active = jax.nn.silu(pre).astype(jnp.bfloat16)
        out = jnp.dot(active, down, preferred_element_type=jnp.float32)
        sum_a = sum_a + out * column(weight_a, local)
    for local in range(local_count):
        up, down = w_up[0, local], w_down[0, local]
        pre = jnp.dot(rows_b, up, preferred_element_type=jnp.float32)
        back = jnp.einsum("td,fd->tf", rows_g, down, preferred_element_type=jnp.float32)
        sig = jax.nn.sigmoid(pre)
        scores.append(jnp.sum(back * (pre * sig), axis=-1))
        inner = (back * (sig * (1.0 + pre * (1.0 - sig)))).astype(jnp.bfloat16)
        lifted = jnp.einsum("tf,df->td", inner, up, preferred_element_type=jnp.float32)
        sum_b = sum_b + lifted * column(weight_b, local)
    sum_ab = scatter_sums([sum_a.astype(jnp.bfloat16), sum_b.astype(jnp.bfloat16)], 2)
    mixed = sum_ab[0].astype(jnp.float32)
    layer_out = (hidden32_a + ROUTED_SCALE * mixed).astype(jnp.bfloat16)

    flat = jnp.stack(scores).reshape(-1)
    padded = jnp.pad(flat, (0, -flat.shape[0] % 2048)).reshape(-1, 128)
    score = gather_all([padded], 4)[0].reshape(n_expert, -1)[:, : flat.shape[0]]
    score = score.reshape(expert_count, -1).T
    score = jnp.where(aff_b > 0.0, score, 0.0)
    gate_grad = ROUTED_SCALE * score
    logit_grad = (
        aff_b
        * (1.0 - aff_b)
        * (gate_grad - jnp.sum(gate_grad * weight_b, axis=1, keepdims=True))
        / total_b
    )
    own_columns = lax.dynamic_slice_in_dim(logit_grad, me * local_count, local_count, axis=1)
    own_term = jnp.dot(
        own_columns.T, rows_b.astype(jnp.float32), precision=lax.Precision.HIGHEST
    )
    mirrored = own_term
    for bit in range(lax.axis_size("pipe").bit_length() - 1):
        mirrored = partner(mirrored, "pipe", bit)
    router_grad = own_term + mirrored

    dense = lax.dynamic_slice_in_dim(logit_grad, me * tok_count, tok_count, axis=0)
    lifted_sum = sum_ab[1].astype(jnp.float32)
    normed_grad = ROUTED_SCALE * lifted_sum + jnp.dot(
        dense, router_segment.astype(jnp.float32), precision=lax.Precision.HIGHEST
    )
    mean_term = jnp.mean(normed_grad * hidden32_b, axis=-1, keepdims=True)
    grad_in = (
        grad_out.astype(jnp.float32) + rinv_b * normed_grad - hidden32_b * rinv_b**3 * mean_term
    )
    return (layer_out[None], grad_in.astype(jnp.bfloat16)[None], router_grad[None])


def fused_kernel(dims, *refs):
    planes, tok, depth, width, kc, dc, rc, n_up, ring, n_pipe = dims
    (hid_a, hid_b, g, routes_a, routes_b, router, wu, wd, out_a, out_b, rg_out) = refs[:11]
    (rows, tabs, wu_b, wd_b, bu, bd, act, pre, back, silu, inner) = refs[11:22]
    (o_buf, y_buf, t_buf, z_buf, f_buf, sc_col, sc_own, sc_all, rg_buf, rg_in) = refs[22:32]
    (router_t, rinv_b, mixed, extra, dots, lifted) = refs[32:38]
    (own_s, zs, zr, ys, yr, xs, xr, ms, mr, bus, bds) = refs[38:49]
    (rys, ryr, rzs, rzr, rfs, scs, scr, gs, gr) = refs[49:58]
    slots = 2 * planes
    experts = 2 * slots
    m_rows = slots * tok
    chunks = depth // dc
    half_d = depth // 2
    half_f = width // 2
    half_t = tok // 2
    up_rows = half_d // n_up
    tile = 256
    lanes = tabs.shape[-1]
    me, z, y, x, x_near, y_near = place()
    p = lax.axis_index("pipe")
    mirror = n_pipe - 1 - p
    part = (2 * p) // n_pipe
    slot_me = y * planes + z
    pair = z + 1 - 2 * (z % 2)
    opposite = (z + 2) % planes
    other = (pair + 2) % planes
    middle = (z + 1) // 2 == 1

    def copy(src, dst, send, recv, expert, pipe=p):
        return pltpu.make_async_remote_copy(
            src_ref=src,
            dst_ref=dst,
            send_sem=send,
            recv_sem=recv,
            device_id={"pipe": pipe, "expert": expert},
            device_id_type=MESH,
        )

    def chip(plane, row):
        return plane * PLANE + row * 2 + x

    def of_slot(s):
        return chip(s % planes, s // planes)

    barrier = pltpu.get_barrier_semaphore()

    def hello(pipe, expert):
        pl.semaphore_signal(
            barrier, inc=1, device_id={"pipe": pipe, "expert": expert}, device_id_type=MESH
        )

    for i in range(1, slots):
        hello(p, of_slot((slot_me + i) % slots))
    hello(p, x_near)
    hello(mirror, me)
    hello(mirror, x_near)

    own_g = pltpu.make_async_copy(g, rows.at[2, slot_me], own_s.at[0])
    own_g.start()

    pl.semaphore_wait(barrier, slots - 1 + 3)

    def up_region(which, i):
        return pl.ds(pl.multiple_of(which * half_d + i * up_rows, up_rows), up_rows)

    def up_x(i):
        r = up_region(part, i)
        return copy(wu.at[r], wu_b.at[r], xs.at[i], xr.at[i], x_near)

    def up_m(i, which):
        r = up_region(which, i)
        return copy(wu_b.at[r], wu_b.at[r], ms.at[i], mr.at[i], me, mirror)

    def down_rows(which):
        return pl.ds(pl.multiple_of(which * half_f, half_f), half_f)

    def columns(c):
        return pl.ds(pl.multiple_of(c * dc, dc), dc)

    def wide_columns(c):
        return pl.ds(pl.multiple_of(c * kc, kc), kc)

    def fine_columns(c):
        return pl.ds(pl.multiple_of(c * rc, rc), rc)

    def down_x(c):
        r = down_rows(part)
        src = wd.at[r, columns(c)]
        return copy(src, wd_b.at[c, r], xs.at[n_up + c], xr.at[n_up + c], x_near)

    def down_m(c, which):
        ref = wd_b.at[c, down_rows(which)]
        return copy(ref, ref, ms.at[n_up + c], mr.at[n_up + c], me, mirror)

    for i in range(n_up):
        up_x(i).start()
    for c in range(chunks):
        down_x(c).start()

    bufs = [tabs, rows.at[0], rows.at[1], rows.at[2]]

    def block(k, row, source):
        return bufs[k].at[row * planes + source]

    def mine(k):
        return g if k == 3 else bufs[k].at[slot_me]

    def z_send(k, target):
        dst = bufs[k].at[slot_me]
        return copy(mine(k), dst, zs.at[k, target], zr.at[k, z], chip(target, y))

    def z_take(k, source):
        ref = block(k, y, source)
        return copy(ref, ref, zs.at[k, source], zr.at[k, source], chip(source, y))

    def z_relay(k):
        ref = block(k, y, opposite)
        return copy(ref, ref, zs.at[k, z], zr.at[k, opposite], chip(pair, y))

    def late(ref):
        return ref.at[pl.ds(half_t, half_t)]

    def early(ref):
        return ref.at[pl.ds(0, half_t)]

    def cross(k, source):
        ref = late(block(k, 1 - y, source))
        return copy(ref, ref, zs.at[k, planes], zr.at[k, planes], chip(pair, y))

    def y_send(k):
        return copy(mine(k), bufs[k].at[slot_me], ys.at[k, z], yr.at[k, z], y_near)

    def y_copy(k, source, row):
        ref = block(k, row, source)
        return copy(ref, ref, ys.at[k, source], yr.at[k, source], y_near)

    def y_half(k, row):
        ref = early(block(k, row, pair))
        return copy(ref, ref, ys.at[k, pair], yr.at[k, pair], y_near)

    def spread(k):
        if k < 3:
            y_send(k).start()

        @pl.when(middle)
        def _():
            if k < 2:
                z_send(k, pair).start()
            z_send(k, other).start()

        @pl.when(jnp.logical_not(middle))
        def _():
            z_send(k, pair).start()
            if k == 0:
                z_send(k, other).start()

        z_send(k, opposite).start()

    def serve(k, i):
        if i == 0:
            z_take(k, pair).wait_recv()
            if k < 2:
                y_copy(k, pair, y).start()
            else:
                y_half(k, y).start()
                y_copy(k, z, 1 - y).wait_recv()
                cross(k, z).start()
        if i == 1:
            z_take(k, opposite).wait_recv()

            @pl.when(middle)
            def _():
                if k > 0:
                    z_relay(k).start()
                if 0 < k < 3:
                    z_send(k + 1, pair).start()

            y_copy(k, opposite, y).start()
        if i == 2:
            z_take(k, other).wait_recv()
            y_copy(k, other, y).start()

    def arrived(k):
        if k < 2:
            y_copy(k, z, 1 - y).wait_recv()
            y_copy(k, pair, 1 - y).wait_recv()
        else:
            y_half(k, 1 - y).wait_recv()
            cross(k, pair).wait_recv()
        y_copy(k, opposite, 1 - y).wait_recv()
        y_copy(k, other, 1 - y).wait_recv()

    y_send(3).start()

    def nn(lhs, rhs):
        return jnp.dot(lhs, rhs, preferred_element_type=jnp.float32)

    def nt(lhs, rhs):
        return lax.dot_general(
            lhs, rhs, (((1,), (1,)), ((), ())), preferred_element_type=jnp.float32
        )

    def normalize(k, src):
        step = 16

        def body(i, carry):
            r = pl.ds(pl.multiple_of(i * step, step), step)
            h = src[r, :].astype(jnp.float32)
            rinv = lax.rsqrt(jnp.mean(h * h, axis=-1, keepdims=True) + EPSILON)
            rows[k, slot_me, r, :] = (h * rinv).astype(rows.dtype)
            if k == 1:
                rinv_b[r, :] = jnp.broadcast_to(rinv, (step, lanes))
            return carry

        lax.fori_loop(0, tok // step, body, 0)

    normalize(0, hid_a)
    normalize(1, hid_b)
    for i in range(3):
        router_t[i * experts : (i + 1) * experts] = router[...]
    router_t[3 * experts :] = jnp.zeros((lanes - 3 * experts, depth), router_t.dtype)
    lane = lax.broadcasted_iota(jnp.int32, (tok, lanes), 1)
    expert_lane = lax.rem(lane, experts)

    def affinity(k, routes, section):
        logits = nt(rows[k, slot_me], router_t[...])
        named = routes[...].T
        chosen = expert_lane == named[:, 0:1]
        for i in range(1, named.shape[1]):
            chosen = jnp.logical_or(chosen, expert_lane == named[:, i : i + 1])
        sig = jnp.where(chosen, jax.nn.sigmoid(logits), 0.0)
        here = jnp.where(lax.div(lane, experts) == section, sig, 0.0)
        return sig, here, jnp.sum(here, axis=-1, keepdims=True)

    _, here_a, total_a = affinity(0, routes_a, 0)
    sig_b, here_b, total_b = affinity(1, routes_b, 1)
    slope_b = jnp.where(lax.div(lane, experts) == 2, sig_b * (1.0 - sig_b), 0.0)
    tabs[slot_me] = here_a / total_a + here_b / total_b + slope_b / total_b

    for k in range(4):
        spread(k)

    def chunk_of(k, cols):
        return rows[k, :, :, cols].reshape(m_rows, cols.size)

    class Pieces:
        def __init__(self, src, dst, sem):
            self.whole = pltpu.make_async_copy(src, dst, sem)
            count = 4
            step = dst.shape[0] // count
            self.parts = [
                pltpu.make_async_copy(src.at[r], dst.at[r], sem)
                for r in (pl.ds(i * step, step) for i in range(count))
            ]

        def start(self):
            for part_copy in self.parts:
                part_copy.start()

        def wait(self):
            self.whole.wait()

    depth_of = bu.shape[0]

    def load_up(c):
        return Pieces(wu.at[wide_columns(c)], bu.at[c % depth_of], bus.at[c % depth_of])

    def load_fine(c):
        return Pieces(wu.at[fine_columns(c)], bu.at[c % depth_of, pl.ds(0, rc)], bus.at[c % depth_of])

    def load_down(c):
        dst = bd.at[c % depth_of, :, pl.ds(0, dc)]
        return Pieces(wd.at[:, columns(c)], dst, bds.at[c % depth_of])

    def prime(load, lo, hi):
        for c in range(lo, min(hi, lo + depth_of - 1)):
            load(c).start()

    def next_chunk(load, c, count=chunks):
        load(c).wait()

        @pl.when(c + depth_of - 1 < count)
        def _():
            load(c + depth_of - 1).start()

    def block_rows(s):
        return pl.ds(pl.multiple_of(s * tok, tok), tok)

    def clear(dst):
        def body(s, carry):
            dst[block_rows(s), :] = jnp.zeros((tok, width), jnp.float32)
            return carry

        lax.fori_loop(0, slots, body, 0)

    def project(k, partner, dst):
        clear(dst)
        count = depth // kc
        if not partner:
            prime(load_up, 0, count)

        def body(c, carry):
            if not partner:
                next_chunk(load_up, c, count)
            lhs = chunk_of(k, wide_columns(c))
            for n in range(width // tile):
                cols = pl.ds(n * tile, tile)
                rhs = wu_b[wide_columns(c), cols] if partner else bu[c % depth_of, :, cols]
                dst[:, cols] += nn(lhs, rhs)
            return carry

        lax.fori_loop(0, count, body, 0)

    def pick(s, column):
        return jnp.sum(jnp.where(lane == column, tabs[s], 0.0), axis=-1, keepdims=True)

    expert_of = [me, x_near]

    def activate(which, src):
        def body(s, carry):
            v = src[block_rows(s), :]
            weight = pick(s, expert_of[which])
            act[which, block_rows(s), :] = (v * jax.nn.sigmoid(v) * weight).astype(act.dtype)
            return carry

        lax.fori_loop(0, slots, body, 0)

    def prepare_b(which):
        def body(s, carry):
            r = block_rows(s)
            v = pre[which, r, :]
            sig = jax.nn.sigmoid(v)
            silu[which, r, :] = (v * sig).astype(silu.dtype)
            weight = pick(s, experts + expert_of[which])
            pre[which, r, :] = sig * (1.0 + v * (1.0 - sig)) * weight
            return carry

        lax.fori_loop(0, slots, body, 0)

    def invert(which):
        def body(s, carry):
            r = block_rows(s)
            bk = back[which, r, :]
            score = jnp.sum(bk * silu[which, r, :].astype(jnp.float32), axis=-1, keepdims=True)
            inner[which, r, :] = (bk * pre[which, r, :]).astype(inner.dtype)
            at = x if which == 0 else 1 - x
            held = 0.0 if which == 0 else sc_col[s]
            sc_col[s] = jnp.where(lane == at, score, held)
            return carry

        lax.fori_loop(0, slots, body, 0)

    fine = depth // rc
    steps = 2 * fine

    def rs_y(q):
        src = o_buf.at[q % ring, pl.ds((1 - y) * planes, planes)]
        return copy(src, y_buf.at[q], rys.at[q], ryr.at[q], y_near)

    def rs_z(q, target, place_at):
        src = t_buf.at[q % ring, target]
        return copy(src, z_buf.at[q, place_at], rzs.at[q], rzr.at[q], chip(target, y))

    def rs_far(q):
        src = t_buf.at[q % ring, other]
        return copy(src, f_buf.at[q], rzs.at[q], rfs.at[q], chip(pair, y))

    def direct(q):
        return isinstance(q, int) and q >= steps - 1

    def sent_z(q):
        src = t_buf.at[q % ring, pl.ds(0, planes - 1)]
        dst = z_buf.at[q, pl.ds(0, planes - 1)]
        copy(src, dst, rzs.at[q], rzr.at[q], chip(pair, y)).wait_send()

    def fold_y(q):
        rs_y(q).wait_recv()

        def clean():
            sent_z(q - ring)

        if isinstance(q, int):
            if q >= ring:
                clean()
        else:
            pl.when(q >= ring)(clean)
        for k in range(planes):
            first = o_buf[q % ring, y * planes + k].astype(jnp.float32)
            t_buf[q % ring, k] = (first + y_buf[q, k].astype(jnp.float32)).astype(t_buf.dtype)
        if direct(q):
            pl.when(middle)(lambda: rs_z(q, opposite, 1).start())
            rs_z(q, other, 2).start()
            pl.when(jnp.logical_not(middle))(lambda: rs_z(q, opposite, 1).start())
            rs_z(q, pair, 0).start()
            return

        @pl.when(middle)
        def _():
            rs_z(q, other, 2).start()

        @pl.when(jnp.logical_not(middle))
        def _():
            rs_far(q).start()
            rs_z(q, opposite, 1).start()

        rs_z(q, pair, 0).start()

    def relay_z(q):
        if direct(q):
            return

        @pl.when(middle)
        def _():
            rs_far(q).wait_recv()
            total = t_buf[q % ring, opposite].astype(jnp.float32) + f_buf[q].astype(jnp.float32)
            t_buf[q % ring, opposite] = total.astype(t_buf.dtype)
            rs_z(q, opposite, 1).start()

    def take_z(q, count):
        src = t_buf.at[q % ring, pl.ds(0, count)]
        dst = z_buf.at[q, pl.ds(0, count)]
        copy(src, dst, rzs.at[q], rzr.at[q], chip(pair, y)).wait_recv()
        total = t_buf[q % ring, z].astype(jnp.float32)
        for i in range(count):
            total = total + z_buf[q, i].astype(jnp.float32)
        return total

    def finish_b(c, total):
        cols = fine_columns(c)
        v = ROUTED_SCALE * total + extra[:, cols]
        lifted[:, cols] = v
        prod = v * hid_b[:, cols].astype(jnp.float32)
        for i in range(rc // lanes):
            dots[...] += prod[:, i * lanes : (i + 1) * lanes]

    def fold_z(q):
        def settle(total):
            def of_a():
                mixed[:, fine_columns(q)] = (ROUTED_SCALE * total).astype(mixed.dtype)

            def of_b():
                lifted[:, fine_columns(q - fine)] = total

            if isinstance(q, int):
                finish_b(q - fine, total)
            else:
                pl.when(q < fine)(of_a)
                pl.when(q >= fine)(of_b)

        if direct(q):
            settle(take_z(q, planes - 1))
            return

        @pl.when(middle)
        def _():
            settle(take_z(q, planes - 1))

        @pl.when(jnp.logical_not(middle))
        def _():
            settle(take_z(q, planes - 2))

    lags = ((4, fold_y), (6, relay_z), (8, fold_z))

    def behind(q):
        for lag, stage in lags:
            if isinstance(q, int):
                if lag <= q < steps + lag:
                    stage(q - lag)
            else:
                pl.when(q >= lag)(functools.partial(stage, q - lag))

    def store(q, value):
        def clean():
            rs_y(q - ring).wait_send()

        pl.when(q >= ring)(clean)
        o_buf[q % ring] = value.reshape(slots, tok, rc).astype(o_buf.dtype)
        rs_y(q).start()

    def take_up(i):
        up_x(i).wait_recv()
        up_m(i, part).start()

    def load_wide(c):
        return Pieces(wd.at[:, wide_columns(c)], bd.at[c % depth_of], bds.at[c % depth_of])

    def own_back(c, carry):
        next_chunk(load_wide, c, depth // kc)
        lhs = chunk_of(2, wide_columns(c))
        for n in range(width // tile):
            cols = pl.ds(n * tile, tile)
            back[0, :, cols] += nt(lhs, bd[c % depth_of, cols, :])
        return carry

    def partner_back(c, carry):
        lhs = chunk_of(2, columns(c))
        for n in range(width // tile):
            cols = pl.ds(n * tile, tile)
            back[1, :, cols] += nt(lhs, wd_b[c, cols, :])
        return carry

    for k in range(2):
        for i in range(3):
            serve(k, i)
    serve(2, 0)
    serve(2, 1)
    own_g.wait()
    arrived(0)
    arrived(1)
    take_up(0)
    take_up(1)
    project(0, False, back.at[0])
    activate(0, back.at[0])
    serve(2, 2)

    def serve_last():
        serve(3, 0)
        serve(3, 1)

    pl.when(middle)(serve_last)
    for i in range(2, n_up):
        take_up(i)
    for i in range(n_up):
        up_m(i, 1 - part).wait_recv()
    project(0, True, back.at[1])
    activate(1, back.at[1])
    pl.when(jnp.logical_not(middle))(serve_last)
    marks = [chunks * i // 14 for i in (3, 5, 7, 9)]
    hold = marks[2]
    prime(load_down, 0, hold + 1)
    clear(back.at[0])
    clear(back.at[1])

    def take_down(c):
        down_x(c).wait_recv()
        down_m(c, part).start()

    take_down(0)
    take_down(1)
    def forward(c, carry):
        load_down(c).wait()
        ahead = c + depth_of - 1

        @pl.when(jnp.logical_and(ahead < chunks, jnp.logical_or(ahead <= hold, c > hold)))
        def _():
            load_down(ahead).start()

        down_m(c, 1 - part).wait_recv()
        for n in range(dc // rc):
            cols = pl.ds(n * rc, rc)
            value = nn(act[0], bd[c % depth_of, :, cols]) + nn(act[1], wd_b[c, :, cols])
            store(c * (dc // rc) + n, value)

        @pl.when(c == 0)
        def _():
            serve(3, 2)

        @pl.when(c == marks[0])
        def _():
            arrived(2)
            project(1, False, pre.at[0])
            prepare_b(0)

        @pl.when(c == marks[1])
        def _():
            project(1, True, pre.at[1])
            prepare_b(1)

        @pl.when(c == hold)
        def _():
            arrived(3)
            prime(load_wide, 0, depth // kc)
            lax.fori_loop(0, depth // kc, own_back, 0)
            prime(load_down, hold + 1, chunks)
            prime(load_fine, 0, fine)

        @pl.when(c == marks[3])
        def _():
            lax.fori_loop(0, marks[3] + 1, partner_back, 0)
            invert(0)

        @pl.when(c > marks[3])
        def _():
            partner_back(c, 0)

        @pl.when(c + 1 < chunks)
        def _():
            for n in range(dc // rc):
                behind(c * (dc // rc) + n)

        @pl.when(c + 3 < chunks)
        def _():
            take_down(c + 2)

        @pl.when(c + 2 == chunks)
        def _():
            take_down(c + 1)

        return carry

    lax.fori_loop(0, chunks, forward, 0)
    invert(1)

    def score_copy(i, slot):
        target = of_slot((slot_me + i) % slots)
        return copy(sc_own, sc_all.at[slot], scs.at[i - 1], scr.at[i - 1], target)

    save_a = pltpu.make_async_copy(mixed, out_a, own_s.at[1])

    def backward(c, carry):
        next_chunk(load_fine, c, fine)
        q = fine + c
        value = nt(inner[0], bu[c % depth_of, :rc, :]) + nt(inner[1], wu_b[fine_columns(c), :])
        store(q, value)
        behind(q - 1)

        @pl.when(c == min(lags[-1][0] + 1, fine - 1))
        def _():
            save_a.start()

        @pl.when(c == 1)
        def _():
            sc_own[...] = sc_col[...].reshape(m_rows, lanes).T[:8]
            for i in range(1, slots):
                score_copy(i, slot_me).start()

        return carry

    lax.fori_loop(0, fine, backward, 0)

    sc_all[slot_me] = sc_own[...]
    for i in range(1, slots):
        score_copy(i, (slot_me - i + slots) % slots).wait_recv()
    table = tabs[...].reshape(m_rows, lanes).T
    lines = []
    for e in range(experts):
        plane, row, odd = e // PLANE, (e // 2) % 2, e % 2
        lines.append(sc_all[row * planes + plane, odd : odd + 1, :])
    score = jnp.concatenate(lines, axis=0)
    gate = ROUTED_SCALE * score
    mean = jnp.sum(gate * table[experts : 2 * experts], axis=0, keepdims=True)
    logit = table[2 * experts : 3 * experts] * (gate - mean)
    order = lax.broadcasted_iota(jnp.int32, (experts, m_rows), 0)
    one = jnp.sum(jnp.where(order == me, logit, 0.0), axis=0, keepdims=True)
    two = jnp.sum(jnp.where(order == x_near, logit, 0.0), axis=0, keepdims=True)
    both = jnp.concatenate([one, two, jnp.zeros((6, m_rows), jnp.float32)], axis=0)

    def thirds(v):
        high = v.astype(jnp.bfloat16)
        rest = v - high.astype(jnp.float32)
        medium = rest.astype(jnp.bfloat16)
        return (high, medium, (rest - medium.astype(jnp.float32)).astype(jnp.bfloat16))

    pieces = thirds(both)
    for c in range(depth // kc):
        cols = pl.ds(c * kc, kc)
        rhs = rows[1, :, :, cols].reshape(m_rows, kc)
        rg_buf[:, cols] = nn(pieces[0], rhs) + nn(pieces[1], rhs) + nn(pieces[2], rhs)

    def grad_copy(i):
        expert = me if i == 0 else x_near
        pipe = p if i == 1 else mirror
        return copy(rg_buf, rg_in.at[i], gs.at[i], gr.at[i], expert, pipe)

    for i in range(3):
        grad_copy(i).start()
    padded = jnp.concatenate([logit, jnp.zeros((lanes - experts, m_rows), jnp.float32)], axis=0)
    sc_col[...] = padded.T.reshape(slots, tok, lanes)
    dense = thirds(sc_col[slot_me])
    dots[...] = jnp.zeros(dots.shape, jnp.float32)
    for c in range(depth // kc):
        cols = pl.ds(c * kc, kc)
        rhs = router_t[:, cols]
        extra[:, cols] = nn(dense[0], rhs) + nn(dense[1], rhs) + nn(dense[2], rhs)
    for q in range(fine, steps - 1 - lags[-1][0]):
        finish_b(q - fine, lifted[:, fine_columns(q - fine)])
    relay_z(steps - 7)
    for q in range(steps - 5, steps):
        fold_y(q)
        relay_z(q - 1)
        fold_z(q - 4)
    relay_z(steps - 1)
    for q in range(steps - 4, steps):
        fold_z(q)

    inv = rinv_b[:, 0:1]
    slope = inv * inv * inv * (jnp.sum(dots[...], axis=-1, keepdims=True) / depth)
    for c in range(depth // kc):
        cols = pl.ds(c * kc, kc)
        delta = inv * lifted[:, cols] - hid_b[:, cols].astype(jnp.float32) * slope
        out_b[:, cols] = delta.astype(out_b.dtype)
    for i in range(3):
        grad_copy(i).wait_recv()
    rg_out[0:1, :] = rg_buf[0:1, :] + rg_in[0, 0:1, :]
    rg_out[1:2, :] = rg_in[1, 1:2, :] + rg_in[2, 1:2, :]

    save_a.wait()
    for k in range(4):
        z_send(k, pair).wait_send()
        z_send(k, opposite).wait_send()

        if k == 0:
            z_send(k, other).wait_send()
        else:

            @pl.when(middle)
            def _():
                z_send(k, other).wait_send()
                z_relay(k).wait_send()

        y_send(k).wait_send()
        if k < 2:
            y_copy(k, pair, y).wait_send()
        else:
            cross(k, z).wait_send()
            y_half(k, y).wait_send()
        for source in (opposite, other):
            y_copy(k, source, y).wait_send()
    for i in range(n_up):
        up_x(i).wait_send()
        up_m(i, part).wait_send()

    def drain(c, carry):
        down_x(c).wait_send()
        down_m(c, part).wait_send()
        return carry

    lax.fori_loop(0, chunks, drain, 0)

    def drain_rs(q, carry):
        rs_y(q).wait_send()
        sent_z(q)
        return carry

    lax.fori_loop(steps - ring, steps, drain_rs, 0)
    for i in range(1, slots):
        score_copy(i, slot_me).wait_send()
    for i in range(3):
        grad_copy(i).wait_send()


N_UP = 4
RING = 8
AHEAD = 3


def fused_plan(n, tok, depth, width):
    planes = n // PLANE
    slots = 2 * planes
    m_rows = slots * tok
    kc = 512 if depth % 512 == 0 else 256
    dc = rc = 256
    chunks = depth // dc
    steps = 2 * (depth // rc)
    bf, f32 = jnp.bfloat16, jnp.float32
    buffers = [
        ((3, slots, tok, depth), bf),
        ((slots, tok, 128), f32),
        ((depth, width), bf),
        ((chunks, width, dc), bf),
        ((AHEAD, kc, width), bf),
        ((AHEAD, width, kc), bf),
        ((2, m_rows, width), bf),
        ((2, m_rows, width), f32),
        ((2, m_rows, width), f32),
        ((2, m_rows, width), bf),
        ((2, m_rows, width), bf),
        ((RING, slots, tok, rc), bf),
        ((steps, planes, tok, rc), bf),
        ((RING, planes, tok, rc), bf),
        ((steps, planes - 1, tok, rc), bf),
        ((steps, tok, rc), bf),
        ((slots, tok, 128), f32),
        ((8, m_rows), f32),
        ((slots, 8, m_rows), f32),
        ((8, depth), f32),
        ((3, 8, depth), f32),
        ((128, depth), bf),
        ((tok, 128), f32),
        ((tok, depth), bf),
        ((tok, depth), f32),
        ((tok, 128), f32),
        ((tok, depth), f32),
    ]
    sems = (
        [(2,)]
        + [(4, planes + 1)] * 2
        + [(4, planes)] * 2
        + [(N_UP + chunks,)] * 4
        + [(AHEAD,)] * 2
        + [(steps,)] * 5
        + [(slots - 1,)] * 2
        + [(3,)] * 2
    )
    total = sum(math.prod(shape) * jnp.dtype(kind).itemsize for shape, kind in buffers)
    fits = total + 4 * tok * depth * 2 < 64_500_000 and 3 * n <= 128 and planes == 4
    return fits, (planes, tok, depth, width, kc, dc, rc, N_UP, RING), buffers, sems


def fused(plan, *args):
    _, dims, buffers, sems = plan
    tok, depth = dims[1:3]
    vmem = pl.BlockSpec(memory_space=pltpu.VMEM)
    hbm = pl.BlockSpec(memory_space=pl.ANY)
    return pl.pallas_call(
        functools.partial(fused_kernel, dims + (lax.axis_size("pipe"),)),
        out_shape=[
            jax.ShapeDtypeStruct((tok, depth), jnp.bfloat16),
            jax.ShapeDtypeStruct((tok, depth), jnp.bfloat16),
            jax.ShapeDtypeStruct((2, depth), jnp.float32),
        ],
        in_specs=[vmem] * 6 + [hbm] * 2,
        out_specs=[hbm, vmem, vmem],
        scratch_shapes=[pltpu.VMEM(shape, kind) for shape, kind in buffers]
        + [DMA(shape) for shape in sems],
        compiler_params=pltpu.CompilerParams(
            collective_id=7, has_side_effects=True, vmem_limit_bytes=67_000_000
        ),
    )(*args)


def on_device_fused(
    plan, hidden_a, routes_a, hidden_b, routes_b, grad_out_b, router, w_up, w_down
):
    mixed, delta, terms = fused(
        plan,
        hidden_a[0],
        hidden_b[0],
        grad_out_b[0],
        routes_a[0].T,
        routes_b[0].T,
        router[0],
        w_up[0, 0],
        w_down[0, 0],
    )
    layer_out = (hidden_a[0].astype(jnp.float32) + mixed.astype(jnp.float32)).astype(jnp.bfloat16)
    grad_in = (grad_out_b[0].astype(jnp.float32) + delta.astype(jnp.float32)).astype(jnp.bfloat16)
    return (layer_out[None], grad_in[None], jnp.sum(terms, axis=0)[None, None])


def solution(mesh):
    placed = (
        P("pipe", "expert", None),
        P("pipe", "expert", None),
        P("pipe", "expert", None),
        P("pipe", "expert", None),
        P("pipe", "expert", None),
        P("pipe", None, None),
        P("pipe", "expert", None, None),
        P("pipe", "expert", None, None),
    )

    def body(*args):
        w_up = args[6]
        plan = fused_plan(lax.axis_size("expert"), args[0].shape[1], w_up.shape[2], w_up.shape[3])
        if w_up.shape[1] == 1 and plan[0]:
            return on_device_fused(plan, *args)
        return on_device(*args)

    return jax.shard_map(
        body,
        mesh=mesh,
        in_specs=placed,
        out_specs=(P("pipe", "expert", None), P("pipe", "expert", None), P("pipe", "expert", None)),
        check_vma=False,
    )
```

```python
import functools
import math

import jax
import jax.numpy as jnp
from jax import lax
from jax.experimental import pallas as pl
from jax.experimental.pallas import tpu as pltpu
from jax.sharding import PartitionSpec as P

ROUTED_SCALE = 2.5
EPSILON = 1e-06


def partner(block, axis, bit):
    count = lax.axis_size(axis)
    route = []
    for low in range(count):
        high = low | 1 << bit
        if high != low and high < count:
            route += [(low, high), (high, low)]
    return lax.ppermute(block, axis, route)


MESH = pl.DeviceIdType.MESH
DMA = pltpu.SemaphoreType.DMA
PLANE = 4


def remote(src, dst, send_sem, recv_sem, target):
    return pltpu.make_async_remote_copy(
        src_ref=src,
        dst_ref=dst,
        send_sem=send_sem,
        recv_sem=recv_sem,
        device_id={"expert": target},
        device_id_type=MESH,
    )


def place():
    me = lax.axis_index("expert")
    z, y, x = me // PLANE, (me // 2) % 2, me % 2
    return (me, z, y, x, me + 1 - 2 * x, me + 2 - 4 * y)


def greet(planes):
    me, z, y, x, x_near, y_near = place()
    barrier = pltpu.get_barrier_semaphore()
    pl.semaphore_signal(barrier, inc=1, device_id={"expert": x_near}, device_id_type=MESH)
    pl.semaphore_signal(barrier, inc=1, device_id={"expert": y_near}, device_id_type=MESH)

    @pl.when(z < planes - 1)
    def _():
        pl.semaphore_signal(barrier, inc=1, device_id={"expert": me + PLANE}, device_id_type=MESH)

    @pl.when(z > 0)
    def _():
        pl.semaphore_signal(barrier, inc=1, device_id={"expert": me - PLANE}, device_id_type=MESH)

    ends = jnp.where(z == 0, 1, 0) + jnp.where(z == planes - 1, 1, 0)
    pl.semaphore_wait(barrier, 4 - ends)


def gather_kernel(count, planes, *refs):
    ins, outs = refs[:count], refs[count : 2 * count]
    own_sem, up_s, down_s, z_r, x_s, x_r, y_s, y_r, d_s, d_r = refs[2 * count :]
    me, z, y, x, x_near, y_near = place()

    def up(k, p, src):
        return remote(src, outs[k].at[p * PLANE + y * 2 + x], up_s.at[k, p], z_r.at[k, p], me + PLANE)

    def down(k, p, src):
        return remote(src, outs[k].at[p * PLANE + y * 2 + x], down_s.at[k, p], z_r.at[k, p], me - PLANE)

    def to_x(k, p, src):
        return remote(src, outs[k].at[p * PLANE + y * 2 + x], x_s.at[k, p], x_r.at[k, p], x_near)

    def to_y(k, p, src):
        return remote(src, outs[k].at[p * PLANE + y * 2 + x], y_s.at[k, p], y_r.at[k, p], y_near)

    def half(k, p, way):
        if way == 0:
            ref = outs[k].at[p * PLANE + y * 2 + 1 - x, 0]
            return remote(ref, ref, d_s.at[k, p, 0], d_r.at[k, p, 0], y_near)
        ref = outs[k].at[p * PLANE + (1 - y) * 2 + x, 1]
        return remote(ref, ref, d_s.at[k, p, 1], d_r.at[k, p, 1], x_near)

    def each(d, act):
        if d == 0:
            act(z, 0)
            return

        @pl.when(z >= d)
        def _():
            act(z - d, 1)

        @pl.when(z + d < planes)
        def _():
            act(z + d, -1)

    def spread(k, p, way, wait):
        src = ins[k] if way == 0 else outs[k].at[p * PLANE + y * 2 + x]

        def do(copy):
            copy.wait_send() if wait else copy.start()

        if way != 0 and not wait:
            up(k, p, src).wait_recv()
        if way >= 0:

            @pl.when(z < planes - 1)
            def _():
                do(up(k, p, src))

        if way <= 0:

            @pl.when(z > 0)
            def _():
                do(down(k, p, src))

        do(to_x(k, p, src))
        do(to_y(k, p, src))

    def relay(k, p, way):
        to_x(k, p, ins[k]).wait_recv()
        half(k, p, 0).start()
        to_y(k, p, ins[k]).wait_recv()
        half(k, p, 1).start()

    def finish(k, p, way):
        for route in range(2):
            half(k, p, route).wait()
        spread(k, p, way, True)

    greet(planes)
    for k in range(count):
        pltpu.make_async_copy(ins[k], outs[k].at[me], own_sem.at[k]).start()
        each(0, lambda p, way: spread(k, p, way, False))
    for k in range(count):
        for d in range(1, planes):
            each(d, lambda p, way: spread(k, p, way, False))
            each(d - 1, lambda p, way: relay(k, p, way))
        each(planes - 1, lambda p, way: relay(k, p, way))
    for k in range(count):
        for d in range(planes):
            each(d, lambda p, way: finish(k, p, way))
        pltpu.make_async_copy(ins[k], outs[k].at[me], own_sem.at[k]).wait()


def gather_all(blocks, collective_id):
    n = lax.axis_size("expert")
    planes = n // PLANE
    count = len(blocks)
    halved = [b.reshape(2, b.shape[0] // 2, b.shape[1]) for b in blocks]
    outs = pl.pallas_call(
        functools.partial(gather_kernel, count, planes),
        out_shape=[jax.ShapeDtypeStruct((n,) + b.shape, b.dtype) for b in halved],
        in_specs=[pl.BlockSpec(memory_space=pltpu.VMEM)] * count,
        out_specs=[pl.BlockSpec(memory_space=pl.ANY)] * count,
        scratch_shapes=[DMA((count,))] + [DMA((count, planes))] * 7 + [DMA((count, planes, 2))] * 2,
        compiler_params=pltpu.CompilerParams(collective_id=collective_id, has_side_effects=True),
    )(*halved)
    return [o.reshape(n * b.shape[0], b.shape[1]) for o, b in zip(outs, blocks)]


def scatter_stages(planes, part, out, a_r, c_r, b_x, b_y, total, z_r, *sems):
    ax_s, ax_r, ay_s, ay_r, cx_s, cx_r, cy_s, cy_r, z_s, up_r, down_r = sems
    me, z, y, x, x_near, y_near = place()
    rows, cols = part.shape[2:]
    step = 16

    def slot(p, yy, xx):
        return p * PLANE + yy * 2 + xx

    def add(dst, *srcs):
        def body(i, carry):
            r = pl.ds(pl.multiple_of(i * step, step), step)
            acc = srcs[0][r, :].astype(jnp.float32)
            for s in srcs[1:]:
                acc = acc + s[r, :].astype(jnp.float32)
            dst[r, :] = acc.astype(dst.dtype)
            return carry

        lax.fori_loop(0, rows // step, body, 0)

    def diagonal(p):
        src = slot(p, 1 - y, 1 - x)
        return (
            remote(part.at[src, 0], a_r.at[p, 0], ay_s.at[p], ay_r.at[p], y_near),
            remote(part.at[src, 1], a_r.at[p, 1], ax_s.at[p], ax_r.at[p], x_near),
        )

    def beside(p):
        return (
            remote(b_x.at[p, 0], c_r.at[p, 0, 0], cx_s.at[p, 0], cx_r.at[p, 0], x_near),
            remote(part.at[slot(p, y, 1 - x), 1], c_r.at[p, 0, 1], cx_s.at[p, 1], cx_r.at[p, 1], x_near),
            remote(b_y.at[p, 0], c_r.at[p, 1, 1], cy_s.at[p, 0], cy_r.at[p, 0], y_near),
            remote(part.at[slot(p, 1 - y, x), 0], c_r.at[p, 1, 0], cy_s.at[p, 1], cy_r.at[p, 1], y_near),
        )

    def rise(p):
        return remote(total.at[p], z_r.at[0, p], z_s.at[p], up_r.at[p], me + PLANE)

    def sink(p):
        return remote(total.at[p], z_r.at[1, p], z_s.at[p], down_r.at[p], me - PLANE)

    def first(p, way):
        for copy in diagonal(p):
            copy.start()
        beside(p)[1].start()
        beside(p)[3].start()

    def second(p, way):
        to_y, to_x = diagonal(p)
        to_y.wait_recv()
        add(b_x.at[p, 0], part.at[slot(p, y, 1 - x), 0], a_r.at[p, 0])
        beside(p)[0].start()
        to_x.wait_recv()
        add(b_y.at[p, 0], part.at[slot(p, 1 - y, x), 1], a_r.at[p, 1])
        beside(p)[2].start()

    def third(p, way):
        for copy in beside(p):
            copy.wait_recv()
        for h in range(2):
            add(total.at[p, h], part.at[slot(p, y, x), h], c_r.at[p, 0, h], c_r.at[p, 1, h])

        def take(copy, level):
            copy.wait_recv()
            for h in range(2):
                add(total.at[p, h], total.at[p, h], z_r.at[level, p, h])

        if way >= 0:

            @pl.when(z > 0)
            def _():
                take(rise(p), 0)

        if way <= 0:

            @pl.when(z < planes - 1)
            def _():
                take(sink(p), 1)

        if way > 0:
            rise(p).start()
        if way < 0:
            sink(p).start()
        if way == 0:
            out[...] = total[p]

    def finish(p, way):
        for copy in diagonal(p) + beside(p):
            copy.wait_send()
        if way != 0:
            rise(p).wait_send()

    return (first, second, third, finish)


def scatter_kernel(planes, count, *refs):
    parts, outs, rest = refs[:count], refs[count : 2 * count], refs[2 * count :]
    per = len(rest) // count
    z = place()[1]
    stages = [
        scatter_stages(planes, parts[k], outs[k], *rest[k * per : (k + 1) * per])
        for k in range(count)
    ]

    def each(d, act):
        if d == 0:
            act(z, 0)
            return

        @pl.when(z >= d)
        def _():
            act(z - d, -1)

        @pl.when(z + d < planes)
        def _():
            act(z + d, 1)

    greet(planes)
    order = list(range(planes - 1, -1, -1))
    for k in range(count):
        for d in order:
            each(d, stages[k][0])
    for i, d in enumerate(order):
        for k in range(count):
            each(d, stages[k][1])
        if i > 0:
            for k in range(count):
                each(order[i - 1], stages[k][2])
    for k in range(count):
        each(0, stages[k][2])
    for k in range(count):
        for d in order:
            each(d, stages[k][3])


def scatter_sums(parts, collective_id):
    n = lax.axis_size("expert")
    planes = n // PLANE
    tokens, cols = parts[0].shape
    rows = tokens // n // 2
    half = (rows, cols)
    kind = parts[0].dtype
    count = len(parts)
    if count > 1 and count * 3 * parts[0].size * kind.itemsize > 56 << 20:
        return [scatter_sums([part], collective_id + k)[0] for k, part in enumerate(parts)]
    outs = pl.pallas_call(
        functools.partial(scatter_kernel, planes, count),
        out_shape=[jax.ShapeDtypeStruct((2,) + half, kind)] * count,
        in_specs=[pl.BlockSpec(memory_space=pltpu.VMEM)] * count,
        out_specs=[pl.BlockSpec(memory_space=pltpu.VMEM)] * count,
        scratch_shapes=(
            [
                pltpu.VMEM((planes, 2) + half, kind),
                pltpu.VMEM((planes, 2, 2) + half, kind),
                pltpu.VMEM((planes, 1) + half, kind),
                pltpu.VMEM((planes, 1) + half, kind),
                pltpu.VMEM((planes, 2) + half, kind),
                pltpu.VMEM((2, planes, 2) + half, kind),
            ]
            + [DMA((planes,))] * 4
            + [DMA((planes, 2))] * 4
            + [DMA((planes,))] * 3
        )
        * count,
        compiler_params=pltpu.CompilerParams(
            collective_id=collective_id, has_side_effects=True, vmem_limit_bytes=60 << 20
        ),
    )(*[part.reshape((n, 2) + half) for part in parts])
    return [out.reshape(2 * rows, cols) for out in outs]


def prepare(hidden, routes, router_segment):
    expert_count = router_segment.shape[0]
    hidden32 = hidden.astype(jnp.float32)
    rinv = lax.rsqrt(jnp.mean(hidden32 * hidden32, axis=-1, keepdims=True) + EPSILON)
    normed = (hidden32 * rinv).astype(jnp.bfloat16)
    logits = jnp.einsum("td,ed->te", normed, router_segment, preferred_element_type=jnp.float32)
    chosen = jnp.any(
        routes[:, :, None] == jnp.arange(expert_count, dtype=jnp.int32)[None, None, :], axis=1
    )
    affinity = jnp.where(chosen, jax.nn.sigmoid(logits), 0.0)
    return (hidden32, rinv, normed, affinity)


def on_device(hidden_a, routes_a, hidden_b, routes_b, grad_out_b, router, w_up, w_down):
    n_expert = lax.axis_size("expert")
    me = lax.axis_index("expert")
    tok_count = hidden_a.shape[1]
    router_segment = router[0]
    expert_count = router_segment.shape[0]
    local_count = w_up.shape[1]
    hidden32_a, rinv_a, normed_a, affinity_a = prepare(hidden_a[0], routes_a[0], router_segment)
    hidden32_b, rinv_b, normed_b, affinity_b = prepare(hidden_b[0], routes_b[0], router_segment)
    grad_out = grad_out_b[0]
    affinity_ab = jnp.concatenate([affinity_a, affinity_b], axis=1)
    lanes = -(-2 * expert_count // 128) * 128
    affinity_ab = jnp.pad(affinity_ab, ((0, 0), (0, lanes - 2 * expert_count)))
    rows_a, rows_b, rows_g, affinities = gather_all([normed_a, normed_b, grad_out, affinity_ab], 1)
    aff_a, aff_b = affinities[:, :expert_count], affinities[:, expert_count : 2 * expert_count]
    total_b = jnp.sum(aff_b, axis=1, keepdims=True)
    weight_a = aff_a / jnp.sum(aff_a, axis=1, keepdims=True)
    weight_b = aff_b / total_b

    def column(table, local):
        return lax.dynamic_slice_in_dim(table, me * local_count + local, 1, axis=1)

    sum_a = 0.0
    sum_b = 0.0
    scores = []
    for local in range(local_count):
        up, down = w_up[0, local], w_down[0, local]
        pre = jnp.dot(rows_a, up, preferred_element_type=jnp.float32)
        active = jax.nn.silu(pre).astype(jnp.bfloat16)
        out = jnp.dot(active, down, preferred_element_type=jnp.float32)
        sum_a = sum_a + out * column(weight_a, local)
    for local in range(local_count):
        up, down = w_up[0, local], w_down[0, local]
        pre = jnp.dot(rows_b, up, preferred_element_type=jnp.float32)
        back = jnp.einsum("td,fd->tf", rows_g, down, preferred_element_type=jnp.float32)
        sig = jax.nn.sigmoid(pre)
        scores.append(jnp.sum(back * (pre * sig), axis=-1))
        inner = (back * (sig * (1.0 + pre * (1.0 - sig)))).astype(jnp.bfloat16)
        lifted = jnp.einsum("tf,df->td", inner, up, preferred_element_type=jnp.float32)
        sum_b = sum_b + lifted * column(weight_b, local)
    sum_ab = scatter_sums([sum_a.astype(jnp.bfloat16), sum_b.astype(jnp.bfloat16)], 2)
    mixed = sum_ab[0].astype(jnp.float32)
    layer_out = (hidden32_a + ROUTED_SCALE * mixed).astype(jnp.bfloat16)

    flat = jnp.stack(scores).reshape(-1)
    padded = jnp.pad(flat, (0, -flat.shape[0] % 2048)).reshape(-1, 128)
    score = gather_all([padded], 4)[0].reshape(n_expert, -1)[:, : flat.shape[0]]
    score = score.reshape(expert_count, -1).T
    score = jnp.where(aff_b > 0.0, score, 0.0)
    gate_grad = ROUTED_SCALE * score
    logit_grad = (
        aff_b
        * (1.0 - aff_b)
        * (gate_grad - jnp.sum(gate_grad * weight_b, axis=1, keepdims=True))
        / total_b
    )
    own_columns = lax.dynamic_slice_in_dim(logit_grad, me * local_count, local_count, axis=1)
    own_term = jnp.dot(
        own_columns.T, rows_b.astype(jnp.float32), precision=lax.Precision.HIGHEST
    )
    mirrored = own_term
    for bit in range(lax.axis_size("pipe").bit_length() - 1):
        mirrored = partner(mirrored, "pipe", bit)
    router_grad = own_term + mirrored

    dense = lax.dynamic_slice_in_dim(logit_grad, me * tok_count, tok_count, axis=0)
    lifted_sum = sum_ab[1].astype(jnp.float32)
    normed_grad = ROUTED_SCALE * lifted_sum + jnp.dot(
        dense, router_segment.astype(jnp.float32), precision=lax.Precision.HIGHEST
    )
    mean_term = jnp.mean(normed_grad * hidden32_b, axis=-1, keepdims=True)
    grad_in = (
        grad_out.astype(jnp.float32) + rinv_b * normed_grad - hidden32_b * rinv_b**3 * mean_term
    )
    return (layer_out[None], grad_in.astype(jnp.bfloat16)[None], router_grad[None])


def fused_kernel(dims, *refs):
    planes, tok, depth, width, kc, dc, rc, n_up, ring, n_pipe = dims
    (hid_a, hid_b, g, routes_a, routes_b, router, wu, wd, out_a, out_b, rg_out) = refs[:11]
    (rows, tabs, wu_b, wd_b, bu, bd, act, pre, back, silu, inner) = refs[11:22]
    (o_buf, y_buf, t_buf, z_buf, f_buf, sc_col, sc_own, sc_all, rg_buf, rg_in) = refs[22:32]
    (router_t, rinv_b, mixed, extra, dots, lifted) = refs[32:38]
    (own_s, zs, zr, ys, yr, xs, xr, ms, mr, bus, bds) = refs[38:49]
    (rys, ryr, rzs, rzr, rfs, scs, scr, gs, gr, lys, lyr) = refs[49:60]
    slots = 2 * planes
    experts = 2 * slots
    m_rows = slots * tok
    chunks = depth // dc
    half_d = depth // 2
    half_f = width // 2
    half_t = tok // 2
    up_rows = half_d // n_up
    tile = 256
    lanes = tabs.shape[-1]
    me, z, y, x, x_near, y_near = place()
    p = lax.axis_index("pipe")
    mirror = n_pipe - 1 - p
    part = (2 * p) // n_pipe
    slot_me = y * planes + z
    pair = z + 1 - 2 * (z % 2)
    opposite = (z + 2) % planes
    other = (pair + 2) % planes
    middle = (z + 1) // 2 == 1

    def copy(src, dst, send, recv, expert, pipe=p):
        return pltpu.make_async_remote_copy(
            src_ref=src,
            dst_ref=dst,
            send_sem=send,
            recv_sem=recv,
            device_id={"pipe": pipe, "expert": expert},
            device_id_type=MESH,
        )

    def chip(plane, row):
        return plane * PLANE + row * 2 + x

    def of_slot(s):
        return chip(s % planes, s // planes)

    barrier = pltpu.get_barrier_semaphore()

    def hello(pipe, expert):
        pl.semaphore_signal(
            barrier, inc=1, device_id={"pipe": pipe, "expert": expert}, device_id_type=MESH
        )

    for i in range(1, slots):
        hello(p, of_slot((slot_me + i) % slots))
    hello(p, x_near)
    hello(mirror, me)
    hello(mirror, x_near)

    own_g = pltpu.make_async_copy(g, rows.at[2, slot_me], own_s.at[0])
    own_g.start()

    pl.semaphore_wait(barrier, slots - 1 + 3)

    def up_region(which, i):
        return pl.ds(pl.multiple_of(which * half_d + i * up_rows, up_rows), up_rows)

    def up_x(i):
        r = up_region(part, i)
        return copy(wu.at[r], wu_b.at[r], xs.at[i], xr.at[i], x_near)

    def up_m(i, which):
        r = up_region(which, i)
        return copy(wu_b.at[r], wu_b.at[r], ms.at[i], mr.at[i], me, mirror)

    def down_rows(which):
        return pl.ds(pl.multiple_of(which * half_f, half_f), half_f)

    def columns(c):
        return pl.ds(pl.multiple_of(c * dc, dc), dc)

    def wide_columns(c):
        return pl.ds(pl.multiple_of(c * kc, kc), kc)

    def fine_columns(c):
        return pl.ds(pl.multiple_of(c * rc, rc), rc)

    def down_x(c):
        r = down_rows(part)
        src = wd.at[r, columns(c)]
        return copy(src, wd_b.at[c, r], xs.at[n_up + c], xr.at[n_up + c], x_near)

    def down_m(c, which):
        ref = wd_b.at[c, down_rows(which)]
        return copy(ref, ref, ms.at[n_up + c], mr.at[n_up + c], me, mirror)

    for i in range(n_up):
        up_x(i).start()
    for c in range(chunks):
        down_x(c).start()

    bufs = [tabs, rows.at[0], rows.at[1], rows.at[2]]

    def block(k, row, source):
        return bufs[k].at[row * planes + source]

    def mine(k):
        return g if k == 3 else bufs[k].at[slot_me]

    def z_send(k, target):
        dst = bufs[k].at[slot_me]
        return copy(mine(k), dst, zs.at[k, target], zr.at[k, z], chip(target, y))

    def z_take(k, source):
        ref = block(k, y, source)
        return copy(ref, ref, zs.at[k, source], zr.at[k, source], chip(source, y))

    def z_relay(k):
        ref = block(k, y, opposite)
        return copy(ref, ref, zs.at[k, z], zr.at[k, opposite], chip(pair, y))

    def late(ref):
        return ref.at[pl.ds(half_t, half_t)]

    def early(ref):
        return ref.at[pl.ds(0, half_t)]

    def cross(k, source):
        ref = late(block(k, 1 - y, source))
        return copy(ref, ref, zs.at[k, planes], zr.at[k, planes], chip(pair, y))

    def y_send(k):
        return copy(mine(k), bufs[k].at[slot_me], ys.at[k, z], yr.at[k, z], y_near)

    def y_copy(k, source, row):
        ref = block(k, row, source)
        return copy(ref, ref, ys.at[k, source], yr.at[k, source], y_near)

    def y_half(k, row):
        ref = early(block(k, row, pair))
        return copy(ref, ref, ys.at[k, pair], yr.at[k, pair], y_near)

    def spread(k):
        if k < 3:
            y_send(k).start()

        @pl.when(middle)
        def _():
            if k < 2:
                z_send(k, pair).start()
            z_send(k, other).start()

        @pl.when(jnp.logical_not(middle))
        def _():
            z_send(k, pair).start()
            if k == 0:
                z_send(k, other).start()

        z_send(k, opposite).start()

    def serve(k, i):
        if i == 0:
            z_take(k, pair).wait_recv()
            if k < 2:
                y_copy(k, pair, y).start()
            else:
                y_half(k, y).start()
                y_copy(k, z, 1 - y).wait_recv()
                cross(k, z).start()
        if i == 1:
            z_take(k, opposite).wait_recv()

            @pl.when(middle)
            def _():
                if k > 0:
                    z_relay(k).start()
                if 0 < k < 3:
                    z_send(k + 1, pair).start()

            y_copy(k, opposite, y).start()
        if i == 2:
            z_take(k, other).wait_recv()
            y_copy(k, other, y).start()

    def arrived(k):
        if k < 2:
            y_copy(k, z, 1 - y).wait_recv()
            y_copy(k, pair, 1 - y).wait_recv()
        else:
            y_half(k, 1 - y).wait_recv()
            cross(k, pair).wait_recv()
        y_copy(k, opposite, 1 - y).wait_recv()
        y_copy(k, other, 1 - y).wait_recv()

    y_send(3).start()

    def nn(lhs, rhs):
        return jnp.dot(lhs, rhs, preferred_element_type=jnp.float32)

    def nt(lhs, rhs):
        return lax.dot_general(
            lhs, rhs, (((1,), (1,)), ((), ())), preferred_element_type=jnp.float32
        )

    def normalize(k, src):
        step = 16

        def body(i, carry):
            r = pl.ds(pl.multiple_of(i * step, step), step)
            h = src[r, :].astype(jnp.float32)
            rinv = lax.rsqrt(jnp.mean(h * h, axis=-1, keepdims=True) + EPSILON)
            rows[k, slot_me, r, :] = (h * rinv).astype(rows.dtype)
            if k == 1:
                rinv_b[r, :] = jnp.broadcast_to(rinv, (step, lanes))
            return carry

        lax.fori_loop(0, tok // step, body, 0)

    normalize(0, hid_a)
    normalize(1, hid_b)
    for i in range(3):
        router_t[i * experts : (i + 1) * experts] = router[...]
    router_t[3 * experts :] = jnp.zeros((lanes - 3 * experts, depth), router_t.dtype)
    lane = lax.broadcasted_iota(jnp.int32, (tok, lanes), 1)
    expert_lane = lax.rem(lane, experts)

    def affinity(k, routes, section):
        logits = nt(rows[k, slot_me], router_t[...])
        named = routes[...].T
        chosen = expert_lane == named[:, 0:1]
        for i in range(1, named.shape[1]):
            chosen = jnp.logical_or(chosen, expert_lane == named[:, i : i + 1])
        sig = jnp.where(chosen, jax.nn.sigmoid(logits), 0.0)
        here = jnp.where(lax.div(lane, experts) == section, sig, 0.0)
        return sig, here, jnp.sum(here, axis=-1, keepdims=True)

    _, here_a, total_a = affinity(0, routes_a, 0)
    sig_b, here_b, total_b = affinity(1, routes_b, 1)
    slope_b = jnp.where(lax.div(lane, experts) == 2, sig_b * (1.0 - sig_b), 0.0)
    tabs[slot_me] = here_a / total_a + here_b / total_b + slope_b / total_b

    for k in range(4):
        spread(k)

    def chunk_of(k, cols):
        return rows[k, :, :, cols].reshape(m_rows, cols.size)

    class Pieces:
        def __init__(self, src, dst, sem):
            self.whole = pltpu.make_async_copy(src, dst, sem)
            count = 4
            step = dst.shape[0] // count
            self.parts = [
                pltpu.make_async_copy(src.at[r], dst.at[r], sem)
                for r in (pl.ds(i * step, step) for i in range(count))
            ]

        def start(self):
            for part_copy in self.parts:
                part_copy.start()

        def wait(self):
            self.whole.wait()

    depth_of = bu.shape[0]

    def load_up(c):
        return Pieces(wu.at[wide_columns(c)], bu.at[c % depth_of], bus.at[c % depth_of])

    def load_fine(c):
        return Pieces(wu.at[fine_columns(c)], bu.at[c % depth_of, pl.ds(0, rc)], bus.at[c % depth_of])

    def load_down(c):
        dst = bd.at[c % depth_of, :, pl.ds(0, dc)]
        return Pieces(wd.at[:, columns(c)], dst, bds.at[c % depth_of])

    def prime(load, lo, hi):
        for c in range(lo, min(hi, lo + depth_of - 1)):
            load(c).start()

    def next_chunk(load, c, count=chunks):
        load(c).wait()

        @pl.when(c + depth_of - 1 < count)
        def _():
            load(c + depth_of - 1).start()

    def block_rows(s):
        return pl.ds(pl.multiple_of(s * tok, tok), tok)

    def clear(dst):
        def body(s, carry):
            dst[block_rows(s), :] = jnp.zeros((tok, width), jnp.float32)
            return carry

        lax.fori_loop(0, slots, body, 0)

    def project(k, partner, dst):
        clear(dst)
        count = depth // kc
        if not partner:
            prime(load_up, 0, count)

        def body(c, carry):
            if not partner:
                next_chunk(load_up, c, count)
            lhs = chunk_of(k, wide_columns(c))
            for n in range(width // tile):
                cols = pl.ds(n * tile, tile)
                rhs = wu_b[wide_columns(c), cols] if partner else bu[c % depth_of, :, cols]
                dst[:, cols] += nn(lhs, rhs)
            return carry

        lax.fori_loop(0, count, body, 0)

    def pick(s, column):
        return jnp.sum(jnp.where(lane == column, tabs[s], 0.0), axis=-1, keepdims=True)

    expert_of = [me, x_near]

    def activate(which, src):
        def body(s, carry):
            v = src[block_rows(s), :]
            weight = pick(s, expert_of[which])
            act[which, block_rows(s), :] = (v * jax.nn.sigmoid(v) * weight).astype(act.dtype)
            return carry

        lax.fori_loop(0, slots, body, 0)

    def prepare_b(which):
        def body(s, carry):
            r = block_rows(s)
            v = pre[which, r, :]
            sig = jax.nn.sigmoid(v)
            silu[which, r, :] = (v * sig).astype(silu.dtype)
            weight = pick(s, experts + expert_of[which])
            pre[which, r, :] = sig * (1.0 + v * (1.0 - sig)) * weight
            return carry

        lax.fori_loop(0, slots, body, 0)

    def invert(which):
        def body(s, carry):
            r = block_rows(s)
            bk = back[which, r, :]
            score = jnp.sum(bk * silu[which, r, :].astype(jnp.float32), axis=-1, keepdims=True)
            inner[which, r, :] = (bk * pre[which, r, :]).astype(inner.dtype)
            at = x if which == 0 else 1 - x
            held = 0.0 if which == 0 else sc_col[s]
            sc_col[s] = jnp.where(lane == at, score, held)
            return carry

        lax.fori_loop(0, slots, body, 0)

    fine = depth // rc
    steps = 2 * fine

    def rs_y(q):
        src = o_buf.at[q % ring, pl.ds((1 - y) * planes, planes)]
        return copy(src, y_buf.at[q], rys.at[q], ryr.at[q], y_near)

    def rs_last(i):
        q, plane = steps - 1, (other, opposite, pair, z)[i]
        src = o_buf.at[q % ring, (1 - y) * planes + plane]
        return copy(src, y_buf.at[q, plane], lys.at[i], lyr.at[i], y_near)

    def fold_last():
        q = steps - 1
        sent_z(q - ring)
        for i, plane in enumerate((other, opposite, pair, z)):
            rs_last(i).wait_recv()
            first = o_buf[q % ring, y * planes + plane].astype(jnp.float32)
            both = first + y_buf[q, plane].astype(jnp.float32)
            t_buf[q % ring, plane] = both.astype(t_buf.dtype)
            if i < planes - 1:
                rs_z(q, plane, (2, 1, 0)[i]).start()

    def rs_z(q, target, place_at):
        src = t_buf.at[q % ring, target]
        return copy(src, z_buf.at[q, place_at], rzs.at[q], rzr.at[q], chip(target, y))

    def rs_far(q):
        src = t_buf.at[q % ring, other]
        return copy(src, f_buf.at[q], rzs.at[q], rfs.at[q], chip(pair, y))

    def direct(q):
        return isinstance(q, int) and q >= steps - 1

    def sent_z(q):
        src = t_buf.at[q % ring, pl.ds(0, planes - 1)]
        dst = z_buf.at[q, pl.ds(0, planes - 1)]
        copy(src, dst, rzs.at[q], rzr.at[q], chip(pair, y)).wait_send()

    def fold_y(q):
        rs_y(q).wait_recv()

        def clean():
            sent_z(q - ring)

        if isinstance(q, int):
            if q >= ring:
                clean()
        else:
            pl.when(q >= ring)(clean)
        for k in range(planes):
            first = o_buf[q % ring, y * planes + k].astype(jnp.float32)
            t_buf[q % ring, k] = (first + y_buf[q, k].astype(jnp.float32)).astype(t_buf.dtype)
        if direct(q):
            pl.when(middle)(lambda: rs_z(q, opposite, 1).start())
            rs_z(q, other, 2).start()
            pl.when(jnp.logical_not(middle))(lambda: rs_z(q, opposite, 1).start())
            rs_z(q, pair, 0).start()
            return

        @pl.when(middle)
        def _():
            rs_z(q, other, 2).start()

        @pl.when(jnp.logical_not(middle))
        def _():
            rs_far(q).start()
            rs_z(q, opposite, 1).start()

        rs_z(q, pair, 0).start()

    def relay_z(q):
        if direct(q):
            return

        @pl.when(middle)
        def _():
            rs_far(q).wait_recv()
            total = t_buf[q % ring, opposite].astype(jnp.float32) + f_buf[q].astype(jnp.float32)
            t_buf[q % ring, opposite] = total.astype(t_buf.dtype)
            rs_z(q, opposite, 1).start()

    def take_z(q, count):
        src = t_buf.at[q % ring, pl.ds(0, count)]
        dst = z_buf.at[q, pl.ds(0, count)]
        copy(src, dst, rzs.at[q], rzr.at[q], chip(pair, y)).wait_recv()
        total = t_buf[q % ring, z].astype(jnp.float32)
        for i in range(count):
            total = total + z_buf[q, i].astype(jnp.float32)
        return total

    def finish_b(c, total):
        cols = fine_columns(c)
        v = ROUTED_SCALE * total + extra[:, cols]
        lifted[:, cols] = v
        prod = v * hid_b[:, cols].astype(jnp.float32)
        for i in range(rc // lanes):
            dots[...] += prod[:, i * lanes : (i + 1) * lanes]

    def fold_z(q):
        def settle(total):
            def of_a():
                mixed[:, fine_columns(q)] = (ROUTED_SCALE * total).astype(mixed.dtype)

            def of_b():
                lifted[:, fine_columns(q - fine)] = total

            if isinstance(q, int):
                finish_b(q - fine, total)
            else:
                pl.when(q < fine)(of_a)
                pl.when(q >= fine)(of_b)

        if direct(q):
            settle(take_z(q, planes - 1))
            return

        @pl.when(middle)
        def _():
            settle(take_z(q, planes - 1))

        @pl.when(jnp.logical_not(middle))
        def _():
            settle(take_z(q, planes - 2))

    lags = ((4, fold_y), (6, relay_z), (8, fold_z))

    def behind(q):
        for lag, stage in lags:
            if isinstance(q, int):
                if lag <= q < steps + lag:
                    stage(q - lag)
            else:
                pl.when(q >= lag)(functools.partial(stage, q - lag))

    def store(q, value):
        def clean():
            rs_y(q - ring).wait_send()

        pl.when(q >= ring)(clean)
        o_buf[q % ring] = value.reshape(slots, tok, rc).astype(o_buf.dtype)

        @pl.when(q < steps - 1)
        def _():
            rs_y(q).start()

        @pl.when(q == steps - 1)
        def _():
            for i in range(planes):
                rs_last(i).start()


    def take_up(i):
        up_x(i).wait_recv()
        up_m(i, part).start()

    def load_wide(c):
        return Pieces(wd.at[:, wide_columns(c)], bd.at[c % depth_of], bds.at[c % depth_of])

    def own_back(c, carry):
        next_chunk(load_wide, c, depth // kc)
        lhs = chunk_of(2, wide_columns(c))
        for n in range(width // tile):
            cols = pl.ds(n * tile, tile)
            back[0, :, cols] += nt(lhs, bd[c % depth_of, cols, :])
        return carry

    def partner_back(c, carry):
        lhs = chunk_of(2, columns(c))
        for n in range(width // tile):
            cols = pl.ds(n * tile, tile)
            back[1, :, cols] += nt(lhs, wd_b[c, cols, :])
        return carry

    for k in range(2):
        for i in range(3):
            serve(k, i)
    serve(2, 0)
    serve(2, 1)
    own_g.wait()
    arrived(0)
    arrived(1)
    take_up(0)
    take_up(1)
    project(0, False, back.at[0])
    activate(0, back.at[0])
    serve(2, 2)

    def serve_last():
        serve(3, 0)
        serve(3, 1)

    pl.when(middle)(serve_last)
    for i in range(2, n_up):
        take_up(i)
    for i in range(n_up):
        up_m(i, 1 - part).wait_recv()
    project(0, True, back.at[1])
    activate(1, back.at[1])
    pl.when(jnp.logical_not(middle))(serve_last)
    marks = [chunks * i // 14 for i in (0, 3, 6, 8)]
    hold = marks[2]
    prime(load_down, 0, hold + 1)
    clear(back.at[0])
    clear(back.at[1])

    def take_down(c):
        down_x(c).wait_recv()
        down_m(c, part).start()

    take_down(0)
    take_down(1)
    def forward(c, carry):
        load_down(c).wait()
        ahead = c + depth_of - 1

        @pl.when(jnp.logical_and(ahead < chunks, jnp.logical_or(ahead <= hold, c > hold)))
        def _():
            load_down(ahead).start()

        down_m(c, 1 - part).wait_recv()
        for n in range(dc // rc):
            cols = pl.ds(n * rc, rc)
            value = nn(act[0], bd[c % depth_of, :, cols]) + nn(act[1], wd_b[c, :, cols])
            store(c * (dc // rc) + n, value)

        @pl.when(c == marks[0])
        def _():
            arrived(2)
            project(1, False, pre.at[0])
            prepare_b(0)

        @pl.when(c == 1)
        def _():
            serve(3, 2)

        @pl.when(c == marks[1])
        def _():
            project(1, True, pre.at[1])
            prepare_b(1)

        @pl.when(c == hold)
        def _():
            arrived(3)
            prime(load_wide, 0, depth // kc)
            lax.fori_loop(0, depth // kc, own_back, 0)
            prime(load_down, hold + 1, chunks)
            prime(load_fine, 0, fine)

        @pl.when(c == marks[3])
        def _():
            lax.fori_loop(0, marks[3] + 1, partner_back, 0)
            invert(0)

        @pl.when(c > marks[3])
        def _():
            partner_back(c, 0)

        @pl.when(c + 1 < chunks)
        def _():
            for n in range(dc // rc):
                behind(c * (dc // rc) + n)

        @pl.when(c + 3 < chunks)
        def _():
            take_down(c + 2)

        @pl.when(c + 2 == chunks)
        def _():
            take_down(c + 1)

        return carry

    lax.fori_loop(0, chunks, forward, 0)
    invert(1)

    def score_copy(i, slot):
        target = of_slot((slot_me + i) % slots)
        return copy(sc_own, sc_all.at[slot], scs.at[i - 1], scr.at[i - 1], target)

    save_a = pltpu.make_async_copy(mixed, out_a, own_s.at[1])

    def backward(c, carry):
        next_chunk(load_fine, c, fine)
        q = fine + c
        value = nt(inner[0], bu[c % depth_of, :rc, :]) + nt(inner[1], wu_b[fine_columns(c), :])
        store(q, value)
        behind(q - 1)

        @pl.when(c == min(lags[-1][0] + 1, fine - 1))
        def _():
            save_a.start()

        @pl.when(c == 1)
        def _():
            sc_own[...] = sc_col[...].reshape(m_rows, lanes).T[:8]
            for i in range(1, slots):
                score_copy(i, slot_me).start()

        return carry

    lax.fori_loop(0, fine, backward, 0)

    sc_all[slot_me] = sc_own[...]
    for i in range(1, slots):
        score_copy(i, (slot_me - i + slots) % slots).wait_recv()
    table = tabs[...].reshape(m_rows, lanes).T
    lines = []
    for e in range(experts):
        plane, row, odd = e // PLANE, (e // 2) % 2, e % 2
        lines.append(sc_all[row * planes + plane, odd : odd + 1, :])
    score = jnp.concatenate(lines, axis=0)
    gate = ROUTED_SCALE * score
    mean = jnp.sum(gate * table[experts : 2 * experts], axis=0, keepdims=True)
    logit = table[2 * experts : 3 * experts] * (gate - mean)
    order = lax.broadcasted_iota(jnp.int32, (experts, m_rows), 0)
    one = jnp.sum(jnp.where(order == me, logit, 0.0), axis=0, keepdims=True)
    two = jnp.sum(jnp.where(order == x_near, logit, 0.0), axis=0, keepdims=True)
    both = jnp.concatenate([one, two, jnp.zeros((6, m_rows), jnp.float32)], axis=0)

    def thirds(v):
        high = v.astype(jnp.bfloat16)
        rest = v - high.astype(jnp.float32)
        medium = rest.astype(jnp.bfloat16)
        return (high, medium, (rest - medium.astype(jnp.float32)).astype(jnp.bfloat16))

    pieces = thirds(both)
    for c in range(depth // kc):
        cols = pl.ds(c * kc, kc)
        rhs = rows[1, :, :, cols].reshape(m_rows, kc)
        rg_buf[:, cols] = nn(pieces[0], rhs) + nn(pieces[1], rhs) + nn(pieces[2], rhs)

    def grad_copy(i):
        expert = me if i == 0 else x_near
        pipe = p if i == 1 else mirror
        return copy(rg_buf, rg_in.at[i], gs.at[i], gr.at[i], expert, pipe)

    for i in range(3):
        grad_copy(i).start()
    padded = jnp.concatenate([logit, jnp.zeros((lanes - experts, m_rows), jnp.float32)], axis=0)
    sc_col[...] = padded.T.reshape(slots, tok, lanes)
    dense = thirds(sc_col[slot_me])
    dots[...] = jnp.zeros(dots.shape, jnp.float32)
    for c in range(depth // kc):
        cols = pl.ds(c * kc, kc)
        rhs = router_t[:, cols]
        extra[:, cols] = nn(dense[0], rhs) + nn(dense[1], rhs) + nn(dense[2], rhs)
    for q in range(fine, steps - 1 - lags[-1][0]):
        finish_b(q - fine, lifted[:, fine_columns(q - fine)])
    relay_z(steps - 7)
    for q in range(steps - 5, steps):
        fold_last() if q == steps - 1 else fold_y(q)
        relay_z(q - 1)
        fold_z(q - 4)
    relay_z(steps - 1)
    for q in range(steps - 4, steps):
        fold_z(q)

    inv = rinv_b[:, 0:1]
    slope = inv * inv * inv * (jnp.sum(dots[...], axis=-1, keepdims=True) / depth)
    for c in range(depth // kc):
        cols = pl.ds(c * kc, kc)
        delta = inv * lifted[:, cols] - hid_b[:, cols].astype(jnp.float32) * slope
        out_b[:, cols] = delta.astype(out_b.dtype)
    for i in range(3):
        grad_copy(i).wait_recv()
    rg_out[0:1, :] = rg_buf[0:1, :] + rg_in[0, 0:1, :]
    rg_out[1:2, :] = rg_in[1, 1:2, :] + rg_in[2, 1:2, :]

    save_a.wait()
    for k in range(4):
        z_send(k, pair).wait_send()
        z_send(k, opposite).wait_send()

        if k == 0:
            z_send(k, other).wait_send()
        else:

            @pl.when(middle)
            def _():
                z_send(k, other).wait_send()
                z_relay(k).wait_send()

        y_send(k).wait_send()
        if k < 2:
            y_copy(k, pair, y).wait_send()
        else:
            cross(k, z).wait_send()
            y_half(k, y).wait_send()
        for source in (opposite, other):
            y_copy(k, source, y).wait_send()
    for i in range(n_up):
        up_x(i).wait_send()
        up_m(i, part).wait_send()

    def drain(c, carry):
        down_x(c).wait_send()
        down_m(c, part).wait_send()
        return carry

    lax.fori_loop(0, chunks, drain, 0)

    def drain_rs(q, carry):
        @pl.when(q < steps - 1)
        def _():
            rs_y(q).wait_send()

        sent_z(q)
        return carry

    lax.fori_loop(steps - ring, steps, drain_rs, 0)
    for i in range(planes):
        rs_last(i).wait_send()
    for i in range(1, slots):
        score_copy(i, slot_me).wait_send()
    for i in range(3):
        grad_copy(i).wait_send()


N_UP = 4
RING = 8
AHEAD = 3


def fused_plan(n, tok, depth, width):
    planes = n // PLANE
    slots = 2 * planes
    m_rows = slots * tok
    kc = 512 if depth % 512 == 0 else 256
    dc = rc = 256
    chunks = depth // dc
    steps = 2 * (depth // rc)
    bf, f32 = jnp.bfloat16, jnp.float32
    buffers = [
        ((3, slots, tok, depth), bf),
        ((slots, tok, 128), f32),
        ((depth, width), bf),
        ((chunks, width, dc), bf),
        ((AHEAD, kc, width), bf),
        ((AHEAD, width, kc), bf),
        ((2, m_rows, width), bf),
        ((2, m_rows, width), f32),
        ((2, m_rows, width), f32),
        ((2, m_rows, width), bf),
        ((2, m_rows, width), bf),
        ((RING, slots, tok, rc), bf),
        ((steps, planes, tok, rc), bf),
        ((RING, planes, tok, rc), bf),
        ((steps, planes - 1, tok, rc), bf),
        ((steps, tok, rc), bf),
        ((slots, tok, 128), f32),
        ((8, m_rows), f32),
        ((slots, 8, m_rows), f32),
        ((8, depth), f32),
        ((3, 8, depth), f32),
        ((128, depth), bf),
        ((tok, 128), f32),
        ((tok, depth), bf),
        ((tok, depth), f32),
        ((tok, 128), f32),
        ((tok, depth), f32),
    ]
    sems = (
        [(2,)]
        + [(4, planes + 1)] * 2
        + [(4, planes)] * 2
        + [(N_UP + chunks,)] * 4
        + [(AHEAD,)] * 2
        + [(steps,)] * 5
        + [(slots - 1,)] * 2
        + [(3,)] * 2
        + [(planes,)] * 2
    )
    total = sum(math.prod(shape) * jnp.dtype(kind).itemsize for shape, kind in buffers)
    fits = total + 4 * tok * depth * 2 < 64_500_000 and 3 * n <= 128 and planes == 4
    return fits, (planes, tok, depth, width, kc, dc, rc, N_UP, RING), buffers, sems


def fused(plan, *args):
    _, dims, buffers, sems = plan
    tok, depth = dims[1:3]
    vmem = pl.BlockSpec(memory_space=pltpu.VMEM)
    hbm = pl.BlockSpec(memory_space=pl.ANY)
    return pl.pallas_call(
        functools.partial(fused_kernel, dims + (lax.axis_size("pipe"),)),
        out_shape=[
            jax.ShapeDtypeStruct((tok, depth), jnp.bfloat16),
            jax.ShapeDtypeStruct((tok, depth), jnp.bfloat16),
            jax.ShapeDtypeStruct((2, depth), jnp.float32),
        ],
        in_specs=[vmem] * 6 + [hbm] * 2,
        out_specs=[hbm, vmem, vmem],
        scratch_shapes=[pltpu.VMEM(shape, kind) for shape, kind in buffers]
        + [DMA(shape) for shape in sems],
        compiler_params=pltpu.CompilerParams(
            collective_id=7, has_side_effects=True, vmem_limit_bytes=67_000_000
        ),
    )(*args)


def on_device_fused(
    plan, hidden_a, routes_a, hidden_b, routes_b, grad_out_b, router, w_up, w_down
):
    mixed, delta, terms = fused(
        plan,
        hidden_a[0],
        hidden_b[0],
        grad_out_b[0],
        routes_a[0].T,
        routes_b[0].T,
        router[0],
        w_up[0, 0],
        w_down[0, 0],
    )
    layer_out = (hidden_a[0].astype(jnp.float32) + mixed.astype(jnp.float32)).astype(jnp.bfloat16)
    grad_in = (grad_out_b[0].astype(jnp.float32) + delta.astype(jnp.float32)).astype(jnp.bfloat16)
    return (layer_out[None], grad_in[None], jnp.sum(terms, axis=0)[None, None])


def solution(mesh):
    placed = (
        P("pipe", "expert", None),
        P("pipe", "expert", None),
        P("pipe", "expert", None),
        P("pipe", "expert", None),
        P("pipe", "expert", None),
        P("pipe", None, None),
        P("pipe", "expert", None, None),
        P("pipe", "expert", None, None),
    )

    def body(*args):
        w_up = args[6]
        plan = fused_plan(lax.axis_size("expert"), args[0].shape[1], w_up.shape[2], w_up.shape[3])
        if w_up.shape[1] == 1 and plan[0]:
            return on_device_fused(plan, *args)
        return on_device(*args)

    return jax.shard_map(
        body,
        mesh=mesh,
        in_specs=placed,
        out_specs=(P("pipe", "expert", None), P("pipe", "expert", None), P("pipe", "expert", None)),
        check_vma=False,
    )
```
